32 devices in a mesh: aux: 8 (over z, x), row: 4 (over y, core).
Axes of the slice: x: 2, y: 2, z: 4, core: 2. Of those that a mesh axis runs over, the one named last changes fastest.
Arguments:
- density: float32 [2, 16, 512, 512], P(None, 'aux', 'row'), may hold values from -6 to 6
- couplings: float32 [4, 512], replicated, may hold values from -3 to 3
- weight_real: float32 [4], replicated, may hold values from -1 to 1
- weight_imag: float32 [4], replicated, may hold values from -1 to 1
- mode_rates: float32 [4], replicated, may hold values from 0.05 to 0.5
- tier_counts: int32 [16, 4], P('aux'), may hold values from 0 to 2
- link_index: int32 [16, 8], replicated, may hold values from -1 to 15, as said below
- link_mirror: int32 [16, 8], replicated, may hold values from 0 to 1, as said below
- block_diagonal: bfloat16 [8, 64, 64], replicated, may hold values from -0.5 to 0.5
- block_outer: bfloat16 [8, 64, 64], replicated, may hold values from -0.5 to 0.5
- block_column: int32 [8], replicated, may hold values from 0 to 7
Outputs:
- evolved: float32 [2, 16, 512, 512], P(None, 'aux', 'row')
The draws below stay inside these ranges and needn't reach their ends.
Inputs may be any that keep to these rules, and one draw needn't show every extreme that they name: Auxiliary a is stored on index a // 2 of aux. For any two different indices of aux, the links of the auxiliaries stored on one of them name at most one distinct pair (link_index, link_mirror) of auxiliaries stored on the other. link_mirror is 0 where link_index is -1.
All inputs are finite; a program needn't handle non-finite values.
Results may differ from the reference program's by a relative error of at most 0.0031.
Values may be sent and summed in bfloat16 or wider, within the bound.
No kernel may reach another device: no remote copies, remote signals or barrier semaphores. Data moves between devices by JAX's collectives and lax.ppermute only.
A program may use at most 128 MiB of HBM per device.

```python
import math
import jax
import jax.numpy as jnp
from jax import lax

STATES = 512
BLOCK = 64
BLOCKS = 8
MODES = 4
LINKS = 8
TOP_TIER = 2
AUX_DEV = 2
AUXES = 16
POOL = 7


def link_tables(key):
    base_key = jax.random.fold_in(key, 11)
    devices = AUXES // AUX_DEV
    total_refs = AUX_DEV * LINKS

    def one_device(device_key, device):
        subkeys = jax.random.split(device_key, 8)
        offsets = 1 + jax.random.permutation(subkeys[0], devices - 1)[:POOL]
        remote_aux = (device + offsets) % devices * AUX_DEV + jax.random.randint(subkeys[1], (POOL,), 0, AUX_DEV)
        remote_flag = jax.random.randint(subkeys[2], (POOL,), 0, 2)
        placing = jax.random.permutation(subkeys[3], total_refs)[:POOL]
        link_kind = jax.random.randint(subkeys[4], (total_refs,), 0, 6)
        repeat = jax.random.randint(subkeys[5], (total_refs,), 0, POOL)
        local_aux = device * AUX_DEV + jax.random.randint(subkeys[6], (total_refs,), 0, AUX_DEV)
        local_flag = jax.random.randint(subkeys[7], (total_refs,), 0, 2)
        index_all = jnp.where(link_kind < 2, remote_aux[repeat], jnp.where(link_kind < 5, local_aux, -1))
        flag_all = jnp.where(link_kind < 2, remote_flag[repeat], jnp.where(link_kind < 5, local_flag, 0))
        index_all = index_all.at[placing].set(remote_aux)
        flag_all = flag_all.at[placing].set(remote_flag)
        return (index_all, flag_all)
    index_all, flag_all = jax.vmap(one_device)(jax.random.split(base_key, devices), jnp.arange(devices, dtype=jnp.int32))
    return (index_all.reshape(AUXES, LINKS).astype(jnp.int32), flag_all.reshape(AUXES, LINKS).astype(jnp.int32))


def draw_link_index(key, part):
    return link_tables(key)[0]


def draw_link_mirror(key, part):
    return link_tables(key)[1]


def set_ends(entries, own_key, least, largest):
    place = [jax.random.randint(jax.random.fold_in(own_key, axis), (), 0, length) for axis, length in enumerate(entries.shape)]
    main_axis = entries.shape.index(max(entries.shape))
    neighbour = place[:main_axis] + [(place[main_axis] + 1) % entries.shape[main_axis]] + place[main_axis + 1:]
    return entries.at[tuple(place)].set(least).at[tuple(neighbour)].set(largest)


def steps_of(rng, dims, pieces, low, largest):
    def one(dim, parts):
        steps = jax.random.uniform(jax.random.fold_in(jax.random.fold_in(rng, 6), dim), (parts,), jnp.float32, low / len(pieces), largest / len(pieces))
        return jnp.repeat(jnp.exp(steps), dims[dim] // parts).reshape((-1,) + (1,) * (len(dims) - dim - 1))

    level = one(*pieces[0])
    for cut in pieces[1:]:
        level = level * one(*cut)
    return level


def scatter_about(stream_key, dims, width, bound, shards=(), kind=jnp.bfloat16):
    level = steps_of(stream_key, dims, shards, -0.22, 0.18) if shards else 1.0
    entries = jax.random.normal(stream_key, dims, jnp.float32) * width * level
    return jnp.minimum(jnp.maximum(entries, -bound), bound).astype(kind)


def setup_inputs(seed: int = 0) -> dict:
    keys = jax.random.split(jax.random.key(seed), 12)
    density = scatter_about(keys[0], (2, AUXES, STATES, STATES), 1.0, 6.0, ((1, 8), (2, 4)), jnp.float32)
    couplings = scatter_about(keys[1], (MODES, STATES), 0.5, 3.0, (), jnp.float32)
    weight_real = jnp.clip(jax.random.uniform(keys[2], (MODES,), jnp.float32, -1.0, 1.0), -1.0, 1.0)
    weight_imag = jnp.clip(jax.random.uniform(keys[3], (MODES,), jnp.float32, -1.0, 1.0), -1.0, 1.0)
    mode_rates = jnp.clip(jnp.exp(jax.random.uniform(keys[4], (MODES,), jnp.float32, math.log(0.05), math.log(0.5))), 0.05, 0.5)
    tier_counts = set_ends(jax.random.randint(keys[5], (AUXES, MODES), 0, TOP_TIER + 1), jax.random.fold_in(keys[5], 1), 0, TOP_TIER).astype(jnp.int32)
    link_index = draw_link_index(jax.random.fold_in(keys[11], 71), 0)
    link_mirror = draw_link_mirror(jax.random.fold_in(keys[11], 71), 0)
    block_diagonal = scatter_about(keys[8], (BLOCKS, BLOCK, BLOCK), (2 * BLOCK) ** -0.5, 0.5)
    block_outer = scatter_about(keys[9], (BLOCKS, BLOCK, BLOCK), (2 * BLOCK) ** -0.5, 0.5)
    block_column = set_ends(jax.random.randint(keys[10], (BLOCKS,), 0, BLOCKS), jax.random.fold_in(keys[10], 1), 0, BLOCKS - 1).astype(jnp.int32)
    return dict(density=density, couplings=couplings, weight_real=weight_real, weight_imag=weight_imag, mode_rates=mode_rates, tier_counts=tier_counts, link_index=link_index, link_mirror=link_mirror, block_diagonal=block_diagonal, block_outer=block_outer, block_column=block_column)


def conj_turn(matrix):
    return jnp.stack([matrix[0].T, -matrix[1].T])


def reference(density, couplings, weight_real, weight_imag, mode_rates, tier_counts, link_index, link_mirror, block_diagonal, block_outer, block_column):
    inner_blocks = block_diagonal.astype(jnp.float32)
    outer_blocks = block_outer.astype(jnp.float32)
    selector = (block_column[:, None] == jnp.arange(BLOCKS, dtype=jnp.int32)[None, :]).astype(jnp.float32)
    coupling_diff = couplings[:, :, None] - couplings[:, None, :]
    coupling_sum = couplings[:, :, None] + couplings[:, None, :]
    counts = tier_counts.astype(jnp.float32)
    damping = jnp.sum(counts * mode_rates[None, :], axis=1)

    def derivative(current):
        rounded = current.astype(jnp.bfloat16)

        def per_auxiliary(position):
            matrix = lax.dynamic_index_in_dim(rounded, position, 1, keepdims=False).astype(jnp.float32)
            row_blocks = matrix.reshape(2, BLOCKS, BLOCK, STATES)
            partner = jnp.einsum('bj,zjrc->zbrc', selector, row_blocks)
            product_left = jnp.einsum('bij,zbjc->zbic', inner_blocks, row_blocks) + jnp.einsum('bij,zbjc->zbic', outer_blocks, partner)
            product_left = product_left.reshape(2, STATES, STATES)
            columns = matrix.reshape(2, STATES, BLOCKS, BLOCK)
            right_own = jnp.einsum('zrbj,bjc->zrbc', columns, inner_blocks)
            right_far = jnp.einsum('zrjk,jkc->zrjc', columns, outer_blocks)
            product_right = (right_own + jnp.einsum('zrjc,jb->zrbc', right_far, selector)).reshape(2, STATES, STATES)
            difference = product_left - product_right
            result = jnp.stack([difference[1], -difference[0]])
            for link_pos in range(LINKS):
                target = link_index[position, link_pos]
                picked = lax.dynamic_index_in_dim(rounded, jnp.maximum(target, 0), 1, keepdims=False).astype(jnp.float32)
                chosen = jnp.where(link_mirror[position, link_pos] == 1, conj_turn(picked), picked)
                chosen = chosen * (target >= 0).astype(jnp.float32)
                mode_pos = link_pos % MODES
                if link_pos < MODES:
                    scale_real = jnp.float32(1.0)
                    scale_imag = jnp.float32(0.0)
                else:
                    scale_real = counts[position, mode_pos] * weight_real[mode_pos]
                    scale_imag = counts[position, mode_pos] * weight_imag[mode_pos]
                real_term = scale_real * coupling_diff[mode_pos] * chosen[1] + scale_imag * coupling_sum[mode_pos] * chosen[0]
                imag_term = -scale_real * coupling_diff[mode_pos] * chosen[0] + scale_imag * coupling_sum[mode_pos] * chosen[1]
                result = result + jnp.stack([real_term, imag_term])
            current_aux = lax.dynamic_index_in_dim(current, position, 1, keepdims=False)
            return result - damping[position] * current_aux

        return jnp.moveaxis(lax.map(per_auxiliary, jnp.arange(AUXES, dtype=jnp.int32)), 0, 1)

    slope_one = derivative(density)
    slope_two = derivative(density + 0.25 * slope_one)
    slope_three = derivative(density + 0.25 * slope_two)
    slope_four = derivative(density + 0.5 * slope_three)
    return density + (0.5 / 6.0) * (slope_one + 2.0 * slope_two + 2.0 * slope_three + slope_four)
```

```python
import functools

import jax
import jax.numpy as jnp
from jax import lax
from jax.experimental import pallas as pl
from jax.experimental.pallas import tpu as pltpu
from jax.sharding import PartitionSpec as P

MODES = 4
LINKS = 8
LANES = 128
STEP = 0.5
BOTH = ("aux", "row")

F32 = jnp.float32
BF16 = jnp.bfloat16


class Sizes:
    def __init__(self, groups, rows, per_device, band, extent):
        self.groups, self.rows, self.per_device = groups, rows, per_device
        self.band, self.extent = band, extent
        self.devices = groups * rows
        self.local = band // groups
        self.auxes = per_device * groups
        self.za = 2 * self.auxes
        self.lanes = self.local * self.za
        self.fold = max(1, LANES // self.za)
        self.tile = self.fold * self.za
        self.tiles = self.local // self.fold
        self.joined = self.local % 16 == 0


def dot(a, b, dims=((1,), (0,))):
    return lax.dot_general(a, b, (dims, ((), ())), preferred_element_type=F32)


def run(kernel, outs, args, scratch=(), flops=0):
    spec = pl.BlockSpec(memory_space=pltpu.VMEM)
    moved = sum(a.size * a.dtype.itemsize for a in args)
    moved += sum(o.size * o.dtype.itemsize for o in outs)
    return pl.pallas_call(
        kernel,
        out_shape=list(outs),
        in_specs=[spec] * len(args),
        out_specs=[spec] * len(outs),
        scratch_shapes=list(scratch),
        compiler_params=pltpu.CompilerParams(vmem_limit_bytes=48 << 20),
        cost_estimate=pl.CostEstimate(flops=flops, bytes_accessed=moved, transcendentals=0),
    )(*args)


def shape(*dims, dtype=F32):
    return jax.ShapeDtypeStruct(dims, dtype)


def one_hot(target, count):
    return (target[:, None] == jnp.arange(count, dtype=jnp.int32)[None, :]).astype(BF16)


def matrix_index(s, index, device):
    group, row = device // s.rows, device % s.rows
    return row * s.band + index * s.groups + group


def row_blocks(extent, size=128):
    return range(0, extent, size)


def send_start_kernel(d_ref, pick_rows, pick_cols, out_ref):
    planes, number, band, extent = d_ref.shape
    flat = d_ref[...].reshape(planes * number * band, extent).astype(BF16)
    for b in row_blocks(flat.shape[0]):
        moved = dot(pick_rows[b : b + 128, :], flat).astype(BF16)
        out_ref[b : b + 128, :] = dot(moved, pick_cols[...]).astype(BF16)


def take_start_kernel(got_ref, pick_lanes, message_rows, s_ref, m_ref):
    for b in row_blocks(got_ref.shape[1]):
        s_ref[b : b + 128, :] = dot(
            got_ref[:, b : b + 128], pick_lanes[...], ((0,), (0,))
        ).astype(BF16)
    for b in row_blocks(m_ref.shape[0]):
        m_ref[b : b + 128, :] = dot(message_rows[b : b + 128, :], s_ref[...]).astype(BF16)


def turn(s, load, order, swap, put):
    size = order.shape[0]
    span = size // s.local
    for block in range(s.extent // size):
        moved = dot(order[...], load(block * size, size))
        parts = []
        for ih in range(s.tiles):
            for jh in range(s.tiles):
                lanes = slice(jh * s.tile, (jh + 1) * s.tile)
                pieces = [
                    moved[(ih * s.fold + f) * span : (ih * s.fold + f + 1) * span, lanes]
                    for f in range(s.fold)
                ]
                parts.append(jnp.concatenate(pieces, axis=1) if s.fold > 1 else pieces[0])
        turned = dot(jnp.concatenate(parts, axis=0).astype(BF16), swap[...])
        for ih in range(s.tiles):
            for jh in range(s.tiles):
                start = (ih * s.tiles + jh) * span
                for f in range(s.fold):
                    first = (jh * s.fold + f) * s.devices + block * span
                    put(
                        slice(first, first + span),
                        slice(ih * s.tile, (ih + 1) * s.tile),
                        turned[start : start + span, f * s.tile : (f + 1) * s.tile],
                    )


def take_columns_kernel(s, got_ref, order, swap, first_rows, left_rows, s_ref, t_ref, *message):
    def put(rows, lanes, value):
        t_ref[rows, lanes] = value.astype(BF16)

    turn(s, lambda start, size: got_ref[start : start + size, :], order, swap, put)
    write_messages(s, first_rows, left_rows, s_ref, t_ref, message)


def write_messages(s, right_rows, left_rows, s_ref, t_ref, message):
    pairs = ((left_rows, t_ref), (right_rows, s_ref))
    if not s.joined and len(message) == 1:
        pairs = pairs[:1]
    both = s.joined and message[0].shape[0] == 2 * s.extent
    for part, (matrix, state) in enumerate(pairs):
        if s.joined and part == 1 and not both:
            continue
        for b in row_blocks(s.extent):
            product = dot(matrix[b : b + 128, :], state[...]).astype(BF16)
            if not s.joined:
                message[part][b : b + 128, :] = product
            elif not both:
                message[0][b : b + 128, :] = product
            else:
                for k in range(128 // s.local):
                    start = ((b // s.local + k) * 2 + part) * s.local
                    message[0][start : start + s.local, :] = product[
                        k * s.local : (k + 1) * s.local, :
                    ]


def slope_kernel(
    s, with_columns, s_ref, t_ref, ys_ref, yt_ref, damp, q_ref, right, left, unit, wa_s, wb_s, wa_t, wb_t, *rest
):
    if with_columns:
        ks_ref, kt_ref, turned = rest
    else:
        ks_ref, turned = rest

    def one(direct, mirror, y_ref, h, wa, wb, out_ref, sign):
        for th in range(s.tiles):
            lanes = slice(th * s.tile, (th + 1) * s.tile)
            turned[:, lanes] = dot(direct[:, lanes], unit[...]).astype(BF16)
        for b in row_blocks(s.extent):
            rows = slice(b, b + 128)
            whole = dot(h[rows, :], turned[...])
            for th in range(s.tiles):
                lanes = slice(th * s.tile, (th + 1) * s.tile)
                source = jnp.concatenate([direct[rows, lanes], mirror[rows, lanes]], axis=1)
                source = jnp.concatenate([source, source], axis=1)
                total = dot(source, wa[th]) - damp[:, lanes] * y_ref[rows, lanes].astype(F32)
                total = total + sign * whole[:, lanes]
                fields = dot(source, wb[...])
                for k in range(MODES):
                    total = total + q_ref[rows, k : k + 1] * fields[:, k * s.tile : (k + 1) * s.tile]
                out_ref[rows, lanes] = total

    one(s_ref, t_ref, ys_ref, right, wa_s, wb_s, ks_ref, -1.0)
    if with_columns:
        one(t_ref, s_ref, yt_ref, left, wa_t, wb_t, kt_ref, 1.0)


def part_loader(s, refs, part):
    def load(start, size):
        if not s.joined:
            return refs[part][start : start + size, :]
        step = s.local
        pieces = []
        for first in range(start, start + size, step):
            at = (first // step * 2 + part) * step
            pieces.append(refs[0][at : at + step, :])
        return jnp.concatenate(pieces, axis=0)

    return load


def next_kernel(s, weight, step, has_total, both, got_count, *refs):
    got = refs[:got_count]
    refs = refs[got_count:]
    order, swap, right_rows, left_rows, ks_ref, kt_ref, ds_ref, dt_ref = refs[:8]
    refs = refs[8:]
    total_in = None
    if has_total:
        total_in, refs = refs[0], refs[1:]
    s_ref, t_ref, ys_ref, yt_ref, total_ref = refs[:5]
    message, arrived = refs[5:-1], refs[-1]

    def put(rows, lanes, value):
        arrived[rows, lanes] = value

    for part in range(2):
        turn(s, part_loader(s, got, part), order, swap, put)
        for b in row_blocks(s.extent, 64):
            rows = slice(b, b + 64)
            if part == 0:
                slope = ks_ref[rows, :] + arrived[rows, :]
                grown = weight * slope
                total_ref[rows, :] = total_in[rows, :] + grown if has_total else grown
                state = ds_ref[rows, :].astype(F32) + step * slope
                ys_ref[rows, :] = state
                s_ref[rows, :] = state.astype(BF16)
            else:
                slope = kt_ref[rows, :] - arrived[rows, :]
                state = dt_ref[rows, :].astype(F32) + step * slope
                yt_ref[rows, :] = state
                t_ref[rows, :] = state.astype(BF16)
    write_messages(s, right_rows, left_rows, s_ref, t_ref, message)


def last_kernel(s, weight, got_ref, order, swap, ks_ref, total_in, pick_lanes, out_ref, arrived, grown):
    def put(rows, lanes, value):
        arrived[rows, lanes] = value

    turn(s, lambda start, size: got_ref[start : start + size, :], order, swap, put)
    for b in row_blocks(s.extent, 64):
        rows = slice(b, b + 64)
        change = total_in[rows, :] + weight * (ks_ref[rows, :] + arrived[rows, :])
        grown[rows, :] = change.astype(BF16)
    for b in row_blocks(s.lanes):
        out_ref[b : b + 128, :] = dot(
            pick_lanes[b : b + 128, :], grown[...], ((1,), (1,))
        ).astype(BF16)


def finish_kernel(got_ref, place_rows, place_cols, d_ref, out_ref):
    planes, number, band, extent = d_ref.shape
    for z in range(planes):
        for n in range(number):
            at = (z * number + n) * band
            for b in range(0, band, min(band, 128)):
                size = min(band, 128)
                rows = slice(at + b, at + b + size)
                moved = dot(place_rows[rows, :], got_ref[...]).astype(BF16)
                out_ref[z, n, b : b + size, :] = d_ref[z, n, b : b + size, :] + dot(
                    moved, place_cols[...]
                )


def link_matrices(s, counts, weight_real, weight_imag, link_index, link_mirror):
    ones = jnp.ones_like(counts)
    real = jnp.stack([ones, counts * weight_real[None, :]], 1)
    imag = jnp.stack([jnp.zeros_like(counts), counts * weight_imag[None, :]], 1)
    index = link_index.reshape(s.auxes, 2, MODES)
    mirror = link_mirror.reshape(s.auxes, 2, MODES)
    source = jnp.arange(s.auxes, dtype=jnp.int32)
    hit = index[None] == source[:, None, None, None]
    kinds = jnp.stack([hit & (mirror[None] == 0), hit & (mirror[None] == 1)]).astype(F32)
    along = jnp.sum(kinds * real, 3)
    cross = jnp.sum(kinds * imag, 3)
    along, cross = (jnp.transpose(m, (0, 3, 1, 2)) for m in (along, cross))
    flip = jnp.array([1.0, -1.0], F32).reshape(2, 1, 1, 1)

    def build(sign):
        upper = jnp.concatenate([cross, -sign * along], 3)
        lower = jnp.concatenate([sign * along, cross], 3) * flip
        return jnp.concatenate([upper, lower], 2)

    return build(1.0), build(-1.0)


def two_pieces(weights, axis):
    high = lax.reduce_precision(weights, 8, 7)
    low = weights - high
    return jnp.concatenate([high.astype(BF16), low.astype(BF16)], axis)


def coupling_weights(s, by_local, by_first, local_q):
    eye = jnp.eye(s.fold, dtype=F32)
    near = jnp.einsum("ki,xkuv->ixuv", local_q, by_local, precision=lax.Precision.HIGHEST)
    near = near.reshape(s.tiles, s.fold, 2, s.za, s.za)
    near = jnp.transpose(near, (0, 2, 1, 3, 4))[:, :, :, :, None, :] * eye[None, None, :, None, :, None]
    near = near.reshape(s.tiles, 2 * s.tile, s.tile)
    far = jnp.transpose(by_first, (0, 2, 1, 3))[:, None, :, :, None, :] * eye[None, :, None, None, :, None]
    far = far.reshape(2 * s.tile, MODES * s.tile)
    return two_pieces(near, 1), two_pieces(far, 0)


def body(
    density,
    couplings,
    weight_real,
    weight_imag,
    mode_rates,
    tier_counts,
    link_index,
    link_mirror,
    block_diagonal,
    block_outer,
    block_column,
):
    planes, per_device, band, extent = density.shape
    s = Sizes(lax.axis_size("aux"), lax.axis_size("row"), per_device, band, extent)
    blocks, block = block_diagonal.shape[0], block_diagonal.shape[1]
    group, row = lax.axis_index("aux"), lax.axis_index("row")
    device = group * s.rows + row
    cube = 2 * extent * extent * s.lanes

    number = jnp.arange(extent, dtype=jnp.int32)
    first_to_matrix = matrix_index(s, number // s.devices, number % s.devices)
    posted_to_matrix = matrix_index(s, number % s.local, number // s.local)
    posted_to_first = number % s.local * s.devices + number // s.local

    wide = jnp.arange(s.lanes, dtype=jnp.int32)
    sub = planes * per_device * s.local
    start_source = wide % sub * s.groups + wide // sub
    pick_rows = one_hot(start_source, s.lanes)
    pick_cols = one_hot(first_to_matrix, extent).T
    lane_of = (
        wide % s.local * s.za
        + wide // (per_device * s.local) % planes * s.auxes
        + wide // sub * per_device
        + wide // s.local % per_device
    )
    pick_lanes = one_hot(lane_of, s.lanes)
    message_rows = one_hot(posted_to_first, extent)
    start_message = run(
        send_start_kernel,
        [shape(s.lanes, extent, dtype=BF16)],
        [density, pick_rows, pick_cols],
        flops=2 * cube,
    )[0]
    start_got = lax.all_to_all(
        start_message.reshape(s.groups, sub, extent), "aux", split_axis=0, concat_axis=0, tiled=True
    ).reshape(s.lanes, extent)

    selector = block_column[:, None] == jnp.arange(blocks, dtype=jnp.int32)[None, :]
    own = jnp.eye(blocks, dtype=F32)
    whole_h = (
        own[:, None, :, None] * block_diagonal.astype(F32)[:, :, None, :]
        + selector.astype(F32)[:, None, :, None] * block_outer.astype(F32)[:, :, None, :]
    ).reshape(extent, extent).astype(BF16)
    first_h = one_hot(first_to_matrix, extent)
    left = jnp.dot(
        jnp.dot(first_h, whole_h, preferred_element_type=BF16), first_h.T, preferred_element_type=BF16
    )
    right = left.T
    left_rows = jnp.dot(message_rows, left, preferred_element_type=BF16)
    right_rows = jnp.dot(message_rows, right, preferred_element_type=BF16)

    counts = lax.all_gather(tier_counts, "aux", axis=0, tiled=True).astype(F32)
    damping = jnp.sum(counts * mode_rates[None, :], axis=1)
    damp = jnp.tile(damping, (planes * s.local,))[None, :]
    q_first = jnp.dot(
        couplings, first_h.T.astype(F32), precision=lax.Precision.HIGHEST
    ).T
    local_pick = (matrix_index(s, jnp.arange(s.local, dtype=jnp.int32), device)[None, :] == number[:, None])
    local_q = jnp.dot(couplings, local_pick.astype(F32), precision=lax.Precision.HIGHEST)
    by_row, by_column = link_matrices(s, counts, weight_real, weight_imag, link_index, link_mirror)
    wa_s, wb_s = coupling_weights(s, by_row, by_column, local_q)
    wa_t, wb_t = coupling_weights(s, by_column, by_row, local_q)

    lane = jnp.arange(s.za, dtype=jnp.int32)
    unit = jnp.where(
        lane[:, None] == (lane[None, :] + s.auxes) % s.za,
        jnp.where(lane[None, :] < s.auxes, 1.0, -1.0),
        0.0,
    )
    eye_fold = jnp.eye(s.fold, dtype=F32)
    unit_tile = (eye_fold[:, None, :, None] * unit[None, :, None, :]).reshape(s.tile, s.tile).astype(BF16)
    swap = (
        eye_fold[:, None, None, None, :, None]
        * eye_fold[None, :, None, :, None, None]
        * unit[None, None, :, None, None, :]
    ).reshape(s.fold * s.tile, s.fold * s.tile).astype(BF16)
    keep = (
        eye_fold[:, None, None, None, :, None]
        * eye_fold[None, :, None, :, None, None]
        * jnp.eye(s.za, dtype=F32)[None, None, :, None, None, :]
    ).reshape(s.fold * s.tile, s.fold * s.tile).astype(BF16)
    size = min(extent, max(256, 16 * s.local))
    span = size // s.local
    at = jnp.arange(size, dtype=jnp.int32)
    order = one_hot(at % span * s.local + at // span, size)

    state = shape(extent, s.lanes, dtype=BF16)
    full = shape(extent, s.lanes)
    held = pltpu.VMEM((extent, s.lanes), F32)
    held_b = pltpu.VMEM((extent, s.lanes), BF16)

    def exchange(messages):
        parts = [m.reshape(s.devices, -1, s.lanes) for m in messages]
        sent = parts[0] if len(parts) == 1 else jnp.concatenate(parts, 1)
        got = lax.all_to_all(sent, BOTH, split_axis=0, concat_axis=0, tiled=True)
        if len(parts) == 1:
            return [got.reshape(-1, s.lanes)]
        height = s.local
        return [got[:, p * height : (p + 1) * height].reshape(-1, s.lanes) for p in range(2)]

    if s.joined:
        pair = [shape(2 * extent, s.lanes, dtype=BF16)]
    else:
        pair = [state, state]

    s_now, posted = run(
        take_start_kernel, [state, state], [start_got, pick_lanes, message_rows], flops=2 * cube
    )
    got = exchange([posted])
    t_now, *messages = run(
        functools.partial(take_columns_kernel, s),
        [state] + pair,
        [got[0], order, keep, right_rows, left_rows, s_now],
        flops=4 * cube,
    )
    start_s, start_t = s_now, t_now
    ys, yt = s_now, t_now
    total = None
    shares = [STEP / 6.0, STEP / 3.0, STEP / 3.0, STEP / 6.0]
    steps = [0.25, 0.25, 0.5]
    for section in range(4):
        got = exchange(messages)
        columns = section < 3
        slopes = run(
            functools.partial(slope_kernel, s, columns),
            [full, full] if columns else [full],
            [s_now, t_now, ys, yt, damp, q_first, right, left, unit_tile, wa_s, wb_s, wa_t, wb_t],
            scratch=[held_b],
            flops=(12 if columns else 6) * cube,
        )
        if columns:
            args = list(got) + [order, swap, right_rows, left_rows, *slopes, start_s, start_t]
            if total is not None:
                args.append(total)
            outs = [state, state, full, full, full]
            outs += pair if section < 2 else [state]
            s_now, t_now, ys, yt, total, *messages = run(
                functools.partial(
                    next_kernel, s, shares[section], steps[section], total is not None, section < 2, len(got)
                ),
                outs,
                args,
                scratch=[held],
                flops=6 * cube,
            )
    change = run(
        functools.partial(last_kernel, s, shares[3]),
        [shape(s.lanes, extent, dtype=BF16)],
        [got[0], order, swap, slopes[0], total, pick_lanes],
        scratch=[held, held_b],
        flops=3 * cube,
    )[0]
    back = lax.all_to_all(
        change.reshape(s.groups, sub, extent), "aux", split_axis=0, concat_axis=0, tiled=True
    ).reshape(s.lanes, extent)
    return run(
        finish_kernel,
        [shape(planes, per_device, band, extent)],
        [back, pick_rows.T, pick_cols.T, density],
        flops=2 * cube,
    )[0]


def solution(mesh):
    return jax.shard_map(
        body,
        mesh=mesh,
        in_specs=(
            P(None, "aux", "row", None),
            P(),
            P(),
            P(),
            P(),
            P("aux", None),
            P(),
            P(),
            P(),
            P(),
            P(),
        ),
        out_specs=P(None, "aux", "row", None),
        check_vma=False,
    )
```

```python
import functools

import jax
import jax.numpy as jnp
from jax import lax
from jax.experimental import pallas as pl
from jax.experimental.pallas import tpu as pltpu
from jax.sharding import PartitionSpec as P

MODES = 4
LINKS = 8
LANES = 128
STEP = 0.5
BOTH = ("aux", "row")

F32 = jnp.float32
BF16 = jnp.bfloat16


class Sizes:
    def __init__(self, groups, rows, per_device, band, extent):
        self.groups, self.rows, self.per_device = groups, rows, per_device
        self.band, self.extent = band, extent
        self.devices = groups * rows
        self.local = band // groups
        self.auxes = per_device * groups
        self.za = 2 * self.auxes
        self.lanes = self.local * self.za
        self.fold = max(1, LANES // self.za)
        self.tile = self.fold * self.za
        self.tiles = self.local // self.fold
        self.joined = self.local % 16 == 0


def dot(a, b, dims=((1,), (0,))):
    return lax.dot_general(a, b, (dims, ((), ())), preferred_element_type=F32)


def run(kernel, outs, args, scratch=(), flops=0, scalars=()):
    spec = pl.BlockSpec(memory_space=pltpu.VMEM)
    flat = pl.BlockSpec(memory_space=pltpu.SMEM)
    moved = sum(a.size * a.dtype.itemsize for a in args)
    moved += sum(o.size * o.dtype.itemsize for o in outs)
    return pl.pallas_call(
        kernel,
        out_shape=list(outs),
        in_specs=[flat if n in scalars else spec for n in range(len(args))],
        out_specs=[spec] * len(outs),
        scratch_shapes=list(scratch),
        compiler_params=pltpu.CompilerParams(vmem_limit_bytes=16 << 20),
        cost_estimate=pl.CostEstimate(flops=flops, bytes_accessed=moved, transcendentals=0),
    )(*args)


def shape(*dims, dtype=F32):
    return jax.ShapeDtypeStruct(dims, dtype)


def one_hot(target, count):
    return (target[:, None] == jnp.arange(count, dtype=jnp.int32)[None, :]).astype(BF16)


def matrix_index(s, index, device):
    group, row = device // s.rows, device % s.rows
    return row * s.band + index * s.groups + group


def row_blocks(extent, size=128):
    return range(0, extent, size)


def send_start_kernel(d_ref, pick_rows, pick_cols, out_ref):
    planes, number, band, extent = d_ref.shape
    flat = d_ref[...].reshape(planes * number * band, extent).astype(BF16)
    for b in row_blocks(flat.shape[0]):
        moved = dot(pick_rows[b : b + 128, :], flat).astype(BF16)
        out_ref[b : b + 128, :] = dot(moved, pick_cols[...]).astype(BF16)


def take_start_kernel(got_ref, pick_lanes, message_rows, s_ref, m_ref):
    for b in row_blocks(got_ref.shape[1]):
        s_ref[b : b + 128, :] = dot(
            got_ref[:, b : b + 128], pick_lanes[...], ((0,), (0,))
        ).astype(BF16)
    for b in row_blocks(m_ref.shape[0]):
        m_ref[b : b + 128, :] = dot(message_rows[b : b + 128, :], s_ref[...]).astype(BF16)


def turn(s, load, order, swap, put):
    size = order.shape[0]
    span = size // s.local
    for block in range(s.extent // size):
        moved = dot(order[...], load(block * size, size))
        parts = []
        for ih in range(s.tiles):
            for jh in range(s.tiles):
                lanes = slice(jh * s.tile, (jh + 1) * s.tile)
                pieces = [
                    moved[(ih * s.fold + f) * span : (ih * s.fold + f + 1) * span, lanes]
                    for f in range(s.fold)
                ]
                parts.append(jnp.concatenate(pieces, axis=1) if s.fold > 1 else pieces[0])
        turned = dot(jnp.concatenate(parts, axis=0).astype(BF16), swap[...])
        for ih in range(s.tiles):
            for jh in range(s.tiles):
                start = (ih * s.tiles + jh) * span
                for f in range(s.fold):
                    first = (jh * s.fold + f) * s.devices + block * span
                    put(
                        slice(first, first + span),
                        slice(ih * s.tile, (ih + 1) * s.tile),
                        turned[start : start + span, f * s.tile : (f + 1) * s.tile],
                    )


def take_columns_kernel(s, got_ref, order, swap, first_rows, left_rows, s_ref, t_ref, *message):
    def put(rows, lanes, value):
        t_ref[rows, lanes] = value.astype(BF16)

    turn(s, lambda start, size: got_ref[start : start + size, :], order, swap, put)
    write_messages(s, first_rows, left_rows, s_ref, t_ref, message)


def write_messages(s, right_rows, left_rows, s_ref, t_ref, message):
    pairs = ((left_rows, t_ref), (right_rows, s_ref))
    if not s.joined and len(message) == 1:
        pairs = pairs[:1]
    both = s.joined and message[0].shape[0] == 2 * s.extent
    for part, (matrix, state) in enumerate(pairs):
        if s.joined and part == 1 and not both:
            continue
        for b in row_blocks(s.extent):
            product = dot(matrix[b : b + 128, :], state[...]).astype(BF16)
            if not s.joined:
                message[part][b : b + 128, :] = product
            elif not both:
                message[0][b : b + 128, :] = product
            else:
                for k in range(128 // s.local):
                    start = ((b // s.local + k) * 2 + part) * s.local
                    message[0][start : start + s.local, :] = product[
                        k * s.local : (k + 1) * s.local, :
                    ]


def slope_kernel(
    s, with_columns, s_ref, t_ref, ys_ref, yt_ref, damp, q_ref, right, left, unit, wa_s, wb_s, wa_t, wb_t, *rest
):
    if with_columns:
        ks_ref, kt_ref, turned = rest
    else:
        ks_ref, turned = rest

    def one(direct, mirror, y_ref, h, wa, wb, out_ref, sign):
        for th in range(s.tiles):
            lanes = slice(th * s.tile, (th + 1) * s.tile)
            turned[:, lanes] = dot(direct[:, lanes], unit[...]).astype(BF16)
        for b in row_blocks(s.extent):
            rows = slice(b, b + 128)
            whole = dot(h[rows, :], turned[...])
            for th in range(s.tiles):
                lanes = slice(th * s.tile, (th + 1) * s.tile)
                source = jnp.concatenate([direct[rows, lanes], mirror[rows, lanes]], axis=1)
                source = jnp.concatenate([source, source], axis=1)
                total = dot(source, wa[th]) - damp[:, lanes] * y_ref[rows, lanes].astype(F32)
                total = total + sign * whole[:, lanes]
                fields = dot(source, wb[...])
                for k in range(MODES):
                    total = total + q_ref[rows, k : k + 1] * fields[:, k * s.tile : (k + 1) * s.tile]
                out_ref[rows, lanes] = total

    one(s_ref, t_ref, ys_ref, right, wa_s, wb_s, ks_ref, -1.0)
    if with_columns:
        one(t_ref, s_ref, yt_ref, left, wa_t, wb_t, kt_ref, 1.0)


def part_loader(s, refs, part):
    def load(start, size):
        if not s.joined:
            return refs[part][start : start + size, :]
        step = s.local
        pieces = []
        for first in range(start, start + size, step):
            at = (first // step * 2 + part) * step
            pieces.append(refs[0][at : at + step, :])
        return jnp.concatenate(pieces, axis=0)

    return load


def next_kernel(s, weight, step, has_total, both, got_count, *refs):
    got = refs[:got_count]
    refs = refs[got_count:]
    order, swap, right_rows, left_rows, ks_ref, kt_ref, ds_ref, dt_ref = refs[:8]
    refs = refs[8:]
    total_in = None
    if has_total:
        total_in, refs = refs[0], refs[1:]
    s_ref, t_ref, ys_ref, yt_ref, total_ref = refs[:5]
    message, arrived = refs[5:-1], refs[-1]

    def put(rows, lanes, value):
        arrived[rows, lanes] = value

    for part in range(2):
        turn(s, part_loader(s, got, part), order, swap, put)
        for b in row_blocks(s.extent, 64):
            rows = slice(b, b + 64)
            if part == 0:
                slope = ks_ref[rows, :] + arrived[rows, :]
                grown = weight * slope
                total_ref[rows, :] = total_in[rows, :] + grown if has_total else grown
                state = ds_ref[rows, :].astype(F32) + step * slope
                ys_ref[rows, :] = state
                s_ref[rows, :] = state.astype(BF16)
            else:
                slope = kt_ref[rows, :] - arrived[rows, :]
                state = dt_ref[rows, :].astype(F32) + step * slope
                yt_ref[rows, :] = state
                t_ref[rows, :] = state.astype(BF16)
    if message:
        write_messages(s, right_rows, left_rows, s_ref, t_ref, message)


def last_kernel(s, weight, got_ref, order, swap, ks_ref, total_in, pick_lanes, out_ref, arrived, grown):
    def put(rows, lanes, value):
        arrived[rows, lanes] = value

    turn(s, lambda start, size: got_ref[start : start + size, :], order, swap, put)
    for b in row_blocks(s.extent, 64):
        rows = slice(b, b + 64)
        change = total_in[rows, :] + weight * (ks_ref[rows, :] + arrived[rows, :])
        grown[rows, :] = change.astype(BF16)
    for b in row_blocks(s.lanes):
        out_ref[b : b + 128, :] = dot(
            pick_lanes[b : b + 128, :], grown[...], ((1,), (1,))
        ).astype(BF16)


def finish_kernel(got_ref, place_rows, place_cols, d_ref, out_ref):
    planes, number, band, extent = d_ref.shape
    for z in range(planes):
        for n in range(number):
            at = (z * number + n) * band
            for b in range(0, band, min(band, 128)):
                size = min(band, 128)
                rows = slice(at + b, at + b + size)
                moved = dot(place_rows[rows, :], got_ref[...]).astype(BF16)
                out_ref[z, n, b : b + size, :] = d_ref[z, n, b : b + size, :] + dot(
                    moved, place_cols[...]
                )


def link_matrices(s, counts, weight_real, weight_imag, link_index, link_mirror):
    ones = jnp.ones_like(counts)
    real = jnp.stack([ones, counts * weight_real[None, :]], 1)
    imag = jnp.stack([jnp.zeros_like(counts), counts * weight_imag[None, :]], 1)
    index = link_index.reshape(s.auxes, 2, MODES)
    mirror = link_mirror.reshape(s.auxes, 2, MODES)
    source = jnp.arange(s.auxes, dtype=jnp.int32)
    hit = index[None] == source[:, None, None, None]
    kinds = jnp.stack([hit & (mirror[None] == 0), hit & (mirror[None] == 1)]).astype(F32)
    along = jnp.sum(kinds * real, 3)
    cross = jnp.sum(kinds * imag, 3)
    along, cross = (jnp.transpose(m, (0, 3, 1, 2)) for m in (along, cross))
    flip = jnp.array([1.0, -1.0], F32).reshape(2, 1, 1, 1)

    def build(sign):
        upper = jnp.concatenate([cross, -sign * along], 3)
        lower = jnp.concatenate([sign * along, cross], 3) * flip
        return jnp.concatenate([upper, lower], 2)

    return build(1.0), build(-1.0)


def two_pieces(weights, axis):
    high = lax.reduce_precision(weights, 8, 7)
    low = weights - high
    return jnp.concatenate([high.astype(BF16), low.astype(BF16)], axis)


def coupling_weights(s, by_local, by_first, local_q):
    eye = jnp.eye(s.fold, dtype=F32)
    near = jnp.einsum("ki,xkuv->ixuv", local_q, by_local, precision=lax.Precision.HIGHEST)
    near = near.reshape(s.tiles, s.fold, 2, s.za, s.za)
    near = jnp.transpose(near, (0, 2, 1, 3, 4))[:, :, :, :, None, :] * eye[None, None, :, None, :, None]
    near = near.reshape(s.tiles, 2 * s.tile, s.tile)
    far = jnp.transpose(by_first, (0, 2, 1, 3))[:, None, :, :, None, :] * eye[None, :, None, None, :, None]
    far = far.reshape(2 * s.tile, MODES * s.tile)
    return two_pieces(near, 1), two_pieces(far, 0)


def general_body(
    density,
    couplings,
    weight_real,
    weight_imag,
    mode_rates,
    tier_counts,
    link_index,
    link_mirror,
    block_diagonal,
    block_outer,
    block_column,
):
    planes, per_device, band, extent = density.shape
    s = Sizes(lax.axis_size("aux"), lax.axis_size("row"), per_device, band, extent)
    blocks, block = block_diagonal.shape[0], block_diagonal.shape[1]
    group, row = lax.axis_index("aux"), lax.axis_index("row")
    device = group * s.rows + row
    cube = 2 * extent * extent * s.lanes

    number = jnp.arange(extent, dtype=jnp.int32)
    first_to_matrix = matrix_index(s, number // s.devices, number % s.devices)
    posted_to_matrix = matrix_index(s, number % s.local, number // s.local)
    posted_to_first = number % s.local * s.devices + number // s.local

    wide = jnp.arange(s.lanes, dtype=jnp.int32)
    sub = planes * per_device * s.local
    start_source = wide % sub * s.groups + wide // sub
    pick_rows = one_hot(start_source, s.lanes)
    pick_cols = one_hot(first_to_matrix, extent).T
    lane_of = (
        wide % s.local * s.za
        + wide // (per_device * s.local) % planes * s.auxes
        + wide // sub * per_device
        + wide // s.local % per_device
    )
    pick_lanes = one_hot(lane_of, s.lanes)
    message_rows = one_hot(posted_to_first, extent)
    start_message = run(
        send_start_kernel,
        [shape(s.lanes, extent, dtype=BF16)],
        [density, pick_rows, pick_cols],
        flops=2 * cube,
    )[0]
    start_got = lax.all_to_all(
        start_message.reshape(s.groups, sub, extent), "aux", split_axis=0, concat_axis=0, tiled=True
    ).reshape(s.lanes, extent)

    selector = block_column[:, None] == jnp.arange(blocks, dtype=jnp.int32)[None, :]
    own = jnp.eye(blocks, dtype=F32)
    whole_h = (
        own[:, None, :, None] * block_diagonal.astype(F32)[:, :, None, :]
        + selector.astype(F32)[:, None, :, None] * block_outer.astype(F32)[:, :, None, :]
    ).reshape(extent, extent).astype(BF16)
    first_h = one_hot(first_to_matrix, extent)
    left = jnp.dot(
        jnp.dot(first_h, whole_h, preferred_element_type=BF16), first_h.T, preferred_element_type=BF16
    )
    right = left.T
    left_rows = jnp.dot(message_rows, left, preferred_element_type=BF16)
    right_rows = jnp.dot(message_rows, right, preferred_element_type=BF16)

    counts = lax.all_gather(tier_counts, "aux", axis=0, tiled=True).astype(F32)
    damping = jnp.sum(counts * mode_rates[None, :], axis=1)
    damp = jnp.tile(damping, (planes * s.local,))[None, :]
    q_first = jnp.dot(
        couplings, first_h.T.astype(F32), precision=lax.Precision.HIGHEST
    ).T
    local_pick = (matrix_index(s, jnp.arange(s.local, dtype=jnp.int32), device)[None, :] == number[:, None])
    local_q = jnp.dot(couplings, local_pick.astype(F32), precision=lax.Precision.HIGHEST)
    by_row, by_column = link_matrices(s, counts, weight_real, weight_imag, link_index, link_mirror)
    wa_s, wb_s = coupling_weights(s, by_row, by_column, local_q)
    wa_t, wb_t = coupling_weights(s, by_column, by_row, local_q)

    lane = jnp.arange(s.za, dtype=jnp.int32)
    unit = jnp.where(
        lane[:, None] == (lane[None, :] + s.auxes) % s.za,
        jnp.where(lane[None, :] < s.auxes, 1.0, -1.0),
        0.0,
    )
    eye_fold = jnp.eye(s.fold, dtype=F32)
    unit_tile = (eye_fold[:, None, :, None] * unit[None, :, None, :]).reshape(s.tile, s.tile).astype(BF16)
    swap = (
        eye_fold[:, None, None, None, :, None]
        * eye_fold[None, :, None, :, None, None]
        * unit[None, None, :, None, None, :]
    ).reshape(s.fold * s.tile, s.fold * s.tile).astype(BF16)
    keep = (
        eye_fold[:, None, None, None, :, None]
        * eye_fold[None, :, None, :, None, None]
        * jnp.eye(s.za, dtype=F32)[None, None, :, None, None, :]
    ).reshape(s.fold * s.tile, s.fold * s.tile).astype(BF16)
    size = min(extent, max(256, 16 * s.local))
    span = size // s.local
    at = jnp.arange(size, dtype=jnp.int32)
    order = one_hot(at % span * s.local + at // span, size)

    state = shape(extent, s.lanes, dtype=BF16)
    full = shape(extent, s.lanes)
    held = pltpu.VMEM((extent, s.lanes), F32)
    held_b = pltpu.VMEM((extent, s.lanes), BF16)

    def exchange(messages):
        parts = [m.reshape(s.devices, -1, s.lanes) for m in messages]
        sent = parts[0] if len(parts) == 1 else jnp.concatenate(parts, 1)
        got = lax.all_to_all(sent, BOTH, split_axis=0, concat_axis=0, tiled=True)
        if len(parts) == 1:
            return [got.reshape(-1, s.lanes)]
        height = s.local
        return [got[:, p * height : (p + 1) * height].reshape(-1, s.lanes) for p in range(2)]

    if s.joined:
        pair = [shape(2 * extent, s.lanes, dtype=BF16)]
    else:
        pair = [state, state]

    s_now, posted = run(
        take_start_kernel, [state, state], [start_got, pick_lanes, message_rows], flops=2 * cube
    )
    got = exchange([posted])
    t_now, *messages = run(
        functools.partial(take_columns_kernel, s),
        [state] + pair,
        [got[0], order, keep, right_rows, left_rows, s_now],
        flops=4 * cube,
    )
    start_s, start_t = s_now, t_now
    ys, yt = s_now, t_now
    total = None
    shares = [STEP / 6.0, STEP / 3.0, STEP / 3.0, STEP / 6.0]
    steps = [0.25, 0.25, 0.5]
    for section in range(4):
        got = exchange(messages)
        columns = section < 3
        slopes = run(
            functools.partial(slope_kernel, s, columns),
            [full, full] if columns else [full],
            [s_now, t_now, ys, yt, damp, q_first, right, left, unit_tile, wa_s, wb_s, wa_t, wb_t],
            scratch=[held_b],
            flops=(12 if columns else 6) * cube,
        )
        if columns:
            args = list(got) + [order, swap, right_rows, left_rows, *slopes, start_s, start_t]
            if total is not None:
                args.append(total)
            outs = [state, state, full, full, full]
            outs += pair if section < 2 else [state]
            s_now, t_now, ys, yt, total, *messages = run(
                functools.partial(
                    next_kernel, s, shares[section], steps[section], total is not None, section < 2, len(got)
                ),
                outs,
                args,
                scratch=[held],
                flops=6 * cube,
            )
    change = run(
        functools.partial(last_kernel, s, shares[3]),
        [shape(s.lanes, extent, dtype=BF16)],
        [got[0], order, swap, slopes[0], total, pick_lanes],
        scratch=[held, held_b],
        flops=3 * cube,
    )[0]
    back = lax.all_to_all(
        change.reshape(s.groups, sub, extent), "aux", split_axis=0, concat_axis=0, tiled=True
    ).reshape(s.lanes, extent)
    return run(
        finish_kernel,
        [shape(planes, per_device, band, extent)],
        [back, pick_rows.T, pick_cols.T, density],
        flops=2 * cube,
    )[0]


def counts_of_all(s, tier_counts, group):
    if s.groups & (s.groups - 1):
        return lax.all_gather(tier_counts, "aux", axis=0, tiled=True).astype(F32)
    whole = lax.dynamic_update_slice_in_dim(
        jnp.zeros((s.auxes, MODES), F32), tier_counts.astype(F32), group * s.per_device, 0
    )
    step = 1
    while step < s.groups:
        whole = whole + lax.ppermute(whole, "aux", [(i, i ^ step) for i in range(s.groups)])
        step *= 2
    return whole


def iotas(rows, columns):
    return (
        lax.broadcasted_iota(jnp.int32, (rows, columns), 0),
        lax.broadcasted_iota(jnp.int32, (rows, columns), 1),
    )


def post_matrix(s):
    row, column = iotas(s.extent, s.extent)
    return (column == row % s.local * s.devices + row // s.local).astype(F32).astype(BF16)


def place(s, message, part, first, value, lanes=slice(None)):
    for k in range(value.shape[0] // s.local):
        start = ((first // s.local + k) * 2 + part) * s.local
        message[start : start + s.local, lanes] = value[k * s.local : (k + 1) * s.local, :]


def even_start_kernel(s, d_ref, out_ref, post):
    planes, number, band, extent = d_ref.shape
    post[...] = post_matrix(s)
    flat = d_ref[...].reshape(planes * number * band, extent).astype(BF16)
    for b in row_blocks(extent):
        place(s, out_ref, 0, b, dot(post[b : b + 128, :], flat).astype(BF16))
        place(s, out_ref, 1, b, dot(post[b : b + 128, :], flat, ((1,), (1,))).astype(BF16))


def part_rows(s, got_ref, part, devices, lanes=slice(None)):
    pieces = [
        got_ref[(d * 2 + part) * s.local : (d * 2 + part + 1) * s.local, lanes] for d in devices
    ]
    return jnp.concatenate(pieces, axis=0)


def even_take_kernel(s, got_ref, row_lanes, column_lanes, right_rows, left_rows, s_ref, t_ref, message):
    everyone = range(s.devices)
    for b in row_blocks(s.extent):
        s_ref[b : b + 128, :] = dot(
            part_rows(s, got_ref, 0, everyone, slice(b, b + 128)), row_lanes[...], ((0,), (0,))
        ).astype(BF16)
    for q in range(s.rows):
        owners = [g * s.rows + q for g in range(s.groups)]
        pieces = [
            part_rows(s, got_ref, 1, owners, slice(v * s.band, (v + 1) * s.band))
            for v in range(s.extent // s.band)
        ]
        t_ref[q * s.band : (q + 1) * s.band, :] = dot(
            jnp.concatenate(pieces, axis=0), column_lanes[...], ((0,), (0,))
        ).astype(BF16)
    write_messages(s, right_rows, left_rows, s_ref, t_ref, [message])


def even_last_kernel(s, weight, ks_ref, total_in, t_ref, left, unit, row_lanes, column_lanes, out_ref, grown, turned):
    for th in range(s.tiles):
        lanes = slice(th * s.tile, (th + 1) * s.tile)
        turned[:, lanes] = dot(t_ref[:, lanes], unit[...]).astype(BF16)
    for b in row_blocks(s.extent):
        rows = slice(b, b + 128)
        grown[rows, :] = (total_in[rows, :] + weight * ks_ref[rows, :]).astype(BF16)
    for b in row_blocks(s.extent):
        place(s, out_ref, 0, b, dot(row_lanes[b : b + 128, :], grown[...], ((1,), (1,))).astype(BF16))
    for b in row_blocks(s.extent):
        rows = slice(b, b + 128)
        grown[rows, :] = (weight * dot(left[rows, :], turned[...])).astype(BF16)
    for q in range(s.rows):
        value = dot(column_lanes[...], grown[q * s.band : (q + 1) * s.band, :], ((1,), (1,))).astype(BF16)
        for v in range(s.extent // s.band):
            for g in range(s.groups):
                at = (v * s.groups + g) * s.local
                start = ((g * s.rows + q) * 2 + 1) * s.local
                out_ref[start : start + s.local, v * s.band : (v + 1) * s.band] = value[at : at + s.local, :]


def even_finish_kernel(s, got_ref, d_ref, out_ref, post, moved):
    planes, number, band, extent = d_ref.shape
    post[...] = post_matrix(s)
    everyone = range(s.devices)
    for d in everyone:
        moved[d * s.local : (d + 1) * s.local, :] = got_ref[d * 2 * s.local : (d * 2 + 1) * s.local, :]
    for z in range(planes):
        for n in range(number):
            at = (z * number + n) * band
            lanes = slice(at, at + band)
            change = dot(post[:, lanes], moved[...], ((0,), (0,)))
            change = change + dot(part_rows(s, got_ref, 1, everyone, lanes), post[...], ((0,), (0,)))
            out_ref[z, n] = d_ref[z, n] + change


def hamiltonian_kernel(s, own_ref, outer_ref, where_ref, left, right, left_rows, right_rows, post):
    blocks, block = own_ref.shape[0], own_ref.shape[1]
    post[...] = post_matrix(s)
    row, column = iotas(block, s.extent)
    for b in range(blocks):
        spread = column - row
        to_own = (spread == b * block).astype(F32).astype(BF16)
        to_far = (spread == where_ref[b] * block).astype(F32).astype(BF16)
        left[b * block : (b + 1) * block, :] = (dot(own_ref[b], to_own) + dot(outer_ref[b], to_far)).astype(BF16)
    row, column = iotas(s.extent, s.extent)
    same = (row == column).astype(F32).astype(BF16)
    for b in row_blocks(s.extent):
        rows = slice(b, b + 128)
        right[rows, :] = dot(same[rows, :], left[...], ((1,), (1,))).astype(BF16)
        left_rows[rows, :] = dot(post[rows, :], left[...]).astype(BF16)
        right_rows[rows, :] = dot(post[rows, :], left[...], ((1,), (1,))).astype(BF16)


def weights_kernel(s, table, local_q, wa_s, wb_s, wa_t, wb_t):
    depth, wide = 2 * s.tile, MODES * s.tile
    row, column = iotas(depth, wide)
    same = row // s.za % s.fold == column // s.za % s.fold
    source, kind = (row % s.auxes).astype(F32), (row // s.tile).astype(F32)
    from_imag, to_imag = row // s.auxes % 2, column // s.auxes % 2
    up = same & (table[0:1, :] == source) & (table[2:3, :] == kind)
    down = same & (table[1:2, :] == source) & (table[3:4, :] == kind)
    along = jnp.where(up, 1.0, 0.0) + jnp.where(down, table[4:5, :], 0.0)
    cross = jnp.where(down, table[5:6, :], 0.0)
    along = jnp.where(from_imag == 1, along, -along)
    flip = jnp.where((from_imag == 1) & (row // s.tile == 1), -1.0, 1.0)
    by_row = flip * jnp.where(from_imag == to_imag, cross, along)
    by_column = flip * jnp.where(from_imag == to_imag, cross, -along)

    def pieces(value):
        high = value.astype(BF16)
        return high, (value - high.astype(F32)).astype(BF16)

    for near, far, wa, wb in ((by_row, by_column, wa_s, wb_s), (by_column, by_row, wa_t, wb_t)):
        wb[:depth, :], wb[depth:, :] = pieces(far)
        for th in range(s.tiles):
            lanes = slice(th * s.tile, (th + 1) * s.tile)
            total = local_q[0:1, lanes] * near[:, : s.tile]
            for k in range(1, MODES):
                total = total + local_q[k : k + 1, lanes] * near[:, k * s.tile : (k + 1) * s.tile]
            wa[th, :depth, :], wa[th, depth:, :] = pieces(total)


def even_body(
    s,
    density,
    couplings,
    weight_real,
    weight_imag,
    mode_rates,
    tier_counts,
    link_index,
    link_mirror,
    block_diagonal,
    block_outer,
    block_column,
):
    planes, per_device, band, extent = density.shape
    group, row = lax.axis_index("aux"), lax.axis_index("row")
    device = group * s.rows + row
    cube = 2 * extent * extent * s.lanes
    state = shape(extent, s.lanes, dtype=BF16)
    full = shape(extent, s.lanes)
    pair = shape(2 * extent, s.lanes, dtype=BF16)
    held = pltpu.VMEM((extent, s.lanes), F32)
    held_b = pltpu.VMEM((extent, s.lanes), BF16)

    def exchange(message):
        sent = message.reshape(s.devices, -1, s.lanes)
        got = lax.all_to_all(sent, BOTH, split_axis=0, concat_axis=0, tiled=True)
        return got.reshape(-1, s.lanes)

    counts = counts_of_all(s, tier_counts, group)
    message = run(functools.partial(even_start_kernel, s), [pair], [density], scratch=[held_b], flops=2 * cube)[0]
    got = exchange(message)

    left, right, left_rows, right_rows = run(
        functools.partial(hamiltonian_kernel, s),
        [state] * 4,
        [block_diagonal, block_outer, block_column],
        scratch=[held_b],
        flops=4 * cube,
        scalars=(2,),
    )

    def in_lanes(by_mode):
        spread = jnp.broadcast_to(by_mode[:, None, :], (MODES, 2 * s.fold, s.auxes))
        return spread.reshape(1, MODES * s.tile)

    index = link_index.T.astype(F32)
    mirror = link_mirror.T.astype(F32)
    table = jnp.concatenate(
        [
            in_lanes(index[:MODES]),
            in_lanes(index[MODES:]),
            in_lanes(mirror[:MODES]),
            in_lanes(mirror[MODES:]),
            in_lanes((counts * weight_real[None, :]).T),
            in_lanes((counts * weight_imag[None, :]).T),
        ]
    )
    mine = lax.dynamic_slice_in_dim(couplings.reshape(MODES, s.local, s.devices), device, 1, 2)
    local_q = jnp.broadcast_to(mine, (MODES, s.local, s.za)).reshape(MODES, s.lanes)
    wa = shape(s.tiles, 4 * s.tile, s.tile, dtype=BF16)
    wb = shape(4 * s.tile, MODES * s.tile, dtype=BF16)
    wa_s, wb_s, wa_t, wb_t = run(
        functools.partial(weights_kernel, s), [wa, wb, wa, wb], [table, local_q]
    )
    damping = jnp.sum(counts * mode_rates[None, :], axis=1)
    damp = jnp.tile(damping, (planes * s.local,))[None, :]
    q_first = couplings.T

    k, n = iotas(s.lanes, s.lanes)
    parts = band // s.devices
    row_lanes = (
        n
        == (k // s.local % s.rows * parts + k % parts) * s.za
        + k // (parts * per_device) % planes * s.auxes
        + k // (s.local * s.rows) * per_device
        + k // parts % per_device
    ).astype(BF16)
    column_lanes = (
        n
        == k % s.local * s.za
        + k // (s.local * s.groups * per_device) * s.auxes
        + k // s.local % s.groups * per_device
        + k // (s.local * s.groups) % per_device
    ).astype(BF16)

    k, n = iotas(s.tile, s.tile)
    sign = jnp.where(n // s.auxes % 2 == 0, 1.0, -1.0)
    unit = jnp.where(k // s.za * s.za + (k + s.auxes) % s.za == n, sign, 0.0).astype(BF16)
    k, n = iotas(s.fold * s.tile, s.fold * s.tile)
    sign = jnp.where(n // s.auxes % 2 == 0, 1.0, -1.0)
    there = (k // s.za % s.fold * s.fold + k // s.tile) * s.za + (k + s.auxes) % s.za
    swap = jnp.where(there == n, sign, 0.0).astype(BF16)
    size = max(256, 16 * s.local)
    span = size // s.local
    k, n = iotas(size, size)
    order = (n == k % span * s.local + k // span).astype(BF16)

    s_now, t_now, message = run(
        functools.partial(even_take_kernel, s),
        [state, state, pair],
        [got, row_lanes, column_lanes, right_rows, left_rows],
        flops=4 * cube,
    )
    start_s, start_t = s_now, t_now
    ys, yt = s_now, t_now
    total = None
    shares = [STEP / 6.0, STEP / 3.0, STEP / 3.0, STEP / 6.0]
    steps = [0.25, 0.25, 0.5]
    for section in range(4):
        columns = section < 3
        if columns:
            got = exchange(message)
        slopes = run(
            functools.partial(slope_kernel, s, columns),
            [full, full] if columns else [full],
            [s_now, t_now, ys, yt, damp, q_first, right, left, unit, wa_s, wb_s, wa_t, wb_t],
            scratch=[held_b],
            flops=(12 if columns else 6) * cube,
        )
        if columns:
            args = [got, order, swap, right_rows, left_rows, *slopes, start_s, start_t]
            if total is not None:
                args.append(total)
            outs = [state, state, full, full, full]
            more = section < 2
            if more:
                outs.append(pair)
            s_now, t_now, ys, yt, total, *message = run(
                functools.partial(next_kernel, s, shares[section], steps[section], total is not None, more, 1),
                outs,
                args,
                scratch=[held],
                flops=6 * cube,
            )
            message = message[0] if more else None
    message = run(
        functools.partial(even_last_kernel, s, shares[3]),
        [pair],
        [slopes[0], total, t_now, left, unit, row_lanes, column_lanes],
        scratch=[held_b, held_b],
        flops=3 * cube,
    )[0]
    got = exchange(message)
    return run(
        functools.partial(even_finish_kernel, s),
        [shape(planes, per_device, band, extent)],
        [got, density],
        scratch=[held_b, held_b],
        flops=2 * cube,
    )[0]


def body(density, *others):
    planes, per_device, band, extent = density.shape
    s = Sizes(lax.axis_size("aux"), lax.axis_size("row"), per_device, band, extent)
    even = band % s.devices == 0 and s.local % 16 == 0 and LANES % s.za == 0
    if even and s.lanes == extent and planes * per_device * band == extent:
        return even_body(s, density, *others)
    return general_body(density, *others)


def solution(mesh):
    return jax.shard_map(
        body,
        mesh=mesh,
        in_specs=(
            P(None, "aux", "row", None),
            P(),
            P(),
            P(),
            P(),
            P("aux", None),
            P(),
            P(),
            P(),
            P(),
            P(),
        ),
        out_specs=P(None, "aux", "row", None),
        check_vma=False,
    )
```

```python
import functools

import jax
import jax.numpy as jnp
from jax import lax
from jax.experimental import pallas as pl
from jax.experimental.pallas import tpu as pltpu
from jax.sharding import PartitionSpec as P

MODES = 4
LINKS = 8
LANES = 128
STEP = 0.5
BOTH = ("aux", "row")

F32 = jnp.float32
BF16 = jnp.bfloat16


class Sizes:
    def __init__(self, groups, rows, per_device, band, extent):
        self.groups, self.rows, self.per_device = groups, rows, per_device
        self.band, self.extent = band, extent
        self.devices = groups * rows
        self.local = band // groups
        self.auxes = per_device * groups
        self.za = 2 * self.auxes
        self.lanes = self.local * self.za
        self.fold = max(1, LANES // self.za)
        self.tile = self.fold * self.za
        self.tiles = self.local // self.fold
        self.joined = self.local % 16 == 0


def dot(a, b, dims=((1,), (0,))):
    return lax.dot_general(a, b, (dims, ((), ())), preferred_element_type=F32)


def run(kernel, outs, args, scratch=(), flops=0, scalars=()):
    spec = pl.BlockSpec(memory_space=pltpu.VMEM)
    flat = pl.BlockSpec(memory_space=pltpu.SMEM)
    moved = sum(a.size * a.dtype.itemsize for a in args)
    moved += sum(o.size * o.dtype.itemsize for o in outs)
    return pl.pallas_call(
        kernel,
        out_shape=list(outs),
        in_specs=[flat if n in scalars else spec for n in range(len(args))],
        out_specs=[spec] * len(outs),
        scratch_shapes=list(scratch),
        compiler_params=pltpu.CompilerParams(vmem_limit_bytes=16 << 20),
        cost_estimate=pl.CostEstimate(flops=flops, bytes_accessed=moved, transcendentals=0),
    )(*args)


def shape(*dims, dtype=F32):
    return jax.ShapeDtypeStruct(dims, dtype)


def one_hot(target, count):
    return (target[:, None] == jnp.arange(count, dtype=jnp.int32)[None, :]).astype(BF16)


def matrix_index(s, index, device):
    group, row = device // s.rows, device % s.rows
    return row * s.band + index * s.groups + group


def row_blocks(extent, size=128):
    return range(0, extent, size)


def send_start_kernel(d_ref, pick_rows, pick_cols, out_ref):
    planes, number, band, extent = d_ref.shape
    flat = d_ref[...].reshape(planes * number * band, extent).astype(BF16)
    for b in row_blocks(flat.shape[0]):
        moved = dot(pick_rows[b : b + 128, :], flat).astype(BF16)
        out_ref[b : b + 128, :] = dot(moved, pick_cols[...]).astype(BF16)


def take_start_kernel(got_ref, pick_lanes, message_rows, s_ref, m_ref):
    for b in row_blocks(got_ref.shape[1]):
        s_ref[b : b + 128, :] = dot(
            got_ref[:, b : b + 128], pick_lanes[...], ((0,), (0,))
        ).astype(BF16)
    for b in row_blocks(m_ref.shape[0]):
        m_ref[b : b + 128, :] = dot(message_rows[b : b + 128, :], s_ref[...]).astype(BF16)


def turn(s, load, order, swap, put):
    size = order.shape[0]
    span = size // s.local
    for block in range(s.extent // size):
        moved = dot(order[...], load(block * size, size))
        parts = []
        for ih in range(s.tiles):
            for jh in range(s.tiles):
                lanes = slice(jh * s.tile, (jh + 1) * s.tile)
                pieces = [
                    moved[(ih * s.fold + f) * span : (ih * s.fold + f + 1) * span, lanes]
                    for f in range(s.fold)
                ]
                parts.append(jnp.concatenate(pieces, axis=1) if s.fold > 1 else pieces[0])
        turned = dot(jnp.concatenate(parts, axis=0).astype(BF16), swap[...])
        for ih in range(s.tiles):
            for jh in range(s.tiles):
                start = (ih * s.tiles + jh) * span
                for f in range(s.fold):
                    first = (jh * s.fold + f) * s.devices + block * span
                    put(
                        slice(first, first + span),
                        slice(ih * s.tile, (ih + 1) * s.tile),
                        turned[start : start + span, f * s.tile : (f + 1) * s.tile],
                    )


def take_columns_kernel(s, got_ref, order, swap, first_rows, left_rows, s_ref, t_ref, *message):
    def put(rows, lanes, value):
        t_ref[rows, lanes] = value.astype(BF16)

    turn(s, lambda start, size: got_ref[start : start + size, :], order, swap, put)
    write_messages(s, first_rows, left_rows, s_ref, t_ref, message)


def write_messages(s, right_rows, left_rows, s_ref, t_ref, message):
    pairs = ((left_rows, t_ref), (right_rows, s_ref))
    if not s.joined and len(message) == 1:
        pairs = pairs[:1]
    both = s.joined and message[0].shape[0] == 2 * s.extent
    for part, (matrix, state) in enumerate(pairs):
        if s.joined and part == 1 and not both:
            continue
        for b in row_blocks(s.extent):
            product = dot(matrix[b : b + 128, :], state[...]).astype(BF16)
            if not s.joined:
                message[part][b : b + 128, :] = product
            elif not both:
                message[0][b : b + 128, :] = product
            else:
                for k in range(128 // s.local):
                    start = ((b // s.local + k) * 2 + part) * s.local
                    message[0][start : start + s.local, :] = product[
                        k * s.local : (k + 1) * s.local, :
                    ]


def slope_kernel(
    s, with_columns, s_ref, t_ref, ys_ref, yt_ref, damp, q_ref, right, left, unit, wa_s, wb_s, wa_t, wb_t, *rest
):
    if with_columns:
        ks_ref, kt_ref, turned = rest
    else:
        ks_ref, turned = rest

    def one(direct, mirror, y_ref, h, wa, wb, out_ref, sign):
        for th in range(s.tiles):
            lanes = slice(th * s.tile, (th + 1) * s.tile)
            turned[:, lanes] = dot(direct[:, lanes], unit[...]).astype(BF16)
        for b in row_blocks(s.extent):
            rows = slice(b, b + 128)
            whole = dot(h[rows, :], turned[...])
            for th in range(s.tiles):
                lanes = slice(th * s.tile, (th + 1) * s.tile)
                source = jnp.concatenate([direct[rows, lanes], mirror[rows, lanes]], axis=1)
                source = jnp.concatenate([source, source], axis=1)
                total = dot(source, wa[th]) - damp[:, lanes] * y_ref[rows, lanes].astype(F32)
                total = total + sign * whole[:, lanes]
                fields = dot(source, wb[...])
                for k in range(MODES):
                    total = total + q_ref[rows, k : k + 1] * fields[:, k * s.tile : (k + 1) * s.tile]
                out_ref[rows, lanes] = total

    one(s_ref, t_ref, ys_ref, right, wa_s, wb_s, ks_ref, -1.0)
    if with_columns:
        one(t_ref, s_ref, yt_ref, left, wa_t, wb_t, kt_ref, 1.0)


def part_loader(s, refs, part):
    def load(start, size):
        if not s.joined:
            return refs[part][start : start + size, :]
        step = s.local
        pieces = []
        for first in range(start, start + size, step):
            at = (first // step * 2 + part) * step
            pieces.append(refs[0][at : at + step, :])
        return jnp.concatenate(pieces, axis=0)

    return load


def next_kernel(s, weight, step, has_total, both, got_count, *refs):
    got = refs[:got_count]
    refs = refs[got_count:]
    order, swap, right_rows, left_rows, ks_ref, kt_ref, ds_ref, dt_ref = refs[:8]
    refs = refs[8:]
    total_in = None
    if has_total:
        total_in, refs = refs[0], refs[1:]
    s_ref, t_ref, ys_ref, yt_ref, total_ref = refs[:5]
    message, arrived = refs[5:-1], refs[-1]

    def put(rows, lanes, value):
        arrived[rows, lanes] = value

    for part in range(2):
        turn(s, part_loader(s, got, part), order, swap, put)
        for b in row_blocks(s.extent, 64):
            rows = slice(b, b + 64)
            if part == 0:
                slope = ks_ref[rows, :] + arrived[rows, :]
                grown = weight * slope
                total_ref[rows, :] = total_in[rows, :] + grown if has_total else grown
                state = ds_ref[rows, :].astype(F32) + step * slope
                ys_ref[rows, :] = state
                s_ref[rows, :] = state.astype(BF16)
            else:
                slope = kt_ref[rows, :] - arrived[rows, :]
                state = dt_ref[rows, :].astype(F32) + step * slope
                yt_ref[rows, :] = state
                t_ref[rows, :] = state.astype(BF16)
    if message:
        write_messages(s, right_rows, left_rows, s_ref, t_ref, message)


def last_kernel(s, weight, got_ref, order, swap, ks_ref, total_in, pick_lanes, out_ref, arrived, grown):
    def put(rows, lanes, value):
        arrived[rows, lanes] = value

    turn(s, lambda start, size: got_ref[start : start + size, :], order, swap, put)
    for b in row_blocks(s.extent, 64):
        rows = slice(b, b + 64)
        change = total_in[rows, :] + weight * (ks_ref[rows, :] + arrived[rows, :])
        grown[rows, :] = change.astype(BF16)
    for b in row_blocks(s.lanes):
        out_ref[b : b + 128, :] = dot(
            pick_lanes[b : b + 128, :], grown[...], ((1,), (1,))
        ).astype(BF16)


def finish_kernel(got_ref, place_rows, place_cols, d_ref, out_ref):
    planes, number, band, extent = d_ref.shape
    for z in range(planes):
        for n in range(number):
            at = (z * number + n) * band
            for b in range(0, band, min(band, 128)):
                size = min(band, 128)
                rows = slice(at + b, at + b + size)
                moved = dot(place_rows[rows, :], got_ref[...]).astype(BF16)
                out_ref[z, n, b : b + size, :] = d_ref[z, n, b : b + size, :] + dot(
                    moved, place_cols[...]
                )


def link_matrices(s, counts, weight_real, weight_imag, link_index, link_mirror):
    ones = jnp.ones_like(counts)
    real = jnp.stack([ones, counts * weight_real[None, :]], 1)
    imag = jnp.stack([jnp.zeros_like(counts), counts * weight_imag[None, :]], 1)
    index = link_index.reshape(s.auxes, 2, MODES)
    mirror = link_mirror.reshape(s.auxes, 2, MODES)
    source = jnp.arange(s.auxes, dtype=jnp.int32)
    hit = index[None] == source[:, None, None, None]
    kinds = jnp.stack([hit & (mirror[None] == 0), hit & (mirror[None] == 1)]).astype(F32)
    along = jnp.sum(kinds * real, 3)
    cross = jnp.sum(kinds * imag, 3)
    along, cross = (jnp.transpose(m, (0, 3, 1, 2)) for m in (along, cross))
    flip = jnp.array([1.0, -1.0], F32).reshape(2, 1, 1, 1)

    def build(sign):
        upper = jnp.concatenate([cross, -sign * along], 3)
        lower = jnp.concatenate([sign * along, cross], 3) * flip
        return jnp.concatenate([upper, lower], 2)

    return build(1.0), build(-1.0)


def two_pieces(weights, axis):
    high = lax.reduce_precision(weights, 8, 7)
    low = weights - high
    return jnp.concatenate([high.astype(BF16), low.astype(BF16)], axis)


def coupling_weights(s, by_local, by_first, local_q):
    eye = jnp.eye(s.fold, dtype=F32)
    near = jnp.einsum("ki,xkuv->ixuv", local_q, by_local, precision=lax.Precision.HIGHEST)
    near = near.reshape(s.tiles, s.fold, 2, s.za, s.za)
    near = jnp.transpose(near, (0, 2, 1, 3, 4))[:, :, :, :, None, :] * eye[None, None, :, None, :, None]
    near = near.reshape(s.tiles, 2 * s.tile, s.tile)
    far = jnp.transpose(by_first, (0, 2, 1, 3))[:, None, :, :, None, :] * eye[None, :, None, None, :, None]
    far = far.reshape(2 * s.tile, MODES * s.tile)
    return two_pieces(near, 1), two_pieces(far, 0)


def general_body(
    density,
    couplings,
    weight_real,
    weight_imag,
    mode_rates,
    tier_counts,
    link_index,
    link_mirror,
    block_diagonal,
    block_outer,
    block_column,
):
    planes, per_device, band, extent = density.shape
    s = Sizes(lax.axis_size("aux"), lax.axis_size("row"), per_device, band, extent)
    blocks, block = block_diagonal.shape[0], block_diagonal.shape[1]
    group, row = lax.axis_index("aux"), lax.axis_index("row")
    device = group * s.rows + row
    cube = 2 * extent * extent * s.lanes

    number = jnp.arange(extent, dtype=jnp.int32)
    first_to_matrix = matrix_index(s, number // s.devices, number % s.devices)
    posted_to_matrix = matrix_index(s, number % s.local, number // s.local)
    posted_to_first = number % s.local * s.devices + number // s.local

    wide = jnp.arange(s.lanes, dtype=jnp.int32)
    sub = planes * per_device * s.local
    start_source = wide % sub * s.groups + wide // sub
    pick_rows = one_hot(start_source, s.lanes)
    pick_cols = one_hot(first_to_matrix, extent).T
    lane_of = (
        wide % s.local * s.za
        + wide // (per_device * s.local) % planes * s.auxes
        + wide // sub * per_device
        + wide // s.local % per_device
    )
    pick_lanes = one_hot(lane_of, s.lanes)
    message_rows = one_hot(posted_to_first, extent)
    start_message = run(
        send_start_kernel,
        [shape(s.lanes, extent, dtype=BF16)],
        [density, pick_rows, pick_cols],
        flops=2 * cube,
    )[0]
    start_got = lax.all_to_all(
        start_message.reshape(s.groups, sub, extent), "aux", split_axis=0, concat_axis=0, tiled=True
    ).reshape(s.lanes, extent)

    selector = block_column[:, None] == jnp.arange(blocks, dtype=jnp.int32)[None, :]
    own = jnp.eye(blocks, dtype=F32)
    whole_h = (
        own[:, None, :, None] * block_diagonal.astype(F32)[:, :, None, :]
        + selector.astype(F32)[:, None, :, None] * block_outer.astype(F32)[:, :, None, :]
    ).reshape(extent, extent).astype(BF16)
    first_h = one_hot(first_to_matrix, extent)
    left = jnp.dot(
        jnp.dot(first_h, whole_h, preferred_element_type=BF16), first_h.T, preferred_element_type=BF16
    )
    right = left.T
    left_rows = jnp.dot(message_rows, left, preferred_element_type=BF16)
    right_rows = jnp.dot(message_rows, right, preferred_element_type=BF16)

    counts = lax.all_gather(tier_counts, "aux", axis=0, tiled=True).astype(F32)
    damping = jnp.sum(counts * mode_rates[None, :], axis=1)
    damp = jnp.tile(damping, (planes * s.local,))[None, :]
    q_first = jnp.dot(
        couplings, first_h.T.astype(F32), precision=lax.Precision.HIGHEST
    ).T
    local_pick = (matrix_index(s, jnp.arange(s.local, dtype=jnp.int32), device)[None, :] == number[:, None])
    local_q = jnp.dot(couplings, local_pick.astype(F32), precision=lax.Precision.HIGHEST)
    by_row, by_column = link_matrices(s, counts, weight_real, weight_imag, link_index, link_mirror)
    wa_s, wb_s = coupling_weights(s, by_row, by_column, local_q)
    wa_t, wb_t = coupling_weights(s, by_column, by_row, local_q)

    lane = jnp.arange(s.za, dtype=jnp.int32)
    unit = jnp.where(
        lane[:, None] == (lane[None, :] + s.auxes) % s.za,
        jnp.where(lane[None, :] < s.auxes, 1.0, -1.0),
        0.0,
    )
    eye_fold = jnp.eye(s.fold, dtype=F32)
    unit_tile = (eye_fold[:, None, :, None] * unit[None, :, None, :]).reshape(s.tile, s.tile).astype(BF16)
    swap = (
        eye_fold[:, None, None, None, :, None]
        * eye_fold[None, :, None, :, None, None]
        * unit[None, None, :, None, None, :]
    ).reshape(s.fold * s.tile, s.fold * s.tile).astype(BF16)
    keep = (
        eye_fold[:, None, None, None, :, None]
        * eye_fold[None, :, None, :, None, None]
        * jnp.eye(s.za, dtype=F32)[None, None, :, None, None, :]
    ).reshape(s.fold * s.tile, s.fold * s.tile).astype(BF16)
    size = min(extent, max(256, 16 * s.local))
    span = size // s.local
    at = jnp.arange(size, dtype=jnp.int32)
    order = one_hot(at % span * s.local + at // span, size)

    state = shape(extent, s.lanes, dtype=BF16)
    full = shape(extent, s.lanes)
    held = pltpu.VMEM((extent, s.lanes), F32)
    held_b = pltpu.VMEM((extent, s.lanes), BF16)

    def exchange(messages):
        parts = [m.reshape(s.devices, -1, s.lanes) for m in messages]
        sent = parts[0] if len(parts) == 1 else jnp.concatenate(parts, 1)
        got = lax.all_to_all(sent, BOTH, split_axis=0, concat_axis=0, tiled=True)
        if len(parts) == 1:
            return [got.reshape(-1, s.lanes)]
        height = s.local
        return [got[:, p * height : (p + 1) * height].reshape(-1, s.lanes) for p in range(2)]

    if s.joined:
        pair = [shape(2 * extent, s.lanes, dtype=BF16)]
    else:
        pair = [state, state]

    s_now, posted = run(
        take_start_kernel, [state, state], [start_got, pick_lanes, message_rows], flops=2 * cube
    )
    got = exchange([posted])
    t_now, *messages = run(
        functools.partial(take_columns_kernel, s),
        [state] + pair,
        [got[0], order, keep, right_rows, left_rows, s_now],
        flops=4 * cube,
    )
    start_s, start_t = s_now, t_now
    ys, yt = s_now, t_now
    total = None
    shares = [STEP / 6.0, STEP / 3.0, STEP / 3.0, STEP / 6.0]
    steps = [0.25, 0.25, 0.5]
    for section in range(4):
        got = exchange(messages)
        columns = section < 3
        slopes = run(
            functools.partial(slope_kernel, s, columns),
            [full, full] if columns else [full],
            [s_now, t_now, ys, yt, damp, q_first, right, left, unit_tile, wa_s, wb_s, wa_t, wb_t],
            scratch=[held_b],
            flops=(12 if columns else 6) * cube,
        )
        if columns:
            args = list(got) + [order, swap, right_rows, left_rows, *slopes, start_s, start_t]
            if total is not None:
                args.append(total)
            outs = [state, state, full, full, full]
            outs += pair if section < 2 else [state]
            s_now, t_now, ys, yt, total, *messages = run(
                functools.partial(
                    next_kernel, s, shares[section], steps[section], total is not None, section < 2, len(got)
                ),
                outs,
                args,
                scratch=[held],
                flops=6 * cube,
            )
    change = run(
        functools.partial(last_kernel, s, shares[3]),
        [shape(s.lanes, extent, dtype=BF16)],
        [got[0], order, swap, slopes[0], total, pick_lanes],
        scratch=[held, held_b],
        flops=3 * cube,
    )[0]
    back = lax.all_to_all(
        change.reshape(s.groups, sub, extent), "aux", split_axis=0, concat_axis=0, tiled=True
    ).reshape(s.lanes, extent)
    return run(
        finish_kernel,
        [shape(planes, per_device, band, extent)],
        [back, pick_rows.T, pick_cols.T, density],
        flops=2 * cube,
    )[0]


def iotas(rows, columns):
    return (
        lax.broadcasted_iota(jnp.int32, (rows, columns), 0),
        lax.broadcasted_iota(jnp.int32, (rows, columns), 1),
    )


def mask_to(value):
    return value.astype(F32).astype(BF16)


def post_matrix(s):
    row, column = iotas(s.extent, s.extent)
    return mask_to(column == row % s.local * s.devices + row // s.local)


class Stage:
    def __init__(self, sources, buffers, targets, results, semaphores):
        self.buffers, self.results, self.targets = buffers, results, targets
        self.semaphores, self.next = semaphores, 0
        self.coming = [self.copy(a, b) for a, b in zip(sources, buffers)]
        self.going = []

    def copy(self, source, target):
        made = pltpu.make_async_copy(source, target, self.semaphores.at[self.next])
        self.next += 1
        made.start()
        return made

    def need(self, index):
        if self.coming[index] is not None:
            self.coming[index].wait()
            self.coming[index] = None
        return self.buffers[index]

    def send(self, index):
        self.going.append(self.copy(self.results[index], self.targets[index]))

    def finish(self):
        for made in self.going:
            made.wait()


def run_staged(body, outs, args, temporaries=(), scalars=(), flops=0):
    arrays, views = [], []
    for arg in args:
        array, part = arg if isinstance(arg, tuple) else (arg, None)
        if not any(array is a for a in arrays):
            arrays.append(array)
        views.append(([array is a for a in arrays].index(True), part))
    shapes, places = [], []
    for out in outs:
        if isinstance(out, tuple):
            for part in range(out[1]):
                places.append((len(shapes), part))
            shapes.append(out[0])
        else:
            places.append((len(shapes), None))
            shapes.append(out)
    tall = lambda x, part: x.shape if part is None else x.shape[:1] + x.shape[2:]
    buffers = [pltpu.VMEM(tall(arrays[k], part), arrays[k].dtype) for k, part in views]
    results = [pltpu.VMEM(tall(shapes[k], part), shapes[k].dtype) for k, part in places]
    count = len(buffers) + len(results)

    def kernel(*refs):
        small, refs = refs[: len(scalars)], refs[len(scalars) :]
        source, refs = refs[: len(arrays)], refs[len(arrays) :]
        target, refs = refs[: len(shapes)], refs[len(shapes) :]
        own, refs = refs[: len(buffers)], refs[len(buffers) :]
        made, refs = refs[: len(results)], refs[len(results) :]
        pick = lambda ref, part: ref if part is None else ref.at[:, part]
        stage = Stage(
            [pick(source[k], part) for k, part in views],
            own,
            [pick(target[k], part) for k, part in places],
            made,
            refs[-1],
        )
        body(stage, small, refs[:-1])
        stage.finish()

    moved = sum(a.size * a.dtype.itemsize for a in arrays)
    moved += sum(o.size * o.dtype.itemsize for o in shapes)
    far = pl.BlockSpec(memory_space=pltpu.HBM)
    return pl.pallas_call(
        kernel,
        out_shape=shapes,
        in_specs=[pl.BlockSpec(memory_space=pltpu.SMEM)] * len(scalars) + [far] * len(arrays),
        out_specs=[far] * len(shapes),
        scratch_shapes=buffers + results + list(temporaries) + [pltpu.SemaphoreType.DMA((count,))],
        compiler_params=pltpu.CompilerParams(vmem_limit_bytes=48 << 20),
        cost_estimate=pl.CostEstimate(flops=flops, bytes_accessed=moved, transcendentals=0),
    )(*scalars, *arrays)


def fill(s, result, first, value, lanes=slice(None)):
    count = value.shape[0] // s.local
    device = first // s.local
    result[device : device + count, :, lanes] = value.reshape(count, s.local, value.shape[1])


def flat_rows(ref, rows, lanes=slice(None)):
    piece = ref[rows, :, lanes]
    return piece.reshape(piece.shape[0] * piece.shape[1], piece.shape[2])


def even_start(s, stage, small, temporaries):
    (counts,) = small
    (post,) = temporaries
    post[...] = post_matrix(s)
    blocks = s.extent // s.band
    which = lax.axis_index("row") % s.per_device
    flats = [stage.need(v)[...].reshape(s.band, s.extent).astype(BF16) for v in range(blocks)]
    row, lane = iotas(128, s.band)
    for v in range(blocks):
        count = counts[which, v].astype(F32)
        for b in row_blocks(s.extent):
            value = dot(post[b : b + 128, :], flats[v], ((1,), (1,)))
            own = (row % s.local == 0) & (lane == (row + b) // s.local)
            value = jnp.where(own, count, value).astype(BF16)
            fill(s, stage.results[1], b, value, slice(v * s.band, (v + 1) * s.band))
    stage.send(1)
    flat = jnp.concatenate(flats, axis=0)
    for b in row_blocks(s.extent):
        fill(s, stage.results[0], b, dot(post[b : b + 128, :], flat).astype(BF16))
    stage.send(0)


def send_products(s, stage, matrix, state_ref, index):
    for b in row_blocks(s.extent):
        fill(s, stage.results[index], b, dot(matrix[b : b + 128, :], state_ref[...]).astype(BF16))
    stage.send(index)


def even_take(s, stage, small, temporaries):
    s_ref, t_ref, counts_ref = stage.results[2], stage.results[3], stage.results[4]
    me = lax.axis_index("aux") * s.rows + lax.axis_index("row")
    everyone = slice(0, s.devices)
    rows_in, row_lanes = stage.need(0), stage.need(1)
    for b in row_blocks(s.extent):
        s_ref[b : b + 128, :] = dot(
            flat_rows(rows_in, everyone, slice(b, b + 128)), row_lanes[...], ((0,), (0,))
        ).astype(BF16)
    stage.send(2)
    send_products(s, stage, stage.need(2), s_ref, 1)
    columns_in, column_lanes = stage.need(3), stage.need(4)
    blocks = s.extent // s.band
    parts = s.band // s.devices
    row, lane = iotas(s.devices, s.tile)
    mine = (row == me) & (lane < s.za)
    for q in range(s.rows):
        pieces = []
        for v in range(blocks):
            for g in range(s.groups):
                pieces.append(columns_in[g * s.rows + q, :, v * s.band : (v + 1) * s.band])
        t_ref[q * s.band : (q + 1) * s.band, :] = dot(
            jnp.concatenate(pieces, axis=0), column_lanes[...], ((0,), (0,))
        ).astype(BF16)
        rows = slice(q * s.band, q * s.band + s.devices)
        first = q * parts * s.za
        kept = s_ref[: s.devices, first : first + s.tile].astype(F32)
        t_ref[rows, : s.tile] = jnp.where(mine, kept, t_ref[rows, : s.tile].astype(F32)).astype(BF16)
    stage.send(3)
    send_products(s, stage, stage.need(5), t_ref, 0)
    row, lane = iotas(s.extent, MODES)
    gather = mask_to(row == lane * s.band + me)
    row, lane = iotas(s.auxes, s.per_device * s.groups * s.local)
    wanted = mask_to(lane == row * s.local)
    pieces = [columns_in[a // s.per_device * s.rows + a % s.per_device] for a in range(s.auxes)]
    counts_ref[...] = dot(wanted, dot(jnp.concatenate(pieces, axis=0), gather).astype(BF16))
    stage.send(4)


def even_turn(s, got_ref, order, swap, arrived):
    def load(start, size):
        return flat_rows(got_ref, slice(start // s.local, (start + size) // s.local))

    def put(rows, lanes, value):
        arrived[rows, lanes] = value

    turn(s, load, order, swap, put)


def even_next(s, weight, step, has_total, stage, small, temporaries):
    (arrived,) = temporaries
    s_ref, t_ref, ys_ref, yt_ref, total_ref = stage.results[2:7]
    got_s, order, swap = stage.need(0), stage.need(1), stage.need(2)
    even_turn(s, got_s, order, swap, arrived)
    ks_ref, ds_ref = stage.need(3), stage.need(4)
    total_in = stage.need(10) if has_total else None
    for b in row_blocks(s.extent, 64):
        rows = slice(b, b + 64)
        slope = ks_ref[rows, :] + arrived[rows, :]
        grown = weight * slope
        total_ref[rows, :] = total_in[rows, :] + grown if has_total else grown
        state = ds_ref[rows, :].astype(F32) + step * slope
        ys_ref[rows, :] = state
        s_ref[rows, :] = state.astype(BF16)
    for index in (2, 4, 6):
        stage.send(index)
    send_products(s, stage, stage.need(5), s_ref, 1)
    even_turn(s, stage.need(6), order, swap, arrived)
    kt_ref, dt_ref = stage.need(7), stage.need(8)
    for b in row_blocks(s.extent, 64):
        rows = slice(b, b + 64)
        slope = kt_ref[rows, :] - arrived[rows, :]
        state = dt_ref[rows, :].astype(F32) + step * slope
        yt_ref[rows, :] = state
        t_ref[rows, :] = state.astype(BF16)
    stage.send(3)
    stage.send(5)
    send_products(s, stage, stage.need(9), t_ref, 0)


def even_slope_part(s, direct, mirror, y_ref, h, unit, damp, q_ref, wa, wb, turned, sign, put):
    for th in range(s.tiles):
        lanes = slice(th * s.tile, (th + 1) * s.tile)
        turned[:, lanes] = dot(direct[:, lanes], unit[...]).astype(BF16)
    for b in row_blocks(s.extent):
        rows = slice(b, b + 128)
        whole = dot(h[rows, :], turned[...])
        for th in range(s.tiles):
            lanes = slice(th * s.tile, (th + 1) * s.tile)
            source = jnp.concatenate([direct[rows, lanes], mirror[rows, lanes]], axis=1)
            source = jnp.concatenate([source, source], axis=1)
            total = dot(source, wa[th]) - damp[:, lanes] * y_ref[rows, lanes].astype(F32)
            total = total + sign * whole[:, lanes]
            fields = dot(source, wb[...])
            for k in range(MODES):
                total = total + q_ref[rows, k : k + 1] * fields[:, k * s.tile : (k + 1) * s.tile]
            put(rows, lanes, total)


def even_slope(s, stage, small, temporaries):
    (turned,) = temporaries

    def put_in(index):
        def put(rows, lanes, value):
            stage.results[index][rows, lanes] = value

        return put

    need = stage.need
    unit, damp, q_ref = need(4), need(5), need(6)
    even_slope_part(
        s, need(0), need(1), need(2), need(7), unit, damp, q_ref, need(8), need(9), turned, -1.0, put_in(0)
    )
    stage.send(0)
    even_slope_part(
        s, need(1), need(0), need(3), need(10), unit, damp, q_ref, need(11), need(12), turned, 1.0, put_in(1)
    )
    stage.send(1)


def even_last(s, step, weight_three, weight_four, stage, small, temporaries):
    arrived, s_ref, t_ref, grown, turned, base = temporaries
    need = stage.need
    order, swap = need(1), need(2)
    even_turn(s, need(0), order, swap, arrived)
    kt_ref, dt_ref = need(3), need(4)
    for b in row_blocks(s.extent, 64):
        rows = slice(b, b + 64)
        slope = kt_ref[rows, :] - arrived[rows, :]
        t_ref[rows, :] = (dt_ref[rows, :].astype(F32) + step * slope).astype(BF16)
    unit, left, column_lanes = need(5), need(6), need(7)
    for th in range(s.tiles):
        lanes = slice(th * s.tile, (th + 1) * s.tile)
        turned[:, lanes] = dot(t_ref[:, lanes], unit[...]).astype(BF16)
    for b in row_blocks(s.extent):
        rows = slice(b, b + 128)
        grown[rows, :] = (weight_four * dot(left[rows, :], turned[...])).astype(BF16)
    out = stage.results[1]
    for q in range(s.rows):
        value = dot(column_lanes[...], grown[q * s.band : (q + 1) * s.band, :], ((1,), (1,))).astype(BF16)
        for v in range(s.extent // s.band):
            for g in range(s.groups):
                at = (v * s.groups + g) * s.local
                out[g * s.rows + q, :, v * s.band : (v + 1) * s.band] = value[at : at + s.local, :]
    stage.send(1)
    even_turn(s, need(8), order, swap, arrived)
    ks_ref, ds_ref, total_in = need(9), need(10), need(11)
    for b in row_blocks(s.extent, 64):
        rows = slice(b, b + 64)
        slope = ks_ref[rows, :] + arrived[rows, :]
        base[rows, :] = total_in[rows, :] + weight_three * slope
        state = ds_ref[rows, :].astype(F32) + step * slope
        arrived[rows, :] = state
        s_ref[rows, :] = state.astype(BF16)

    def put(rows, lanes, value):
        grown[rows, lanes] = (base[rows, lanes] + weight_four * value).astype(BF16)

    even_slope_part(
        s, s_ref, t_ref, arrived, need(14), unit, need(12), need(13), need(15), need(16), turned, -1.0, put
    )
    row_lanes = need(17)
    for b in row_blocks(s.extent):
        fill(s, stage.results[0], b, dot(row_lanes[b : b + 128, :], grown[...], ((1,), (1,))).astype(BF16))
    stage.send(0)


def even_finish(s, stage, small, temporaries):
    (post,) = temporaries
    post[...] = post_matrix(s)
    everyone = slice(0, s.devices)
    rows_in, columns_in = stage.need(0), stage.need(1)
    for v in range(s.extent // s.band):
        lanes = slice(v * s.band, (v + 1) * s.band)
        change = dot(post[:, lanes], flat_rows(rows_in, everyone), ((0,), (0,)))
        change = change + dot(flat_rows(columns_in, everyone, lanes), post[...], ((0,), (0,)))
        stage.results[v][...] = (stage.need(2 + v)[...].reshape(s.band, s.extent) + change).reshape(
            stage.results[v].shape
        )
        stage.send(v)


def hamiltonian_kernel(s, own_ref, outer_ref, where_ref, left, right, left_rows, right_rows, post):
    blocks, block = own_ref.shape[0], own_ref.shape[1]
    post[...] = post_matrix(s)
    row, column = iotas(block, s.extent)
    for b in range(blocks):
        spread = column - row
        to_own = mask_to(spread == b * block)
        to_far = mask_to(spread == where_ref[b] * block)
        left[b * block : (b + 1) * block, :] = (dot(own_ref[b], to_own) + dot(outer_ref[b], to_far)).astype(BF16)
    row, column = iotas(s.extent, s.extent)
    same = mask_to(row == column)
    for b in row_blocks(s.extent):
        rows = slice(b, b + 128)
        right[rows, :] = dot(same[rows, :], left[...], ((1,), (1,))).astype(BF16)
        left_rows[rows, :] = dot(post[rows, :], left[...]).astype(BF16)
        right_rows[rows, :] = dot(post[rows, :], left[...], ((1,), (1,))).astype(BF16)


def weights_kernel(
    s, real_ref, imag_ref, rate_ref, counts_ref, index_ref, mirror_ref, couplings_ref, wa_s, wb_s, wa_t, wb_t, damp
):
    me = lax.axis_index("aux") * s.rows + lax.axis_index("row")
    depth, wide = 2 * s.tile, MODES * s.tile
    row, column = iotas(s.auxes, wide)
    by_lane = mask_to(column % s.auxes == row)

    def spread(table):
        return dot(table.astype(F32).astype(BF16), by_lane, ((0,), (0,)))

    counts = spread(counts_ref[...])
    index, mirror = spread(index_ref[...]), spread(mirror_ref[...])
    lane_mode = lax.broadcasted_iota(jnp.int32, (1, wide), 1) // s.tile

    def of_mode(values):
        out = values[0]
        for k in range(1, MODES):
            out = jnp.where(lane_mode == k, values[k], out)
        return out

    take = lambda table, first: of_mode([table[first + k : first + k + 1, :] for k in range(MODES)])
    ups, downs = take(index, 0), take(index, MODES)
    up_kinds, down_kinds = take(mirror, 0), take(mirror, MODES)
    real = of_mode([counts[k : k + 1, :] * real_ref[k] for k in range(MODES)])
    imag = of_mode([counts[k : k + 1, :] * imag_ref[k] for k in range(MODES)])
    rates = counts[0:1, :] * rate_ref[0]
    for k in range(1, MODES):
        rates = rates + counts[k : k + 1, :] * rate_ref[k]
    damp[...] = rates

    row, column = iotas(s.extent, s.lanes)
    pick = (row % s.devices == me) & (row // s.devices == column // s.za)
    local_q = lax.dot_general(
        couplings_ref[...],
        pick.astype(F32),
        (((1,), (0,)), ((), ())),
        precision=lax.Precision.HIGHEST,
        preferred_element_type=F32,
    )

    row, column = iotas(depth, wide)
    same = row // s.za % s.fold == column // s.za % s.fold
    source, kind = (row % s.auxes).astype(F32), (row // s.tile).astype(F32)
    from_imag, to_imag = row // s.auxes % 2, column // s.auxes % 2
    up = same & (ups == source) & (up_kinds == kind)
    down = same & (downs == source) & (down_kinds == kind)
    along = jnp.where(up, 1.0, 0.0) + jnp.where(down, real, 0.0)
    cross = jnp.where(down, imag, 0.0)
    along = jnp.where(from_imag == 1, along, -along)
    flip = jnp.where((from_imag == 1) & (row // s.tile == 1), -1.0, 1.0)
    by_row = flip * jnp.where(from_imag == to_imag, cross, along)
    by_column = flip * jnp.where(from_imag == to_imag, cross, -along)

    def pieces(value):
        high = value.astype(BF16)
        return high, (value - high.astype(F32)).astype(BF16)

    for near, far, wa, wb in ((by_row, by_column, wa_s, wb_s), (by_column, by_row, wa_t, wb_t)):
        wb[:depth, :], wb[depth:, :] = pieces(far)
        for th in range(s.tiles):
            lanes = slice(th * s.tile, (th + 1) * s.tile)
            total = local_q[0:1, lanes] * near[:, : s.tile]
            for k in range(1, MODES):
                total = total + local_q[k : k + 1, lanes] * near[:, k * s.tile : (k + 1) * s.tile]
            wa[th, :depth, :], wa[th, depth:, :] = pieces(total)


def even_body(
    s,
    density,
    couplings,
    weight_real,
    weight_imag,
    mode_rates,
    tier_counts,
    link_index,
    link_mirror,
    block_diagonal,
    block_outer,
    block_column,
):
    planes, per_device, band, extent = density.shape
    cube = 2 * extent * extent * s.lanes
    state = shape(extent, s.lanes, dtype=BF16)
    full = shape(extent, s.lanes)
    pair = (shape(s.devices, 2, s.local, s.lanes, dtype=BF16), 2)
    held = pltpu.VMEM((extent, s.lanes), F32)
    held_b = pltpu.VMEM((extent, s.lanes), BF16)

    def exchange(message):
        return lax.all_to_all(message, BOTH, split_axis=0, concat_axis=0, tiled=True)

    blocks = density.reshape(1, planes * per_device, band, extent)
    message = run_staged(
        functools.partial(even_start, s),
        [pair],
        [(blocks, v) for v in range(planes * per_device)],
        temporaries=[held_b],
        scalars=[tier_counts],
        flops=2 * cube,
    )[0]
    got = exchange(message)

    left, right, left_rows, right_rows = run(
        functools.partial(hamiltonian_kernel, s),
        [state] * 4,
        [block_diagonal, block_outer, block_column],
        scratch=[held_b],
        flops=4 * cube,
        scalars=(2,),
    )
    q_first = couplings.T

    k, n = iotas(s.lanes, s.lanes)
    parts = band // s.devices
    row_lanes = (
        n
        == (k // s.local % s.rows * parts + k % parts) * s.za
        + k // (parts * per_device) % planes * s.auxes
        + k // (s.local * s.rows) * per_device
        + k // parts % per_device
    ).astype(BF16)
    column_lanes = (
        n
        == k % s.local * s.za
        + k // (s.local * s.groups * per_device) * s.auxes
        + k // s.local % s.groups * per_device
        + k // (s.local * s.groups) % per_device
    ).astype(BF16)

    k, n = iotas(s.tile, s.tile)
    sign = jnp.where(n // s.auxes % 2 == 0, 1.0, -1.0)
    unit = jnp.where(k // s.za * s.za + (k + s.auxes) % s.za == n, sign, 0.0).astype(BF16)
    k, n = iotas(s.fold * s.tile, s.fold * s.tile)
    sign = jnp.where(n // s.auxes % 2 == 0, 1.0, -1.0)
    there = (k // s.za % s.fold * s.fold + k // s.tile) * s.za + (k + s.auxes) % s.za
    swap = jnp.where(there == n, sign, 0.0).astype(BF16)
    size = max(256, 16 * s.local)
    span = size // s.local
    k, n = iotas(size, size)
    order = (n == k % span * s.local + k // span).astype(BF16)

    message, s_now, t_now, counts = run_staged(
        functools.partial(even_take, s),
        [pair, state, state, shape(s.auxes, MODES)],
        [(got, 0), row_lanes, right_rows, (got, 1), column_lanes, left_rows],
        flops=4 * cube,
    )
    wa = shape(s.tiles, 4 * s.tile, s.tile, dtype=BF16)
    wb = shape(4 * s.tile, MODES * s.tile, dtype=BF16)
    wa_s, wb_s, wa_t, wb_t, damp = run(
        functools.partial(weights_kernel, s),
        [wa, wb, wa, wb, shape(1, s.lanes)],
        [weight_real, weight_imag, mode_rates, counts, link_index, link_mirror, couplings],
        scalars=(0, 1, 2),
        flops=cube,
    )
    start_s, start_t = s_now, t_now
    ys, yt = s_now, t_now
    total = None
    shares = [STEP / 6.0, STEP / 3.0, STEP / 3.0, STEP / 6.0]
    steps = [0.25, 0.25, 0.5]
    for section in range(3):
        got = exchange(message)
        ks, kt = run_staged(
            functools.partial(even_slope, s),
            [full, full],
            [s_now, t_now, ys, yt, unit, damp, q_first, right, wa_s, wb_s, left, wa_t, wb_t],
            temporaries=[held_b],
            flops=12 * cube,
        )
        if section < 2:
            args = [(got, 0), order, swap, ks, start_s, right_rows, (got, 1), kt, start_t, left_rows]
            if total is not None:
                args.append(total)
            message, s_now, t_now, ys, yt, total = run_staged(
                functools.partial(even_next, s, shares[section], steps[section], total is not None),
                [pair, state, state, full, full, full],
                args,
                temporaries=[held],
                flops=6 * cube,
            )
    message = run_staged(
        functools.partial(even_last, s, steps[2], shares[2], shares[3]),
        [pair],
        [(got, 1), order, swap, kt, start_t, unit, left, column_lanes, (got, 0), ks, start_s, total]
        + [damp, q_first, right, wa_s, wb_s, row_lanes],
        temporaries=[held, held_b, held_b, held_b, held_b, held],
        flops=12 * cube,
    )[0]
    got = exchange(message)
    evolved = run_staged(
        functools.partial(even_finish, s),
        [(shape(1, planes * per_device, band, extent), planes * per_device)],
        [(got, 0), (got, 1)] + [(blocks, v) for v in range(planes * per_device)],
        temporaries=[held_b],
        flops=2 * cube,
    )[0]
    return evolved.reshape(density.shape)


def body(density, *others):
    planes, per_device, band, extent = density.shape
    s = Sizes(lax.axis_size("aux"), lax.axis_size("row"), per_device, band, extent)
    even = band % s.devices == 0 and s.local % 16 == 0 and LANES % s.za == 0
    even = even and s.lanes == extent and planes * per_device * band == extent
    even = even and planes * per_device == MODES and per_device <= s.rows and s.devices <= s.band
    if even:
        return even_body(s, density, *others)
    return general_body(density, *others)


def solution(mesh):
    return jax.shard_map(
        body,
        mesh=mesh,
        in_specs=(
            P(None, "aux", "row", None),
            P(),
            P(),
            P(),
            P(),
            P("aux", None),
            P(),
            P(),
            P(),
            P(),
            P(),
        ),
        out_specs=P(None, "aux", "row", None),
        check_vma=False,
    )
```

```python
import functools

import jax
import jax.numpy as jnp
from jax import lax
from jax.experimental import pallas as pl
from jax.experimental.pallas import tpu as pltpu
from jax.sharding import PartitionSpec as P

MODES = 4
LINKS = 8
LANES = 128
STEP = 0.5
BOTH = ("aux", "row")
GRANT = 59 * (1 << 20) + (384 << 10)

F32 = jnp.float32
BF16 = jnp.bfloat16


class Sizes:
    def __init__(self, groups, rows, per_device, band, extent):
        self.groups, self.rows, self.per_device = groups, rows, per_device
        self.band, self.extent = band, extent
        self.devices = groups * rows
        self.local = band // groups
        self.auxes = per_device * groups
        self.za = 2 * self.auxes
        self.lanes = self.local * self.za
        self.fold = max(1, LANES // self.za)
        self.tile = self.fold * self.za
        self.tiles = self.local // self.fold
        self.joined = self.local % 16 == 0


def dot(a, b, dims=((1,), (0,))):
    return lax.dot_general(a, b, (dims, ((), ())), preferred_element_type=F32)


def run(kernel, outs, args, scratch=(), flops=0, scalars=()):
    spec = pl.BlockSpec(memory_space=pltpu.VMEM)
    flat = pl.BlockSpec(memory_space=pltpu.SMEM)
    moved = sum(a.size * a.dtype.itemsize for a in args)
    moved += sum(o.size * o.dtype.itemsize for o in outs)
    return pl.pallas_call(
        kernel,
        out_shape=list(outs),
        in_specs=[flat if n in scalars else spec for n in range(len(args))],
        out_specs=[spec] * len(outs),
        scratch_shapes=list(scratch),
        compiler_params=pltpu.CompilerParams(vmem_limit_bytes=16 << 20),
        cost_estimate=pl.CostEstimate(flops=flops, bytes_accessed=moved, transcendentals=0),
    )(*args)


def shape(*dims, dtype=F32):
    return jax.ShapeDtypeStruct(dims, dtype)


def one_hot(target, count):
    return (target[:, None] == jnp.arange(count, dtype=jnp.int32)[None, :]).astype(BF16)


def matrix_index(s, index, device):
    group, row = device // s.rows, device % s.rows
    return row * s.band + index * s.groups + group


def row_blocks(extent, size=128):
    return range(0, extent, size)


def send_start_kernel(d_ref, pick_rows, pick_cols, out_ref):
    planes, number, band, extent = d_ref.shape
    flat = d_ref[...].reshape(planes * number * band, extent).astype(BF16)
    for b in row_blocks(flat.shape[0]):
        moved = dot(pick_rows[b : b + 128, :], flat).astype(BF16)
        out_ref[b : b + 128, :] = dot(moved, pick_cols[...]).astype(BF16)


def take_start_kernel(got_ref, pick_lanes, message_rows, s_ref, m_ref):
    for b in row_blocks(got_ref.shape[1]):
        s_ref[b : b + 128, :] = dot(
            got_ref[:, b : b + 128], pick_lanes[...], ((0,), (0,))
        ).astype(BF16)
    for b in row_blocks(m_ref.shape[0]):
        m_ref[b : b + 128, :] = dot(message_rows[b : b + 128, :], s_ref[...]).astype(BF16)


def turn(s, load, order, swap, put):
    size = order.shape[0]
    span = size // s.local
    for block in range(s.extent // size):
        moved = dot(order[...], load(block * size, size))
        parts = []
        for ih in range(s.tiles):
            for jh in range(s.tiles):
                lanes = slice(jh * s.tile, (jh + 1) * s.tile)
                pieces = [
                    moved[(ih * s.fold + f) * span : (ih * s.fold + f + 1) * span, lanes]
                    for f in range(s.fold)
                ]
                parts.append(jnp.concatenate(pieces, axis=1) if s.fold > 1 else pieces[0])
        turned = dot(jnp.concatenate(parts, axis=0).astype(BF16), swap[...])
        for ih in range(s.tiles):
            for jh in range(s.tiles):
                start = (ih * s.tiles + jh) * span
                for f in range(s.fold):
                    first = (jh * s.fold + f) * s.devices + block * span
                    put(
                        slice(first, first + span),
                        slice(ih * s.tile, (ih + 1) * s.tile),
                        turned[start : start + span, f * s.tile : (f + 1) * s.tile],
                    )


def take_columns_kernel(s, got_ref, order, swap, first_rows, left_rows, s_ref, t_ref, *message):
    def put(rows, lanes, value):
        t_ref[rows, lanes] = value.astype(BF16)

    turn(s, lambda start, size: got_ref[start : start + size, :], order, swap, put)
    write_messages(s, first_rows, left_rows, s_ref, t_ref, message)


def write_messages(s, right_rows, left_rows, s_ref, t_ref, message):
    pairs = ((left_rows, t_ref), (right_rows, s_ref))
    if not s.joined and len(message) == 1:
        pairs = pairs[:1]
    both = s.joined and message[0].shape[0] == 2 * s.extent
    for part, (matrix, state) in enumerate(pairs):
        if s.joined and part == 1 and not both:
            continue
        for b in row_blocks(s.extent):
            product = dot(matrix[b : b + 128, :], state[...]).astype(BF16)
            if not s.joined:
                message[part][b : b + 128, :] = product
            elif not both:
                message[0][b : b + 128, :] = product
            else:
                for k in range(128 // s.local):
                    start = ((b // s.local + k) * 2 + part) * s.local
                    message[0][start : start + s.local, :] = product[
                        k * s.local : (k + 1) * s.local, :
                    ]


def slope_kernel(
    s, with_columns, s_ref, t_ref, ys_ref, yt_ref, damp, q_ref, right, left, unit, wa_s, wb_s, wa_t, wb_t, *rest
):
    if with_columns:
        ks_ref, kt_ref, turned = rest
    else:
        ks_ref, turned = rest

    def one(direct, mirror, y_ref, h, wa, wb, out_ref, sign):
        for th in range(s.tiles):
            lanes = slice(th * s.tile, (th + 1) * s.tile)
            turned[:, lanes] = dot(direct[:, lanes], unit[...]).astype(BF16)
        for b in row_blocks(s.extent):
            rows = slice(b, b + 128)
            whole = dot(h[rows, :], turned[...])
            for th in range(s.tiles):
                lanes = slice(th * s.tile, (th + 1) * s.tile)
                source = jnp.concatenate([direct[rows, lanes], mirror[rows, lanes]], axis=1)
                source = jnp.concatenate([source, source], axis=1)
                total = dot(source, wa[th]) - damp[:, lanes] * y_ref[rows, lanes].astype(F32)
                total = total + sign * whole[:, lanes]
                fields = dot(source, wb[...])
                for k in range(MODES):
                    total = total + q_ref[rows, k : k + 1] * fields[:, k * s.tile : (k + 1) * s.tile]
                out_ref[rows, lanes] = total

    one(s_ref, t_ref, ys_ref, right, wa_s, wb_s, ks_ref, -1.0)
    if with_columns:
        one(t_ref, s_ref, yt_ref, left, wa_t, wb_t, kt_ref, 1.0)


def part_loader(s, refs, part):
    def load(start, size):
        if not s.joined:
            return refs[part][start : start + size, :]
        step = s.local
        pieces = []
        for first in range(start, start + size, step):
            at = (first // step * 2 + part) * step
            pieces.append(refs[0][at : at + step, :])
        return jnp.concatenate(pieces, axis=0)

    return load


def next_kernel(s, weight, step, has_total, both, got_count, *refs):
    got = refs[:got_count]
    refs = refs[got_count:]
    order, swap, right_rows, left_rows, ks_ref, kt_ref, ds_ref, dt_ref = refs[:8]
    refs = refs[8:]
    total_in = None
    if has_total:
        total_in, refs = refs[0], refs[1:]
    s_ref, t_ref, ys_ref, yt_ref, total_ref = refs[:5]
    message, arrived = refs[5:-1], refs[-1]

    def put(rows, lanes, value):
        arrived[rows, lanes] = value

    for part in range(2):
        turn(s, part_loader(s, got, part), order, swap, put)
        for b in row_blocks(s.extent, 64):
            rows = slice(b, b + 64)
            if part == 0:
                slope = ks_ref[rows, :] + arrived[rows, :]
                grown = weight * slope
                total_ref[rows, :] = total_in[rows, :] + grown if has_total else grown
                state = ds_ref[rows, :].astype(F32) + step * slope
                ys_ref[rows, :] = state
                s_ref[rows, :] = state.astype(BF16)
            else:
                slope = kt_ref[rows, :] - arrived[rows, :]
                state = dt_ref[rows, :].astype(F32) + step * slope
                yt_ref[rows, :] = state
                t_ref[rows, :] = state.astype(BF16)
    if message:
        write_messages(s, right_rows, left_rows, s_ref, t_ref, message)


def last_kernel(s, weight, got_ref, order, swap, ks_ref, total_in, pick_lanes, out_ref, arrived, grown):
    def put(rows, lanes, value):
        arrived[rows, lanes] = value

    turn(s, lambda start, size: got_ref[start : start + size, :], order, swap, put)
    for b in row_blocks(s.extent, 64):
        rows = slice(b, b + 64)
        change = total_in[rows, :] + weight * (ks_ref[rows, :] + arrived[rows, :])
        grown[rows, :] = change.astype(BF16)
    for b in row_blocks(s.lanes):
        out_ref[b : b + 128, :] = dot(
            pick_lanes[b : b + 128, :], grown[...], ((1,), (1,))
        ).astype(BF16)


def finish_kernel(got_ref, place_rows, place_cols, d_ref, out_ref):
    planes, number, band, extent = d_ref.shape
    for z in range(planes):
        for n in range(number):
            at = (z * number + n) * band
            for b in range(0, band, min(band, 128)):
                size = min(band, 128)
                rows = slice(at + b, at + b + size)
                moved = dot(place_rows[rows, :], got_ref[...]).astype(BF16)
                out_ref[z, n, b : b + size, :] = d_ref[z, n, b : b + size, :] + dot(
                    moved, place_cols[...]
                )


def link_matrices(s, counts, weight_real, weight_imag, link_index, link_mirror):
    ones = jnp.ones_like(counts)
    real = jnp.stack([ones, counts * weight_real[None, :]], 1)
    imag = jnp.stack([jnp.zeros_like(counts), counts * weight_imag[None, :]], 1)
    index = link_index.reshape(s.auxes, 2, MODES)
    mirror = link_mirror.reshape(s.auxes, 2, MODES)
    source = jnp.arange(s.auxes, dtype=jnp.int32)
    hit = index[None] == source[:, None, None, None]
    kinds = jnp.stack([hit & (mirror[None] == 0), hit & (mirror[None] == 1)]).astype(F32)
    along = jnp.sum(kinds * real, 3)
    cross = jnp.sum(kinds * imag, 3)
    along, cross = (jnp.transpose(m, (0, 3, 1, 2)) for m in (along, cross))
    flip = jnp.array([1.0, -1.0], F32).reshape(2, 1, 1, 1)

    def build(sign):
        upper = jnp.concatenate([cross, -sign * along], 3)
        lower = jnp.concatenate([sign * along, cross], 3) * flip
        return jnp.concatenate([upper, lower], 2)

    return build(1.0), build(-1.0)


def two_pieces(weights, axis):
    high = lax.reduce_precision(weights, 8, 7)
    low = weights - high
    return jnp.concatenate([high.astype(BF16), low.astype(BF16)], axis)


def coupling_weights(s, by_local, by_first, local_q):
    eye = jnp.eye(s.fold, dtype=F32)
    near = jnp.einsum("ki,xkuv->ixuv", local_q, by_local, precision=lax.Precision.HIGHEST)
    near = near.reshape(s.tiles, s.fold, 2, s.za, s.za)
    near = jnp.transpose(near, (0, 2, 1, 3, 4))[:, :, :, :, None, :] * eye[None, None, :, None, :, None]
    near = near.reshape(s.tiles, 2 * s.tile, s.tile)
    far = jnp.transpose(by_first, (0, 2, 1, 3))[:, None, :, :, None, :] * eye[None, :, None, None, :, None]
    far = far.reshape(2 * s.tile, MODES * s.tile)
    return two_pieces(near, 1), two_pieces(far, 0)


def general_body(
    density,
    couplings,
    weight_real,
    weight_imag,
    mode_rates,
    tier_counts,
    link_index,
    link_mirror,
    block_diagonal,
    block_outer,
    block_column,
):
    planes, per_device, band, extent = density.shape
    s = Sizes(lax.axis_size("aux"), lax.axis_size("row"), per_device, band, extent)
    blocks, block = block_diagonal.shape[0], block_diagonal.shape[1]
    group, row = lax.axis_index("aux"), lax.axis_index("row")
    device = group * s.rows + row
    cube = 2 * extent * extent * s.lanes

    number = jnp.arange(extent, dtype=jnp.int32)
    first_to_matrix = matrix_index(s, number // s.devices, number % s.devices)
    posted_to_matrix = matrix_index(s, number % s.local, number // s.local)
    posted_to_first = number % s.local * s.devices + number // s.local

    wide = jnp.arange(s.lanes, dtype=jnp.int32)
    sub = planes * per_device * s.local
    start_source = wide % sub * s.groups + wide // sub
    pick_rows = one_hot(start_source, s.lanes)
    pick_cols = one_hot(first_to_matrix, extent).T
    lane_of = (
        wide % s.local * s.za
        + wide // (per_device * s.local) % planes * s.auxes
        + wide // sub * per_device
        + wide // s.local % per_device
    )
    pick_lanes = one_hot(lane_of, s.lanes)
    message_rows = one_hot(posted_to_first, extent)
    start_message = run(
        send_start_kernel,
        [shape(s.lanes, extent, dtype=BF16)],
        [density, pick_rows, pick_cols],
        flops=2 * cube,
    )[0]
    start_got = lax.all_to_all(
        start_message.reshape(s.groups, sub, extent), "aux", split_axis=0, concat_axis=0, tiled=True
    ).reshape(s.lanes, extent)

    selector = block_column[:, None] == jnp.arange(blocks, dtype=jnp.int32)[None, :]
    own = jnp.eye(blocks, dtype=F32)
    whole_h = (
        own[:, None, :, None] * block_diagonal.astype(F32)[:, :, None, :]
        + selector.astype(F32)[:, None, :, None] * block_outer.astype(F32)[:, :, None, :]
    ).reshape(extent, extent).astype(BF16)
    first_h = one_hot(first_to_matrix, extent)
    left = jnp.dot(
        jnp.dot(first_h, whole_h, preferred_element_type=BF16), first_h.T, preferred_element_type=BF16
    )
    right = left.T
    left_rows = jnp.dot(message_rows, left, preferred_element_type=BF16)
    right_rows = jnp.dot(message_rows, right, preferred_element_type=BF16)

    counts = lax.all_gather(tier_counts, "aux", axis=0, tiled=True).astype(F32)
    damping = jnp.sum(counts * mode_rates[None, :], axis=1)
    damp = jnp.tile(damping, (planes * s.local,))[None, :]
    q_first = jnp.dot(
        couplings, first_h.T.astype(F32), precision=lax.Precision.HIGHEST
    ).T
    local_pick = (matrix_index(s, jnp.arange(s.local, dtype=jnp.int32), device)[None, :] == number[:, None])
    local_q = jnp.dot(couplings, local_pick.astype(F32), precision=lax.Precision.HIGHEST)
    by_row, by_column = link_matrices(s, counts, weight_real, weight_imag, link_index, link_mirror)
    wa_s, wb_s = coupling_weights(s, by_row, by_column, local_q)
    wa_t, wb_t = coupling_weights(s, by_column, by_row, local_q)

    lane = jnp.arange(s.za, dtype=jnp.int32)
    unit = jnp.where(
        lane[:, None] == (lane[None, :] + s.auxes) % s.za,
        jnp.where(lane[None, :] < s.auxes, 1.0, -1.0),
        0.0,
    )
    eye_fold = jnp.eye(s.fold, dtype=F32)
    unit_tile = (eye_fold[:, None, :, None] * unit[None, :, None, :]).reshape(s.tile, s.tile).astype(BF16)
    swap = (
        eye_fold[:, None, None, None, :, None]
        * eye_fold[None, :, None, :, None, None]
        * unit[None, None, :, None, None, :]
    ).reshape(s.fold * s.tile, s.fold * s.tile).astype(BF16)
    keep = (
        eye_fold[:, None, None, None, :, None]
        * eye_fold[None, :, None, :, None, None]
        * jnp.eye(s.za, dtype=F32)[None, None, :, None, None, :]
    ).reshape(s.fold * s.tile, s.fold * s.tile).astype(BF16)
    size = min(extent, max(256, 16 * s.local))
    span = size // s.local
    at = jnp.arange(size, dtype=jnp.int32)
    order = one_hot(at % span * s.local + at // span, size)

    state = shape(extent, s.lanes, dtype=BF16)
    full = shape(extent, s.lanes)
    held = pltpu.VMEM((extent, s.lanes), F32)
    held_b = pltpu.VMEM((extent, s.lanes), BF16)

    def exchange(messages):
        parts = [m.reshape(s.devices, -1, s.lanes) for m in messages]
        sent = parts[0] if len(parts) == 1 else jnp.concatenate(parts, 1)
        got = lax.all_to_all(sent, BOTH, split_axis=0, concat_axis=0, tiled=True)
        if len(parts) == 1:
            return [got.reshape(-1, s.lanes)]
        height = s.local
        return [got[:, p * height : (p + 1) * height].reshape(-1, s.lanes) for p in range(2)]

    if s.joined:
        pair = [shape(2 * extent, s.lanes, dtype=BF16)]
    else:
        pair = [state, state]

    s_now, posted = run(
        take_start_kernel, [state, state], [start_got, pick_lanes, message_rows], flops=2 * cube
    )
    got = exchange([posted])
    t_now, *messages = run(
        functools.partial(take_columns_kernel, s),
        [state] + pair,
        [got[0], order, keep, right_rows, left_rows, s_now],
        flops=4 * cube,
    )
    start_s, start_t = s_now, t_now
    ys, yt = s_now, t_now
    total = None
    shares = [STEP / 6.0, STEP / 3.0, STEP / 3.0, STEP / 6.0]
    steps = [0.25, 0.25, 0.5]
    for section in range(4):
        got = exchange(messages)
        columns = section < 3
        slopes = run(
            functools.partial(slope_kernel, s, columns),
            [full, full] if columns else [full],
            [s_now, t_now, ys, yt, damp, q_first, right, left, unit_tile, wa_s, wb_s, wa_t, wb_t],
            scratch=[held_b],
            flops=(12 if columns else 6) * cube,
        )
        if columns:
            args = list(got) + [order, swap, right_rows, left_rows, *slopes, start_s, start_t]
            if total is not None:
                args.append(total)
            outs = [state, state, full, full, full]
            outs += pair if section < 2 else [state]
            s_now, t_now, ys, yt, total, *messages = run(
                functools.partial(
                    next_kernel, s, shares[section], steps[section], total is not None, section < 2, len(got)
                ),
                outs,
                args,
                scratch=[held],
                flops=6 * cube,
            )
    change = run(
        functools.partial(last_kernel, s, shares[3]),
        [shape(s.lanes, extent, dtype=BF16)],
        [got[0], order, swap, slopes[0], total, pick_lanes],
        scratch=[held, held_b],
        flops=3 * cube,
    )[0]
    back = lax.all_to_all(
        change.reshape(s.groups, sub, extent), "aux", split_axis=0, concat_axis=0, tiled=True
    ).reshape(s.lanes, extent)
    return run(
        finish_kernel,
        [shape(planes, per_device, band, extent)],
        [back, pick_rows.T, pick_cols.T, density],
        flops=2 * cube,
    )[0]


def iotas(rows, columns):
    return (
        lax.broadcasted_iota(jnp.int32, (rows, columns), 0),
        lax.broadcasted_iota(jnp.int32, (rows, columns), 1),
    )


def mask_to(value):
    return value.astype(F32).astype(BF16)


def post_matrix(s):
    row, column = iotas(s.extent, s.extent)
    return mask_to(column == row % s.local * s.devices + row // s.local)


class Stage:
    def __init__(self, sources, buffers, targets, results, semaphores):
        self.buffers, self.results, self.targets = buffers, results, targets
        self.semaphores, self.next = semaphores, 0
        self.coming = [self.copy(a, b) for a, b in zip(sources, buffers)]
        self.going = []

    def copy(self, source, target):
        made = pltpu.make_async_copy(source, target, self.semaphores.at[self.next])
        self.next += 1
        made.start()
        return made

    def need(self, index):
        if self.coming[index] is not None:
            self.coming[index].wait()
            self.coming[index] = None
        return self.buffers[index]

    def send(self, index):
        self.going.append(self.copy(self.results[index], self.targets[index]))

    def finish(self):
        for made in self.going:
            made.wait()


def run_staged(body, outs, args, temporaries=(), scalars=(), flops=0):
    arrays, views = [], []
    for arg in args:
        array, part = arg if isinstance(arg, tuple) else (arg, None)
        if not any(array is a for a in arrays):
            arrays.append(array)
        views.append(([array is a for a in arrays].index(True), part))
    shapes, places = [], []
    for out in outs:
        if isinstance(out, tuple):
            for part in range(out[1]):
                places.append((len(shapes), part))
            shapes.append(out[0])
        else:
            places.append((len(shapes), None))
            shapes.append(out)
    tall = lambda x, part: x.shape if part is None else x.shape[:1] + x.shape[2:]
    buffers = [pltpu.VMEM(tall(arrays[k], part), arrays[k].dtype) for k, part in views]
    results = [pltpu.VMEM(tall(shapes[k], part), shapes[k].dtype) for k, part in places]
    count = len(buffers) + len(results)

    def kernel(*refs):
        small, refs = refs[: len(scalars)], refs[len(scalars) :]
        source, refs = refs[: len(arrays)], refs[len(arrays) :]
        target, refs = refs[: len(shapes)], refs[len(shapes) :]
        own, refs = refs[: len(buffers)], refs[len(buffers) :]
        made, refs = refs[: len(results)], refs[len(results) :]
        pick = lambda ref, part: ref if part is None else ref.at[:, part]
        stage = Stage(
            [pick(source[k], part) for k, part in views],
            own,
            [pick(target[k], part) for k, part in places],
            made,
            refs[-1],
        )
        body(stage, small, refs[:-1])
        stage.finish()

    moved = sum(a.size * a.dtype.itemsize for a in arrays)
    moved += sum(o.size * o.dtype.itemsize for o in shapes)
    far = pl.BlockSpec(memory_space=pltpu.HBM)
    return pl.pallas_call(
        kernel,
        out_shape=shapes,
        in_specs=[pl.BlockSpec(memory_space=pltpu.SMEM)] * len(scalars) + [far] * len(arrays),
        out_specs=[far] * len(shapes),
        scratch_shapes=buffers + results + list(temporaries) + [pltpu.SemaphoreType.DMA((count,))],
        compiler_params=pltpu.CompilerParams(vmem_limit_bytes=GRANT),
        cost_estimate=pl.CostEstimate(flops=flops, bytes_accessed=moved, transcendentals=0),
    )(*scalars, *arrays)


def fill(s, result, first, value, lanes=slice(None)):
    count = value.shape[0] // s.local
    device = first // s.local
    result[device : device + count, :, lanes] = value.reshape(count, s.local, value.shape[1])


def flat_rows(ref, rows, lanes=slice(None)):
    piece = ref[rows, :, lanes]
    return piece.reshape(piece.shape[0] * piece.shape[1], piece.shape[2])


def even_start(s, stage, small, temporaries):
    (counts,) = small
    (post,) = temporaries
    post[...] = post_matrix(s)
    blocks = s.extent // s.band
    which = lax.axis_index("row") % s.per_device
    flats = [stage.need(v)[...].reshape(s.band, s.extent).astype(BF16) for v in range(blocks)]
    row, lane = iotas(128, s.band)
    for v in range(blocks):
        count = counts[which, v].astype(F32)
        for b in row_blocks(s.extent):
            value = dot(post[b : b + 128, :], flats[v], ((1,), (1,)))
            own = (row % s.local == 0) & (lane == (row + b) // s.local)
            value = jnp.where(own, count, value).astype(BF16)
            fill(s, stage.results[1], b, value, slice(v * s.band, (v + 1) * s.band))
    stage.send(1)
    flat = jnp.concatenate(flats, axis=0)
    for b in row_blocks(s.extent):
        fill(s, stage.results[0], b, dot(post[b : b + 128, :], flat).astype(BF16))
    stage.send(0)


def send_products(s, stage, matrix, state_ref, index):
    for b in row_blocks(s.extent):
        fill(s, stage.results[index], b, dot(matrix[b : b + 128, :], state_ref[...]).astype(BF16))
    stage.send(index)


def even_take(s, stage, small, temporaries):
    s_ref, t_ref, counts_ref = stage.results[2], stage.results[3], stage.results[4]
    me = lax.axis_index("aux") * s.rows + lax.axis_index("row")
    everyone = slice(0, s.devices)
    rows_in, row_lanes = stage.need(0), stage.need(1)
    for b in row_blocks(s.extent):
        s_ref[b : b + 128, :] = dot(
            flat_rows(rows_in, everyone, slice(b, b + 128)), row_lanes[...], ((0,), (0,))
        ).astype(BF16)
    stage.send(2)
    send_products(s, stage, stage.need(2), s_ref, 1)
    columns_in, column_lanes = stage.need(3), stage.need(4)
    blocks = s.extent // s.band
    parts = s.band // s.devices
    row, lane = iotas(s.devices, s.tile)
    mine = (row == me) & (lane < s.za)
    for q in range(s.rows):
        pieces = []
        for v in range(blocks):
            for g in range(s.groups):
                pieces.append(columns_in[g * s.rows + q, :, v * s.band : (v + 1) * s.band])
        t_ref[q * s.band : (q + 1) * s.band, :] = dot(
            jnp.concatenate(pieces, axis=0), column_lanes[...], ((0,), (0,))
        ).astype(BF16)
        rows = slice(q * s.band, q * s.band + s.devices)
        first = q * parts * s.za
        kept = s_ref[: s.devices, first : first + s.tile].astype(F32)
        t_ref[rows, : s.tile] = jnp.where(mine, kept, t_ref[rows, : s.tile].astype(F32)).astype(BF16)
    stage.send(3)
    send_products(s, stage, stage.need(5), t_ref, 0)
    row, lane = iotas(s.extent, MODES)
    gather = mask_to(row == lane * s.band + me)
    row, lane = iotas(s.auxes, s.per_device * s.groups * s.local)
    wanted = mask_to(lane == row * s.local)
    pieces = [columns_in[a // s.per_device * s.rows + a % s.per_device] for a in range(s.auxes)]
    counts_ref[...] = dot(wanted, dot(jnp.concatenate(pieces, axis=0), gather).astype(BF16))
    stage.send(4)


def even_turn(s, got_ref, order, swap, arrived):
    def load(start, size):
        return flat_rows(got_ref, slice(start // s.local, (start + size) // s.local))

    def put(rows, lanes, value):
        arrived[rows, lanes] = value

    turn(s, load, order, swap, put)


def even_next(s, weight, step, has_total, stage, small, temporaries):
    (arrived,) = temporaries
    s_ref, t_ref, ys_ref, yt_ref, total_ref = stage.results[2:7]
    got_s, order, swap = stage.need(0), stage.need(1), stage.need(2)
    even_turn(s, got_s, order, swap, arrived)
    ks_ref, ds_ref = stage.need(3), stage.need(4)
    total_in = stage.need(10) if has_total else None
    for b in row_blocks(s.extent, 64):
        rows = slice(b, b + 64)
        slope = ks_ref[rows, :] + arrived[rows, :]
        grown = weight * slope
        total_ref[rows, :] = total_in[rows, :] + grown if has_total else grown
        state = ds_ref[rows, :].astype(F32) + step * slope
        ys_ref[rows, :] = state
        s_ref[rows, :] = state.astype(BF16)
    for index in (2, 4, 6):
        stage.send(index)
    send_products(s, stage, stage.need(5), s_ref, 1)
    even_turn(s, stage.need(6), order, swap, arrived)
    kt_ref, dt_ref = stage.need(7), stage.need(8)
    for b in row_blocks(s.extent, 64):
        rows = slice(b, b + 64)
        slope = kt_ref[rows, :] - arrived[rows, :]
        state = dt_ref[rows, :].astype(F32) + step * slope
        yt_ref[rows, :] = state
        t_ref[rows, :] = state.astype(BF16)
    stage.send(3)
    stage.send(5)
    send_products(s, stage, stage.need(9), t_ref, 0)


def even_slope_part(s, direct, mirror, y_ref, h, unit, damp, q_ref, wa, wb, turned, sign, put):
    for th in range(s.tiles):
        lanes = slice(th * s.tile, (th + 1) * s.tile)
        turned[:, lanes] = dot(direct[:, lanes], unit[...]).astype(BF16)
    for b in row_blocks(s.extent):
        rows = slice(b, b + 128)
        whole = dot(h[rows, :], turned[...])
        for th in range(s.tiles):
            lanes = slice(th * s.tile, (th + 1) * s.tile)
            source = jnp.concatenate([direct[rows, lanes], mirror[rows, lanes]], axis=1)
            source = jnp.concatenate([source, source], axis=1)
            total = dot(source, wa[th]) - damp[:, lanes] * y_ref[rows, lanes].astype(F32)
            total = total + sign * whole[:, lanes]
            fields = dot(source, wb[...])
            for k in range(MODES):
                total = total + q_ref[rows, k : k + 1] * fields[:, k * s.tile : (k + 1) * s.tile]
            put(rows, lanes, total)


def even_slope(s, stage, small, temporaries):
    (turned,) = temporaries

    def put_in(index):
        def put(rows, lanes, value):
            stage.results[index][rows, lanes] = value

        return put

    need = stage.need
    unit, damp, q_ref = need(4), need(5), need(6)
    even_slope_part(
        s, need(0), need(1), need(2), need(7), unit, damp, q_ref, need(8), need(9), turned, -1.0, put_in(0)
    )
    stage.send(0)
    even_slope_part(
        s, need(1), need(0), need(3), need(10), unit, damp, q_ref, need(11), need(12), turned, 1.0, put_in(1)
    )
    stage.send(1)


def even_last(s, step, weight_three, weight_four, stage, small, temporaries):
    arrived, s_ref, t_ref, grown, turned, base = temporaries
    need = stage.need
    order, swap = need(1), need(2)
    even_turn(s, need(0), order, swap, arrived)
    kt_ref, dt_ref = need(3), need(4)
    for b in row_blocks(s.extent, 64):
        rows = slice(b, b + 64)
        slope = kt_ref[rows, :] - arrived[rows, :]
        t_ref[rows, :] = (dt_ref[rows, :].astype(F32) + step * slope).astype(BF16)
    unit, left, column_lanes = need(5), need(6), need(7)
    for th in range(s.tiles):
        lanes = slice(th * s.tile, (th + 1) * s.tile)
        turned[:, lanes] = dot(t_ref[:, lanes], unit[...]).astype(BF16)
    for b in row_blocks(s.extent):
        rows = slice(b, b + 128)
        grown[rows, :] = (weight_four * dot(left[rows, :], turned[...])).astype(BF16)
    out = stage.results[1]
    for q in range(s.rows):
        value = dot(column_lanes[...], grown[q * s.band : (q + 1) * s.band, :], ((1,), (1,))).astype(BF16)
        for v in range(s.extent // s.band):
            for g in range(s.groups):
                at = (v * s.groups + g) * s.local
                out[g * s.rows + q, :, v * s.band : (v + 1) * s.band] = value[at : at + s.local, :]
    stage.send(1)
    even_turn(s, need(8), order, swap, arrived)
    ks_ref, ds_ref, total_in = need(9), need(10), need(11)
    for b in row_blocks(s.extent, 64):
        rows = slice(b, b + 64)
        slope = ks_ref[rows, :] + arrived[rows, :]
        base[rows, :] = total_in[rows, :] + weight_three * slope
        state = ds_ref[rows, :].astype(F32) + step * slope
        arrived[rows, :] = state
        s_ref[rows, :] = state.astype(BF16)

    def put(rows, lanes, value):
        grown[rows, lanes] = (base[rows, lanes] + weight_four * value).astype(BF16)

    even_slope_part(
        s, s_ref, t_ref, arrived, need(14), unit, need(12), need(13), need(15), need(16), turned, -1.0, put
    )
    row_lanes = need(17)
    for b in row_blocks(s.extent):
        fill(s, stage.results[0], b, dot(row_lanes[b : b + 128, :], grown[...], ((1,), (1,))).astype(BF16))
    stage.send(0)


def even_finish(s, stage, small, temporaries):
    (post,) = temporaries
    post[...] = post_matrix(s)
    everyone = slice(0, s.devices)
    rows_in, columns_in = stage.need(0), stage.need(1)
    for v in range(s.extent // s.band):
        lanes = slice(v * s.band, (v + 1) * s.band)
        change = dot(post[:, lanes], flat_rows(rows_in, everyone), ((0,), (0,)))
        change = change + dot(flat_rows(columns_in, everyone, lanes), post[...], ((0,), (0,)))
        stage.results[v][...] = (stage.need(2 + v)[...].reshape(s.band, s.extent) + change).reshape(
            stage.results[v].shape
        )
        stage.send(v)


def hamiltonian_kernel(s, own_ref, outer_ref, where_ref, left, right, left_rows, right_rows, post):
    blocks, block = own_ref.shape[0], own_ref.shape[1]
    post[...] = post_matrix(s)
    row, column = iotas(block, s.extent)
    for b in range(blocks):
        spread = column - row
        to_own = mask_to(spread == b * block)
        to_far = mask_to(spread == where_ref[b] * block)
        left[b * block : (b + 1) * block, :] = (dot(own_ref[b], to_own) + dot(outer_ref[b], to_far)).astype(BF16)
    row, column = iotas(s.extent, s.extent)
    same = mask_to(row == column)
    for b in row_blocks(s.extent):
        rows = slice(b, b + 128)
        right[rows, :] = dot(same[rows, :], left[...], ((1,), (1,))).astype(BF16)
        left_rows[rows, :] = dot(post[rows, :], left[...]).astype(BF16)
        right_rows[rows, :] = dot(post[rows, :], left[...], ((1,), (1,))).astype(BF16)


def weights_kernel(
    s, real_ref, imag_ref, rate_ref, counts_ref, index_ref, mirror_ref, couplings_ref, wa_s, wb_s, wa_t, wb_t, damp
):
    me = lax.axis_index("aux") * s.rows + lax.axis_index("row")
    depth, wide = 2 * s.tile, MODES * s.tile
    row, column = iotas(s.auxes, wide)
    by_lane = mask_to(column % s.auxes == row)

    def spread(table):
        return dot(table.astype(F32).astype(BF16), by_lane, ((0,), (0,)))

    counts = spread(counts_ref[...])
    index, mirror = spread(index_ref[...]), spread(mirror_ref[...])
    lane_mode = lax.broadcasted_iota(jnp.int32, (1, wide), 1) // s.tile

    def of_mode(values):
        out = values[0]
        for k in range(1, MODES):
            out = jnp.where(lane_mode == k, values[k], out)
        return out

    take = lambda table, first: of_mode([table[first + k : first + k + 1, :] for k in range(MODES)])
    ups, downs = take(index, 0), take(index, MODES)
    up_kinds, down_kinds = take(mirror, 0), take(mirror, MODES)
    real = of_mode([counts[k : k + 1, :] * real_ref[k] for k in range(MODES)])
    imag = of_mode([counts[k : k + 1, :] * imag_ref[k] for k in range(MODES)])
    rates = counts[0:1, :] * rate_ref[0]
    for k in range(1, MODES):
        rates = rates + counts[k : k + 1, :] * rate_ref[k]
    damp[...] = rates

    row, column = iotas(s.extent, s.lanes)
    pick = (row % s.devices == me) & (row // s.devices == column // s.za)
    local_q = lax.dot_general(
        couplings_ref[...],
        pick.astype(F32),
        (((1,), (0,)), ((), ())),
        precision=lax.Precision.HIGHEST,
        preferred_element_type=F32,
    )

    row, column = iotas(depth, wide)
    same = row // s.za % s.fold == column // s.za % s.fold
    source, kind = (row % s.auxes).astype(F32), (row // s.tile).astype(F32)
    from_imag, to_imag = row // s.auxes % 2, column // s.auxes % 2
    up = same & (ups == source) & (up_kinds == kind)
    down = same & (downs == source) & (down_kinds == kind)
    along = jnp.where(up, 1.0, 0.0) + jnp.where(down, real, 0.0)
    cross = jnp.where(down, imag, 0.0)
    along = jnp.where(from_imag == 1, along, -along)
    flip = jnp.where((from_imag == 1) & (row // s.tile == 1), -1.0, 1.0)
    by_row = flip * jnp.where(from_imag == to_imag, cross, along)
    by_column = flip * jnp.where(from_imag == to_imag, cross, -along)

    def pieces(value):
        high = value.astype(BF16)
        return high, (value - high.astype(F32)).astype(BF16)

    for near, far, wa, wb in ((by_row, by_column, wa_s, wb_s), (by_column, by_row, wa_t, wb_t)):
        wb[:depth, :], wb[depth:, :] = pieces(far)
        for th in range(s.tiles):
            lanes = slice(th * s.tile, (th + 1) * s.tile)
            total = local_q[0:1, lanes] * near[:, : s.tile]
            for k in range(1, MODES):
                total = total + local_q[k : k + 1, lanes] * near[:, k * s.tile : (k + 1) * s.tile]
            wa[th, :depth, :], wa[th, depth:, :] = pieces(total)


def even_body(
    s,
    density,
    couplings,
    weight_real,
    weight_imag,
    mode_rates,
    tier_counts,
    link_index,
    link_mirror,
    block_diagonal,
    block_outer,
    block_column,
):
    planes, per_device, band, extent = density.shape
    cube = 2 * extent * extent * s.lanes
    state = shape(extent, s.lanes, dtype=BF16)
    full = shape(extent, s.lanes)
    pair = (shape(s.devices, 2, s.local, s.lanes, dtype=BF16), 2)
    held = pltpu.VMEM((extent, s.lanes), F32)
    held_b = pltpu.VMEM((extent, s.lanes), BF16)

    def exchange(message):
        return lax.all_to_all(message, BOTH, split_axis=0, concat_axis=0, tiled=True)

    blocks = density.reshape(1, planes * per_device, band, extent)
    message = run_staged(
        functools.partial(even_start, s),
        [pair],
        [(blocks, v) for v in range(planes * per_device)],
        temporaries=[held_b],
        scalars=[tier_counts],
        flops=2 * cube,
    )[0]
    got = exchange(message)

    left, right, left_rows, right_rows = run(
        functools.partial(hamiltonian_kernel, s),
        [state] * 4,
        [block_diagonal, block_outer, block_column],
        scratch=[held_b],
        flops=4 * cube,
        scalars=(2,),
    )
    q_first = couplings.T

    k, n = iotas(s.lanes, s.lanes)
    parts = band // s.devices
    row_lanes = (
        n
        == (k // s.local % s.rows * parts + k % parts) * s.za
        + k // (parts * per_device) % planes * s.auxes
        + k // (s.local * s.rows) * per_device
        + k // parts % per_device
    ).astype(BF16)
    column_lanes = (
        n
        == k % s.local * s.za
        + k // (s.local * s.groups * per_device) * s.auxes
        + k // s.local % s.groups * per_device
        + k // (s.local * s.groups) % per_device
    ).astype(BF16)

    k, n = iotas(s.tile, s.tile)
    sign = jnp.where(n // s.auxes % 2 == 0, 1.0, -1.0)
    unit = jnp.where(k // s.za * s.za + (k + s.auxes) % s.za == n, sign, 0.0).astype(BF16)
    k, n = iotas(s.fold * s.tile, s.fold * s.tile)
    sign = jnp.where(n // s.auxes % 2 == 0, 1.0, -1.0)
    there = (k // s.za % s.fold * s.fold + k // s.tile) * s.za + (k + s.auxes) % s.za
    swap = jnp.where(there == n, sign, 0.0).astype(BF16)
    size = max(256, 16 * s.local)
    span = size // s.local
    k, n = iotas(size, size)
    order = (n == k % span * s.local + k // span).astype(BF16)

    message, s_now, t_now, counts = run_staged(
        functools.partial(even_take, s),
        [pair, state, state, shape(s.auxes, MODES)],
        [(got, 0), row_lanes, right_rows, (got, 1), column_lanes, left_rows],
        flops=4 * cube,
    )
    wa = shape(s.tiles, 4 * s.tile, s.tile, dtype=BF16)
    wb = shape(4 * s.tile, MODES * s.tile, dtype=BF16)
    wa_s, wb_s, wa_t, wb_t, damp = run(
        functools.partial(weights_kernel, s),
        [wa, wb, wa, wb, shape(1, s.lanes)],
        [weight_real, weight_imag, mode_rates, counts, link_index, link_mirror, couplings],
        scalars=(0, 1, 2),
        flops=cube,
    )
    start_s, start_t = s_now, t_now
    ys, yt = s_now, t_now
    total = None
    shares = [STEP / 6.0, STEP / 3.0, STEP / 3.0, STEP / 6.0]
    steps = [0.25, 0.25, 0.5]
    for section in range(3):
        got = exchange(message)
        ks, kt = run_staged(
            functools.partial(even_slope, s),
            [full, full],
            [s_now, t_now, ys, yt, unit, damp, q_first, right, wa_s, wb_s, left, wa_t, wb_t],
            temporaries=[held_b],
            flops=12 * cube,
        )
        if section < 2:
            args = [(got, 0), order, swap, ks, start_s, right_rows, (got, 1), kt, start_t, left_rows]
            if total is not None:
                args.append(total)
            message, s_now, t_now, ys, yt, total = run_staged(
                functools.partial(even_next, s, shares[section], steps[section], total is not None),
                [pair, state, state, full, full, full],
                args,
                temporaries=[held],
                flops=6 * cube,
            )
    message = run_staged(
        functools.partial(even_last, s, steps[2], shares[2], shares[3]),
        [pair],
        [(got, 1), order, swap, kt, start_t, unit, left, column_lanes, (got, 0), ks, start_s, total]
        + [damp, q_first, right, wa_s, wb_s, row_lanes],
        temporaries=[held, held_b, held_b, held_b, held_b, held],
        flops=12 * cube,
    )[0]
    got = exchange(message)
    evolved = run_staged(
        functools.partial(even_finish, s),
        [(shape(1, planes * per_device, band, extent), planes * per_device)],
        [(got, 0), (got, 1)] + [(blocks, v) for v in range(planes * per_device)],
        temporaries=[held_b],
        flops=2 * cube,
    )[0]
    return evolved.reshape(density.shape)


def body(density, *others):
    planes, per_device, band, extent = density.shape
    s = Sizes(lax.axis_size("aux"), lax.axis_size("row"), per_device, band, extent)
    even = band % s.devices == 0 and s.local % 16 == 0 and LANES % s.za == 0
    even = even and s.lanes == extent and planes * per_device * band == extent
    even = even and planes * per_device == MODES and per_device <= s.rows and s.devices <= s.band
    if even:
        return even_body(s, density, *others)
    return general_body(density, *others)


def solution(mesh):
    return jax.shard_map(
        body,
        mesh=mesh,
        in_specs=(
            P(None, "aux", "row", None),
            P(),
            P(),
            P(),
            P(),
            P("aux", None),
            P(),
            P(),
            P(),
            P(),
            P(),
        ),
        out_specs=P(None, "aux", "row", None),
        check_vma=False,
    )
```

```python
import functools

import jax
import jax.numpy as jnp
from jax import lax
from jax.experimental import pallas as pl
from jax.experimental.pallas import tpu as pltpu
from jax.sharding import PartitionSpec as P

MODES = 4
LINKS = 8
LANES = 128
STEP = 0.5
BOTH = ("aux", "row")
GRANT = 52 << 20

F32 = jnp.float32
BF16 = jnp.bfloat16


class Sizes:
    def __init__(self, groups, rows, per_device, band, extent):
        self.groups, self.rows, self.per_device = groups, rows, per_device
        self.band, self.extent = band, extent
        self.devices = groups * rows
        self.local = band // groups
        self.auxes = per_device * groups
        self.za = 2 * self.auxes
        self.lanes = self.local * self.za
        self.fold = max(1, LANES // self.za)
        self.tile = self.fold * self.za
        self.tiles = self.local // self.fold
        self.joined = self.local % 16 == 0


def dot(a, b, dims=((1,), (0,))):
    return lax.dot_general(a, b, (dims, ((), ())), preferred_element_type=F32)


def run(kernel, outs, args, scratch=(), flops=0, scalars=()):
    spec = pl.BlockSpec(memory_space=pltpu.VMEM)
    flat = pl.BlockSpec(memory_space=pltpu.SMEM)
    moved = sum(a.size * a.dtype.itemsize for a in args)
    moved += sum(o.size * o.dtype.itemsize for o in outs)
    return pl.pallas_call(
        kernel,
        out_shape=list(outs),
        in_specs=[flat if n in scalars else spec for n in range(len(args))],
        out_specs=[spec] * len(outs),
        scratch_shapes=list(scratch),
        compiler_params=pltpu.CompilerParams(vmem_limit_bytes=16 << 20),
        cost_estimate=pl.CostEstimate(flops=flops, bytes_accessed=moved, transcendentals=0),
    )(*args)


def shape(*dims, dtype=F32):
    return jax.ShapeDtypeStruct(dims, dtype)


def one_hot(target, count):
    return (target[:, None] == jnp.arange(count, dtype=jnp.int32)[None, :]).astype(BF16)


def matrix_index(s, index, device):
    group, row = device // s.rows, device % s.rows
    return row * s.band + index * s.groups + group


def row_blocks(extent, size=128):
    return range(0, extent, size)


def send_start_kernel(d_ref, pick_rows, pick_cols, out_ref):
    planes, number, band, extent = d_ref.shape
    flat = d_ref[...].reshape(planes * number * band, extent).astype(BF16)
    for b in row_blocks(flat.shape[0]):
        moved = dot(pick_rows[b : b + 128, :], flat).astype(BF16)
        out_ref[b : b + 128, :] = dot(moved, pick_cols[...]).astype(BF16)


def take_start_kernel(got_ref, pick_lanes, message_rows, s_ref, m_ref):
    for b in row_blocks(got_ref.shape[1]):
        s_ref[b : b + 128, :] = dot(
            got_ref[:, b : b + 128], pick_lanes[...], ((0,), (0,))
        ).astype(BF16)
    for b in row_blocks(m_ref.shape[0]):
        m_ref[b : b + 128, :] = dot(message_rows[b : b + 128, :], s_ref[...]).astype(BF16)


def turn(s, load, order, swap, put):
    size = order.shape[0]
    span = size // s.local
    for block in range(s.extent // size):
        moved = dot(order[...], load(block * size, size))
        parts = []
        for ih in range(s.tiles):
            for jh in range(s.tiles):
                lanes = slice(jh * s.tile, (jh + 1) * s.tile)
                pieces = [
                    moved[(ih * s.fold + f) * span : (ih * s.fold + f + 1) * span, lanes]
                    for f in range(s.fold)
                ]
                parts.append(jnp.concatenate(pieces, axis=1) if s.fold > 1 else pieces[0])
        turned = dot(jnp.concatenate(parts, axis=0).astype(BF16), swap[...])
        for ih in range(s.tiles):
            for jh in range(s.tiles):
                start = (ih * s.tiles + jh) * span
                for f in range(s.fold):
                    first = (jh * s.fold + f) * s.devices + block * span
                    put(
                        slice(first, first + span),
                        slice(ih * s.tile, (ih + 1) * s.tile),
                        turned[start : start + span, f * s.tile : (f + 1) * s.tile],
                    )


def take_columns_kernel(s, got_ref, order, swap, first_rows, left_rows, s_ref, t_ref, *message):
    def put(rows, lanes, value):
        t_ref[rows, lanes] = value.astype(BF16)

    turn(s, lambda start, size: got_ref[start : start + size, :], order, swap, put)
    write_messages(s, first_rows, left_rows, s_ref, t_ref, message)


def write_messages(s, right_rows, left_rows, s_ref, t_ref, message):
    pairs = ((left_rows, t_ref), (right_rows, s_ref))
    if not s.joined and len(message) == 1:
        pairs = pairs[:1]
    both = s.joined and message[0].shape[0] == 2 * s.extent
    for part, (matrix, state) in enumerate(pairs):
        if s.joined and part == 1 and not both:
            continue
        for b in row_blocks(s.extent):
            product = dot(matrix[b : b + 128, :], state[...]).astype(BF16)
            if not s.joined:
                message[part][b : b + 128, :] = product
            elif not both:
                message[0][b : b + 128, :] = product
            else:
                for k in range(128 // s.local):
                    start = ((b // s.local + k) * 2 + part) * s.local
                    message[0][start : start + s.local, :] = product[
                        k * s.local : (k + 1) * s.local, :
                    ]


def slope_kernel(
    s, with_columns, s_ref, t_ref, ys_ref, yt_ref, damp, q_ref, right, left, unit, wa_s, wb_s, wa_t, wb_t, *rest
):
    if with_columns:
        ks_ref, kt_ref, turned = rest
    else:
        ks_ref, turned = rest

    def one(direct, mirror, y_ref, h, wa, wb, out_ref, sign):
        for th in range(s.tiles):
            lanes = slice(th * s.tile, (th + 1) * s.tile)
            turned[:, lanes] = dot(direct[:, lanes], unit[...]).astype(BF16)
        for b in row_blocks(s.extent):
            rows = slice(b, b + 128)
            whole = dot(h[rows, :], turned[...])
            for th in range(s.tiles):
                lanes = slice(th * s.tile, (th + 1) * s.tile)
                source = jnp.concatenate([direct[rows, lanes], mirror[rows, lanes]], axis=1)
                source = jnp.concatenate([source, source], axis=1)
                total = dot(source, wa[th]) - damp[:, lanes] * y_ref[rows, lanes].astype(F32)
                total = total + sign * whole[:, lanes]
                fields = dot(source, wb[...])
                for k in range(MODES):
                    total = total + q_ref[rows, k : k + 1] * fields[:, k * s.tile : (k + 1) * s.tile]
                out_ref[rows, lanes] = total

    one(s_ref, t_ref, ys_ref, right, wa_s, wb_s, ks_ref, -1.0)
    if with_columns:
        one(t_ref, s_ref, yt_ref, left, wa_t, wb_t, kt_ref, 1.0)


def part_loader(s, refs, part):
    def load(start, size):
        if not s.joined:
            return refs[part][start : start + size, :]
        step = s.local
        pieces = []
        for first in range(start, start + size, step):
            at = (first // step * 2 + part) * step
            pieces.append(refs[0][at : at + step, :])
        return jnp.concatenate(pieces, axis=0)

    return load


def next_kernel(s, weight, step, has_total, both, got_count, *refs):
    got = refs[:got_count]
    refs = refs[got_count:]
    order, swap, right_rows, left_rows, ks_ref, kt_ref, ds_ref, dt_ref = refs[:8]
    refs = refs[8:]
    total_in = None
    if has_total:
        total_in, refs = refs[0], refs[1:]
    s_ref, t_ref, ys_ref, yt_ref, total_ref = refs[:5]
    message, arrived = refs[5:-1], refs[-1]

    def put(rows, lanes, value):
        arrived[rows, lanes] = value

    for part in range(2):
        turn(s, part_loader(s, got, part), order, swap, put)
        for b in row_blocks(s.extent, 64):
            rows = slice(b, b + 64)
            if part == 0:
                slope = ks_ref[rows, :] + arrived[rows, :]
                grown = weight * slope
                total_ref[rows, :] = total_in[rows, :] + grown if has_total else grown
                state = ds_ref[rows, :].astype(F32) + step * slope
                ys_ref[rows, :] = state
                s_ref[rows, :] = state.astype(BF16)
            else:
                slope = kt_ref[rows, :] - arrived[rows, :]
                state = dt_ref[rows, :].astype(F32) + step * slope
                yt_ref[rows, :] = state
                t_ref[rows, :] = state.astype(BF16)
    if message:
        write_messages(s, right_rows, left_rows, s_ref, t_ref, message)


def last_kernel(s, weight, got_ref, order, swap, ks_ref, total_in, pick_lanes, out_ref, arrived, grown):
    def put(rows, lanes, value):
        arrived[rows, lanes] = value

    turn(s, lambda start, size: got_ref[start : start + size, :], order, swap, put)
    for b in row_blocks(s.extent, 64):
        rows = slice(b, b + 64)
        change = total_in[rows, :] + weight * (ks_ref[rows, :] + arrived[rows, :])
        grown[rows, :] = change.astype(BF16)
    for b in row_blocks(s.lanes):
        out_ref[b : b + 128, :] = dot(
            pick_lanes[b : b + 128, :], grown[...], ((1,), (1,))
        ).astype(BF16)


def finish_kernel(got_ref, place_rows, place_cols, d_ref, out_ref):
    planes, number, band, extent = d_ref.shape
    for z in range(planes):
        for n in range(number):
            at = (z * number + n) * band
            for b in range(0, band, min(band, 128)):
                size = min(band, 128)
                rows = slice(at + b, at + b + size)
                moved = dot(place_rows[rows, :], got_ref[...]).astype(BF16)
                out_ref[z, n, b : b + size, :] = d_ref[z, n, b : b + size, :] + dot(
                    moved, place_cols[...]
                )


def link_matrices(s, counts, weight_real, weight_imag, link_index, link_mirror):
    ones = jnp.ones_like(counts)
    real = jnp.stack([ones, counts * weight_real[None, :]], 1)
    imag = jnp.stack([jnp.zeros_like(counts), counts * weight_imag[None, :]], 1)
    index = link_index.reshape(s.auxes, 2, MODES)
    mirror = link_mirror.reshape(s.auxes, 2, MODES)
    source = jnp.arange(s.auxes, dtype=jnp.int32)
    hit = index[None] == source[:, None, None, None]
    kinds = jnp.stack([hit & (mirror[None] == 0), hit & (mirror[None] == 1)]).astype(F32)
    along = jnp.sum(kinds * real, 3)
    cross = jnp.sum(kinds * imag, 3)
    along, cross = (jnp.transpose(m, (0, 3, 1, 2)) for m in (along, cross))
    flip = jnp.array([1.0, -1.0], F32).reshape(2, 1, 1, 1)

    def build(sign):
        upper = jnp.concatenate([cross, -sign * along], 3)
        lower = jnp.concatenate([sign * along, cross], 3) * flip
        return jnp.concatenate([upper, lower], 2)

    return build(1.0), build(-1.0)


def two_pieces(weights, axis):
    high = lax.reduce_precision(weights, 8, 7)
    low = weights - high
    return jnp.concatenate([high.astype(BF16), low.astype(BF16)], axis)


def coupling_weights(s, by_local, by_first, local_q):
    eye = jnp.eye(s.fold, dtype=F32)
    near = jnp.einsum("ki,xkuv->ixuv", local_q, by_local, precision=lax.Precision.HIGHEST)
    near = near.reshape(s.tiles, s.fold, 2, s.za, s.za)
    near = jnp.transpose(near, (0, 2, 1, 3, 4))[:, :, :, :, None, :] * eye[None, None, :, None, :, None]
    near = near.reshape(s.tiles, 2 * s.tile, s.tile)
    far = jnp.transpose(by_first, (0, 2, 1, 3))[:, None, :, :, None, :] * eye[None, :, None, None, :, None]
    far = far.reshape(2 * s.tile, MODES * s.tile)
    return two_pieces(near, 1), two_pieces(far, 0)


def general_body(
    density,
    couplings,
    weight_real,
    weight_imag,
    mode_rates,
    tier_counts,
    link_index,
    link_mirror,
    block_diagonal,
    block_outer,
    block_column,
):
    planes, per_device, band, extent = density.shape
    s = Sizes(lax.axis_size("aux"), lax.axis_size("row"), per_device, band, extent)
    blocks, block = block_diagonal.shape[0], block_diagonal.shape[1]
    group, row = lax.axis_index("aux"), lax.axis_index("row")
    device = group * s.rows + row
    cube = 2 * extent * extent * s.lanes

    number = jnp.arange(extent, dtype=jnp.int32)
    first_to_matrix = matrix_index(s, number // s.devices, number % s.devices)
    posted_to_matrix = matrix_index(s, number % s.local, number // s.local)
    posted_to_first = number % s.local * s.devices + number // s.local

    wide = jnp.arange(s.lanes, dtype=jnp.int32)
    sub = planes * per_device * s.local
    start_source = wide % sub * s.groups + wide // sub
    pick_rows = one_hot(start_source, s.lanes)
    pick_cols = one_hot(first_to_matrix, extent).T
    lane_of = (
        wide % s.local * s.za
        + wide // (per_device * s.local) % planes * s.auxes
        + wide // sub * per_device
        + wide // s.local % per_device
    )
    pick_lanes = one_hot(lane_of, s.lanes)
    message_rows = one_hot(posted_to_first, extent)
    start_message = run(
        send_start_kernel,
        [shape(s.lanes, extent, dtype=BF16)],
        [density, pick_rows, pick_cols],
        flops=2 * cube,
    )[0]
    start_got = lax.all_to_all(
        start_message.reshape(s.groups, sub, extent), "aux", split_axis=0, concat_axis=0, tiled=True
    ).reshape(s.lanes, extent)

    selector = block_column[:, None] == jnp.arange(blocks, dtype=jnp.int32)[None, :]
    own = jnp.eye(blocks, dtype=F32)
    whole_h = (
        own[:, None, :, None] * block_diagonal.astype(F32)[:, :, None, :]
        + selector.astype(F32)[:, None, :, None] * block_outer.astype(F32)[:, :, None, :]
    ).reshape(extent, extent).astype(BF16)
    first_h = one_hot(first_to_matrix, extent)
    left = jnp.dot(
        jnp.dot(first_h, whole_h, preferred_element_type=BF16), first_h.T, preferred_element_type=BF16
    )
    right = left.T
    left_rows = jnp.dot(message_rows, left, preferred_element_type=BF16)
    right_rows = jnp.dot(message_rows, right, preferred_element_type=BF16)

    counts = lax.all_gather(tier_counts, "aux", axis=0, tiled=True).astype(F32)
    damping = jnp.sum(counts * mode_rates[None, :], axis=1)
    damp = jnp.tile(damping, (planes * s.local,))[None, :]
    q_first = jnp.dot(
        couplings, first_h.T.astype(F32), precision=lax.Precision.HIGHEST
    ).T
    local_pick = (matrix_index(s, jnp.arange(s.local, dtype=jnp.int32), device)[None, :] == number[:, None])
    local_q = jnp.dot(couplings, local_pick.astype(F32), precision=lax.Precision.HIGHEST)
    by_row, by_column = link_matrices(s, counts, weight_real, weight_imag, link_index, link_mirror)
    wa_s, wb_s = coupling_weights(s, by_row, by_column, local_q)
    wa_t, wb_t = coupling_weights(s, by_column, by_row, local_q)

    lane = jnp.arange(s.za, dtype=jnp.int32)
    unit = jnp.where(
        lane[:, None] == (lane[None, :] + s.auxes) % s.za,
        jnp.where(lane[None, :] < s.auxes, 1.0, -1.0),
        0.0,
    )
    eye_fold = jnp.eye(s.fold, dtype=F32)
    unit_tile = (eye_fold[:, None, :, None] * unit[None, :, None, :]).reshape(s.tile, s.tile).astype(BF16)
    swap = (
        eye_fold[:, None, None, None, :, None]
        * eye_fold[None, :, None, :, None, None]
        * unit[None, None, :, None, None, :]
    ).reshape(s.fold * s.tile, s.fold * s.tile).astype(BF16)
    keep = (
        eye_fold[:, None, None, None, :, None]
        * eye_fold[None, :, None, :, None, None]
        * jnp.eye(s.za, dtype=F32)[None, None, :, None, None, :]
    ).reshape(s.fold * s.tile, s.fold * s.tile).astype(BF16)
    size = min(extent, max(256, 16 * s.local))
    span = size // s.local
    at = jnp.arange(size, dtype=jnp.int32)
    order = one_hot(at % span * s.local + at // span, size)

    state = shape(extent, s.lanes, dtype=BF16)
    full = shape(extent, s.lanes)
    held = pltpu.VMEM((extent, s.lanes), F32)
    held_b = pltpu.VMEM((extent, s.lanes), BF16)

    def exchange(messages):
        parts = [m.reshape(s.devices, -1, s.lanes) for m in messages]
        sent = parts[0] if len(parts) == 1 else jnp.concatenate(parts, 1)
        got = lax.all_to_all(sent, BOTH, split_axis=0, concat_axis=0, tiled=True)
        if len(parts) == 1:
            return [got.reshape(-1, s.lanes)]
        height = s.local
        return [got[:, p * height : (p + 1) * height].reshape(-1, s.lanes) for p in range(2)]

    if s.joined:
        pair = [shape(2 * extent, s.lanes, dtype=BF16)]
    else:
        pair = [state, state]

    s_now, posted = run(
        take_start_kernel, [state, state], [start_got, pick_lanes, message_rows], flops=2 * cube
    )
    got = exchange([posted])
    t_now, *messages = run(
        functools.partial(take_columns_kernel, s),
        [state] + pair,
        [got[0], order, keep, right_rows, left_rows, s_now],
        flops=4 * cube,
    )
    start_s, start_t = s_now, t_now
    ys, yt = s_now, t_now
    total = None
    shares = [STEP / 6.0, STEP / 3.0, STEP / 3.0, STEP / 6.0]
    steps = [0.25, 0.25, 0.5]
    for section in range(4):
        got = exchange(messages)
        columns = section < 3
        slopes = run(
            functools.partial(slope_kernel, s, columns),
            [full, full] if columns else [full],
            [s_now, t_now, ys, yt, damp, q_first, right, left, unit_tile, wa_s, wb_s, wa_t, wb_t],
            scratch=[held_b],
            flops=(12 if columns else 6) * cube,
        )
        if columns:
            args = list(got) + [order, swap, right_rows, left_rows, *slopes, start_s, start_t]
            if total is not None:
                args.append(total)
            outs = [state, state, full, full, full]
            outs += pair if section < 2 else [state]
            s_now, t_now, ys, yt, total, *messages = run(
                functools.partial(
                    next_kernel, s, shares[section], steps[section], total is not None, section < 2, len(got)
                ),
                outs,
                args,
                scratch=[held],
                flops=6 * cube,
            )
    change = run(
        functools.partial(last_kernel, s, shares[3]),
        [shape(s.lanes, extent, dtype=BF16)],
        [got[0], order, swap, slopes[0], total, pick_lanes],
        scratch=[held, held_b],
        flops=3 * cube,
    )[0]
    back = lax.all_to_all(
        change.reshape(s.groups, sub, extent), "aux", split_axis=0, concat_axis=0, tiled=True
    ).reshape(s.lanes, extent)
    return run(
        finish_kernel,
        [shape(planes, per_device, band, extent)],
        [back, pick_rows.T, pick_cols.T, density],
        flops=2 * cube,
    )[0]


def iotas(rows, columns):
    return (
        lax.broadcasted_iota(jnp.int32, (rows, columns), 0),
        lax.broadcasted_iota(jnp.int32, (rows, columns), 1),
    )


def mask_to(value):
    return value.astype(F32).astype(BF16)


def post_matrix(s):
    row, column = iotas(s.extent, s.extent)
    return mask_to(column == row % s.local * s.devices + row // s.local)


class Stage:
    def __init__(self, sources, buffers, targets, results, semaphores, offset, lead):
        self.buffers, self.results, self.targets = buffers, results, targets
        self.semaphores, self.next, self.offset = semaphores, 0, offset
        self.sources, self.lead = sources, lead
        self.coming = [self.copy(a, b) for a, b in zip(sources[:lead], buffers)]
        self.going = []

    def copy(self, source, target):
        made = pltpu.make_async_copy(source, target, self.semaphores.at[self.next])
        self.next += 1
        made.start()
        return made

    def front(self, index):
        return self.need(index - self.offset)

    def need(self, index):
        index += self.offset
        if index >= len(self.coming):
            self.start_rest()
        if self.coming[index] is not None:
            self.coming[index].wait()
            self.coming[index] = None
        return self.buffers[index]

    def start_rest(self):
        known = len(self.coming)
        self.coming += [self.copy(a, b) for a, b in zip(self.sources[known:], self.buffers[known:])]

    def send(self, index):
        self.going.append(self.copy(self.results[index], self.targets[index]))

    def finish(self):
        for made in self.going:
            made.wait()


def run_staged(body, outs, args, temporaries=(), scalars=(), front=(), lead=None, flops=0):
    arrays, views = [], []
    for arg in [*front, *args]:
        array, part = arg if isinstance(arg, tuple) else (arg, None)
        if not any(array is a for a in arrays):
            arrays.append(array)
        views.append(([array is a for a in arrays].index(True), part))
    shapes, places = [], []
    for out in outs:
        if isinstance(out, tuple):
            for part in range(out[1]):
                places.append((len(shapes), part))
            shapes.append(out[0])
        else:
            places.append((len(shapes), None))
            shapes.append(out)
    tall = lambda x, part: x.shape if part is None else x.shape[:1] + x.shape[2:]
    buffers = [pltpu.VMEM(tall(arrays[k], part), arrays[k].dtype) for k, part in views]
    results = [pltpu.VMEM(tall(shapes[k], part), shapes[k].dtype) for k, part in places]
    count = len(buffers) + len(results)

    def kernel(*refs):
        small, refs = refs[: len(scalars)], refs[len(scalars) :]
        source, refs = refs[: len(arrays)], refs[len(arrays) :]
        target, refs = refs[: len(shapes)], refs[len(shapes) :]
        own, refs = refs[: len(buffers)], refs[len(buffers) :]
        made, refs = refs[: len(results)], refs[len(results) :]
        pick = lambda ref, part: ref if part is None else ref.at[:, part]
        stage = Stage(
            [pick(source[k], part) for k, part in views],
            own,
            [pick(target[k], part) for k, part in places],
            made,
            refs[-1],
            len(front),
            len(views) if lead is None else lead,
        )
        body(stage, small, refs[:-1])
        stage.finish()

    moved = sum(a.size * a.dtype.itemsize for a in arrays)
    moved += sum(o.size * o.dtype.itemsize for o in shapes)
    far = pl.BlockSpec(memory_space=pltpu.HBM)
    return pl.pallas_call(
        kernel,
        out_shape=shapes,
        in_specs=[pl.BlockSpec(memory_space=pltpu.SMEM)] * len(scalars) + [far] * len(arrays),
        out_specs=[far] * len(shapes),
        scratch_shapes=buffers + results + list(temporaries) + [pltpu.SemaphoreType.DMA((count,))],
        compiler_params=pltpu.CompilerParams(vmem_limit_bytes=GRANT),
        cost_estimate=pl.CostEstimate(flops=flops, bytes_accessed=moved, transcendentals=0),
    )(*scalars, *arrays)


def fill(s, result, first, value, lanes=slice(None)):
    count = value.shape[0] // s.local
    device = first // s.local
    result[device : device + count, :, lanes] = value.reshape(count, s.local, value.shape[1])


def flat_rows(ref, rows, lanes=slice(None)):
    piece = ref[rows, :, lanes]
    return piece.reshape(piece.shape[0] * piece.shape[1], piece.shape[2])


def even_start(s, stage, small, temporaries):
    (post,) = temporaries
    post[...] = post_matrix(s)
    blocks = s.extent // s.band
    which = lax.axis_index("row") % s.per_device
    flats = [stage.need(v)[...].reshape(s.band, s.extent).astype(BF16) for v in range(blocks)]
    row, lane = iotas(128, s.band)
    counts = stage.need(blocks)[...].astype(F32)
    mine = counts[0:1, :]
    for n in range(1, s.per_device):
        mine = jnp.where(which == n, counts[n : n + 1, :], mine)
    for v in range(blocks):
        count = mine[:, v : v + 1]
        for b in row_blocks(s.extent):
            value = dot(post[b : b + 128, :], flats[v], ((1,), (1,)))
            own = (row % s.local == 0) & (lane == (row + b) // s.local)
            value = jnp.where(own, count, value).astype(BF16)
            fill(s, stage.results[1], b, value, slice(v * s.band, (v + 1) * s.band))
    stage.send(1)
    flat = jnp.concatenate(flats, axis=0)
    for b in row_blocks(s.extent):
        fill(s, stage.results[0], b, dot(post[b : b + 128, :], flat).astype(BF16))
    stage.send(0)


def send_products(s, stage, matrix, state_ref, index):
    for b in row_blocks(s.extent):
        fill(s, stage.results[index], b, dot(matrix[b : b + 128, :], state_ref[...]).astype(BF16))
    stage.send(index)


def even_take(s, stage, small, temporaries):
    s_ref, t_ref = stage.results[2], stage.results[3]
    me = lax.axis_index("aux") * s.rows + lax.axis_index("row")
    everyone = slice(0, s.devices)
    rows_in, row_lanes = stage.front(0), stage.need(0)
    for b in row_blocks(s.extent):
        s_ref[b : b + 128, :] = dot(
            flat_rows(rows_in, everyone, slice(b, b + 128)), row_lanes[...], ((0,), (0,))
        ).astype(BF16)
    stage.send(2)
    send_products(s, stage, stage.need(1), s_ref, 1)
    columns_in, column_lanes = stage.front(1), stage.need(2)
    blocks = s.extent // s.band
    parts = s.band // s.devices
    row, lane = iotas(s.devices, s.tile)
    mine = (row == me) & (lane < s.za)
    for q in range(s.rows):
        pieces = []
        for v in range(blocks):
            for g in range(s.groups):
                pieces.append(columns_in[g * s.rows + q, :, v * s.band : (v + 1) * s.band])
        t_ref[q * s.band : (q + 1) * s.band, :] = dot(
            jnp.concatenate(pieces, axis=0), column_lanes[...], ((0,), (0,))
        ).astype(BF16)
        rows = slice(q * s.band, q * s.band + s.devices)
        first = q * parts * s.za
        kept = s_ref[: s.devices, first : first + s.tile].astype(F32)
        t_ref[rows, : s.tile] = jnp.where(mine, kept, t_ref[rows, : s.tile].astype(F32)).astype(BF16)
    stage.send(3)
    send_products(s, stage, stage.need(3), t_ref, 0)


def turn_matrices(s, order, swap):
    size = order.shape[0]
    span = size // s.local
    k, n = lax.broadcasted_iota(jnp.int32, (size, 1), 0), lax.broadcasted_iota(jnp.int32, (1, size), 1)
    order[...] = mask_to(n == k % span * s.local + k // span)
    wide = s.fold * s.tile
    k, n = lax.broadcasted_iota(jnp.int32, (wide, 1), 0), lax.broadcasted_iota(jnp.int32, (1, wide), 1)
    sign = jnp.where(n // s.auxes % 2 == 0, 1.0, -1.0)
    there = (k // s.za % s.fold * s.fold + k // s.tile) * s.za + (k + s.auxes) % s.za
    swap[...] = jnp.where(there == n, sign, 0.0).astype(BF16)


def even_turn(s, got, order, swap, put):
    def load(start, size):
        return flat_rows(got, slice(start // s.local, (start + size) // s.local))

    turn(s, load, order, swap, put)


def updates(s, step, sign, k_ref, d_ref, keep):
    def put(rows, lanes, value):
        own = k_ref[rows, lanes]
        slope = own + value if sign > 0 else own - value
        keep(rows, lanes, d_ref[rows, lanes].astype(F32) + step * slope)

    return put


def even_next(s, step, stage, small, temporaries):
    s_ref, t_ref, order, swap = temporaries
    turn_matrices(s, order, swap)

    def keep_in(ref):
        def keep(rows, lanes, value):
            ref[rows, lanes] = value.astype(BF16)

        return keep

    got = stage.front(0)
    stage.start_rest()
    even_turn(s, got, order, swap, updates(s, step, 1, stage.need(0), stage.need(1), keep_in(s_ref)))
    send_products(s, stage, stage.need(2), s_ref, 1)
    got = stage.need(3)
    even_turn(s, got, order, swap, updates(s, step, -1, stage.need(4), stage.need(5), keep_in(t_ref)))
    send_products(s, stage, stage.need(6), t_ref, 0)


def even_slope_part(s, direct, mirror, y_ref, h, unit, damp, q_ref, wa, wb, turned, sign, put):
    for th in range(s.tiles):
        lanes = slice(th * s.tile, (th + 1) * s.tile)
        turned[:, lanes] = dot(direct[:, lanes], unit[...]).astype(BF16)
    for b in row_blocks(s.extent):
        rows = slice(b, b + 128)
        whole = dot(h[rows, :], turned[...])
        for th in range(s.tiles):
            lanes = slice(th * s.tile, (th + 1) * s.tile)
            source = jnp.concatenate([direct[rows, lanes], mirror[rows, lanes]], axis=1)
            source = jnp.concatenate([source, source], axis=1)
            total = dot(source, wa[th]) - damp[:, lanes] * y_ref[rows, lanes].astype(F32)
            total = total + sign * whole[:, lanes]
            fields = dot(source, wb[...])
            for k in range(MODES):
                total = total + q_ref[rows, k : k + 1] * fields[:, k * s.tile : (k + 1) * s.tile]
            put(rows, lanes, total)


def put_in(ref):
    def put(rows, lanes, value):
        ref[rows, lanes] = value

    return put


def even_first_slope(s, stage, small, temporaries):
    (turned,) = temporaries
    need = stage.need
    first, second = stage.results
    s_ref, t_ref, unit, damp, q_ref = need(0), need(1), need(2), need(3), need(4)
    even_slope_part(
        s, s_ref, t_ref, s_ref, need(5), unit, damp, q_ref, need(6), need(7), turned, -1.0, put_in(first)
    )
    stage.send(0)
    even_slope_part(
        s, t_ref, s_ref, t_ref, need(8), unit, damp, q_ref, need(9), need(10), turned, 1.0, put_in(second)
    )
    stage.send(1)


def even_slope(s, step, ratio, has_total, stage, small, temporaries):
    turned, s_ref, t_ref, ys_ref, yt_ref, order, swap = temporaries
    turn_matrices(s, order, swap)
    need = stage.need
    first, second, total_ref = stage.results

    def keep_in(ref, exact):
        def keep(rows, lanes, value):
            exact[rows, lanes] = value
            ref[rows, lanes] = value.astype(BF16)

        return keep

    ds_ref = need(1)
    even_turn(
        s,
        stage.front(0),
        order,
        swap,
        updates(s, step, 1, need(0), ds_ref, keep_in(s_ref, ys_ref)),
    )
    even_turn(
        s,
        stage.front(1),
        order,
        swap,
        updates(s, step, -1, need(2), need(3), keep_in(t_ref, yt_ref)),
    )
    total_in = need(13) if has_total else None
    for b in row_blocks(s.extent, 64):
        rows = slice(b, b + 64)
        grown = ratio * (ys_ref[rows, :] - ds_ref[rows, :].astype(F32))
        total_ref[rows, :] = total_in[rows, :] + grown if has_total else grown
    stage.send(2)
    unit, damp, q_ref = need(4), need(5), need(6)
    even_slope_part(
        s, s_ref, t_ref, ys_ref, need(7), unit, damp, q_ref, need(8), need(9), turned, -1.0, put_in(first)
    )
    stage.send(0)
    even_slope_part(
        s, t_ref, s_ref, yt_ref, need(10), unit, damp, q_ref, need(11), need(12), turned, 1.0, put_in(second)
    )
    stage.send(1)


def even_last(s, step, ratio, weight, stage, small, temporaries):
    ys_ref, s_ref, t_ref, grown, turned, order, swap = temporaries
    turn_matrices(s, order, swap)
    need = stage.need

    def keep_columns(rows, lanes, value):
        t_ref[rows, lanes] = value.astype(BF16)

    put = updates(s, step, -1, need(0), need(1), keep_columns)
    got = stage.front(0)
    stage.start_rest()
    even_turn(s, got, order, swap, put)
    unit, left, column_lanes = need(2), need(3), need(4)
    for th in range(s.tiles):
        lanes = slice(th * s.tile, (th + 1) * s.tile)
        turned[:, lanes] = dot(t_ref[:, lanes], unit[...]).astype(BF16)
    for b in row_blocks(s.extent):
        rows = slice(b, b + 128)
        grown[rows, :] = (weight * dot(left[rows, :], turned[...])).astype(BF16)
    out = stage.results[1]
    for q in range(s.rows):
        value = dot(column_lanes[...], grown[q * s.band : (q + 1) * s.band, :], ((1,), (1,))).astype(BF16)
        for v in range(s.extent // s.band):
            for g in range(s.groups):
                at = (v * s.groups + g) * s.local
                out[g * s.rows + q, :, v * s.band : (v + 1) * s.band] = value[at : at + s.local, :]
    stage.send(1)

    def keep_rows(rows, lanes, value):
        ys_ref[rows, lanes] = value
        s_ref[rows, lanes] = value.astype(BF16)

    ds_ref = need(6)
    put = updates(s, step, 1, need(5), ds_ref, keep_rows)
    even_turn(s, stage.front(1), order, swap, put)
    total_in = need(7)

    def put_change(rows, lanes, value):
        change = total_in[rows, lanes] + ratio * (ys_ref[rows, lanes] - ds_ref[rows, lanes].astype(F32))
        grown[rows, lanes] = (change + weight * value).astype(BF16)

    even_slope_part(
        s, s_ref, t_ref, ys_ref, need(10), unit, need(8), need(9), need(11), need(12), turned, -1.0, put_change
    )
    row_lanes = need(13)
    for b in row_blocks(s.extent):
        fill(s, stage.results[0], b, dot(row_lanes[b : b + 128, :], grown[...], ((1,), (1,))).astype(BF16))
    stage.send(0)


def even_finish(s, stage, small, temporaries):
    (post,) = temporaries
    post[...] = post_matrix(s)
    everyone = slice(0, s.devices)
    for v in range(s.extent // s.band):
        lanes = slice(v * s.band, (v + 1) * s.band)
        change = dot(post[:, lanes], flat_rows(stage.front(0), everyone), ((0,), (0,)))
        change = change + dot(flat_rows(stage.front(1), everyone, lanes), post[...], ((0,), (0,)))
        stage.results[v][...] = (stage.need(v)[...].reshape(s.band, s.extent) + change).reshape(
            stage.results[v].shape
        )
        stage.send(v)


def even_hamiltonian(s, stage, small, temporaries):
    (where_ref,) = small
    (post,) = temporaries
    left, right, left_rows, right_rows = stage.results
    own_ref, outer_ref = stage.need(0), stage.need(1)
    blocks, block = own_ref.shape[0], own_ref.shape[1]
    post[...] = post_matrix(s)
    row, column = iotas(block, s.extent)
    for b in range(blocks):
        spread = column - row
        to_own = mask_to(spread == b * block)
        to_far = mask_to(spread == where_ref[b] * block)
        left[b * block : (b + 1) * block, :] = (dot(own_ref[b], to_own) + dot(outer_ref[b], to_far)).astype(BF16)
    row, column = iotas(s.extent, s.extent)
    same = mask_to(row == column)
    for b in row_blocks(s.extent):
        rows = slice(b, b + 128)
        right[rows, :] = dot(same[rows, :], left[...], ((1,), (1,))).astype(BF16)
        left_rows[rows, :] = dot(post[rows, :], left[...]).astype(BF16)
        right_rows[rows, :] = dot(post[rows, :], left[...], ((1,), (1,))).astype(BF16)
    for index in range(4):
        stage.send(index)


def even_weights(s, stage, small, temporaries):
    real_ref, imag_ref, rate_ref = small
    wa_s, wb_s, wa_t, wb_t, damp = stage.results
    columns_in, index_ref, mirror_ref, couplings_ref = [stage.need(k) for k in range(4)]
    me = lax.axis_index("aux") * s.rows + lax.axis_index("row")
    depth, wide = 2 * s.tile, MODES * s.tile
    row, column = iotas(s.auxes, wide)
    by_lane = mask_to(column % s.auxes == row)

    def spread(table):
        return dot(table.astype(F32).astype(BF16), by_lane, ((0,), (0,)))

    row, lane = iotas(s.extent, MODES)
    gather = mask_to(row == lane * s.band + me)
    row, lane = iotas(s.auxes, s.auxes * s.local)
    wanted = mask_to(lane == row * s.local)
    pieces = [columns_in[a // s.per_device * s.rows + a % s.per_device] for a in range(s.auxes)]
    counts = spread(dot(wanted, dot(jnp.concatenate(pieces, axis=0), gather).astype(BF16)))
    index, mirror = spread(index_ref[...]), spread(mirror_ref[...])
    lane_mode = lax.broadcasted_iota(jnp.int32, (1, wide), 1) // s.tile

    def of_mode(values):
        out = values[0]
        for k in range(1, MODES):
            out = jnp.where(lane_mode == k, values[k], out)
        return out

    take = lambda table, first: of_mode([table[first + k : first + k + 1, :] for k in range(MODES)])
    ups, downs = take(index, 0), take(index, MODES)
    up_kinds, down_kinds = take(mirror, 0), take(mirror, MODES)
    real = of_mode([counts[k : k + 1, :] * real_ref[k] for k in range(MODES)])
    imag = of_mode([counts[k : k + 1, :] * imag_ref[k] for k in range(MODES)])
    rates = counts[0:1, :] * rate_ref[0]
    for k in range(1, MODES):
        rates = rates + counts[k : k + 1, :] * rate_ref[k]
    damp[...] = rates

    row, column = iotas(s.extent, s.lanes)
    pick = (row % s.devices == me) & (row // s.devices == column // s.za)
    local_q = lax.dot_general(
        couplings_ref[...],
        pick.astype(F32),
        (((1,), (0,)), ((), ())),
        precision=lax.Precision.HIGHEST,
        preferred_element_type=F32,
    )

    row, column = iotas(depth, wide)
    same = row // s.za % s.fold == column // s.za % s.fold
    source, kind = (row % s.auxes).astype(F32), (row // s.tile).astype(F32)
    from_imag, to_imag = row // s.auxes % 2, column // s.auxes % 2
    up = same & (ups == source) & (up_kinds == kind)
    down = same & (downs == source) & (down_kinds == kind)
    along = jnp.where(up, 1.0, 0.0) + jnp.where(down, real, 0.0)
    cross = jnp.where(down, imag, 0.0)
    along = jnp.where(from_imag == 1, along, -along)
    flip = jnp.where((from_imag == 1) & (row // s.tile == 1), -1.0, 1.0)
    by_row = flip * jnp.where(from_imag == to_imag, cross, along)
    by_column = flip * jnp.where(from_imag == to_imag, cross, -along)

    def pieces(value):
        high = value.astype(BF16)
        return high, (value - high.astype(F32)).astype(BF16)

    for near, far, wa, wb in ((by_row, by_column, wa_s, wb_s), (by_column, by_row, wa_t, wb_t)):
        wb[:depth, :], wb[depth:, :] = pieces(far)
        for th in range(s.tiles):
            lanes = slice(th * s.tile, (th + 1) * s.tile)
            total = local_q[0:1, lanes] * near[:, : s.tile]
            for k in range(1, MODES):
                total = total + local_q[k : k + 1, lanes] * near[:, k * s.tile : (k + 1) * s.tile]
            wa[th, :depth, :], wa[th, depth:, :] = pieces(total)
    for index in range(5):
        stage.send(index)


def even_body(
    s,
    density,
    couplings,
    weight_real,
    weight_imag,
    mode_rates,
    tier_counts,
    link_index,
    link_mirror,
    block_diagonal,
    block_outer,
    block_column,
):
    planes, per_device, band, extent = density.shape
    cube = 2 * extent * extent * s.lanes
    state = shape(extent, s.lanes, dtype=BF16)
    full = shape(extent, s.lanes)
    pair = (shape(s.devices, 2, s.local, s.lanes, dtype=BF16), 2)
    held = pltpu.VMEM((extent, s.lanes), F32)
    held_b = pltpu.VMEM((extent, s.lanes), BF16)

    def exchange(message):
        return lax.all_to_all(message, BOTH, split_axis=0, concat_axis=0, tiled=True)

    blocks = density.reshape(1, planes * per_device, band, extent)
    message = run_staged(
        functools.partial(even_start, s),
        [pair],
        [(blocks, v) for v in range(planes * per_device)] + [tier_counts],
        temporaries=[held_b],
        flops=2 * cube,
    )[0]
    got = exchange(message)

    left, right, left_rows, right_rows = run_staged(
        functools.partial(even_hamiltonian, s),
        [state] * 4,
        [block_diagonal, block_outer],
        temporaries=[held_b],
        scalars=[block_column],
        flops=4 * cube,
    )
    q_first = couplings.T

    k, n = iotas(s.lanes, s.lanes)
    parts = band // s.devices
    row_lanes = (
        n
        == (k // s.local % s.rows * parts + k % parts) * s.za
        + k // (parts * per_device) % planes * s.auxes
        + k // (s.local * s.rows) * per_device
        + k // parts % per_device
    ).astype(BF16)
    column_lanes = (
        n
        == k % s.local * s.za
        + k // (s.local * s.groups * per_device) * s.auxes
        + k // s.local % s.groups * per_device
        + k // (s.local * s.groups) % per_device
    ).astype(BF16)

    k, n = iotas(s.tile, s.tile)
    sign = jnp.where(n // s.auxes % 2 == 0, 1.0, -1.0)
    unit = jnp.where(k // s.za * s.za + (k + s.auxes) % s.za == n, sign, 0.0).astype(BF16)
    wide, size = s.fold * s.tile, max(256, 16 * s.local)
    swap, order = pltpu.VMEM((wide, wide), BF16), pltpu.VMEM((size, size), BF16)

    message, s_now, t_now = run_staged(
        functools.partial(even_take, s),
        [pair, state, state],
        [row_lanes, right_rows, column_lanes, left_rows],
        front=[(got, 0), (got, 1)],
        flops=4 * cube,
    )
    wa = shape(s.tiles, 4 * s.tile, s.tile, dtype=BF16)
    wb = shape(4 * s.tile, MODES * s.tile, dtype=BF16)
    wa_s, wb_s, wa_t, wb_t, damp = run_staged(
        functools.partial(even_weights, s),
        [wa, wb, wa, wb, shape(1, s.lanes)],
        [(got, 1), link_index, link_mirror, couplings],
        scalars=[weight_real, weight_imag, mode_rates],
        flops=cube,
    )
    tables = [unit, damp, q_first, right, wa_s, wb_s, left, wa_t, wb_t]
    shares = [STEP / 6.0, STEP / 3.0, STEP / 3.0, STEP / 6.0]
    steps = [0.25, 0.25, 0.5]
    got = exchange(message)
    ks, kt = run_staged(
        functools.partial(even_first_slope, s),
        [full, full],
        [s_now, t_now] + tables,
        temporaries=[held_b],
        flops=12 * cube,
    )
    total = None
    for section in range(2):
        step = steps[section]
        message = run_staged(
            functools.partial(even_next, s, step),
            [pair],
            [ks, s_now, right_rows, (got, 1), kt, t_now, left_rows],
            temporaries=[held_b, held_b, order, swap],
            front=[(got, 0)],
            lead=3,
            flops=5 * cube,
        )[0]
        arrived, got = got, exchange(message)
        ks, kt, total = run_staged(
            functools.partial(even_slope, s, step, shares[section] / step, total is not None),
            [full, full, full],
            [ks, s_now, kt, t_now] + tables + ([] if total is None else [total]),
            temporaries=[held_b, held_b, held_b, held, held, order, swap],
            front=[(arrived, 0), (arrived, 1)],
            flops=15 * cube,
        )
    message = run_staged(
        functools.partial(even_last, s, steps[2], shares[2] / steps[2], shares[3]),
        [pair],
        [kt, t_now, unit, left, column_lanes, ks, s_now, total]
        + [damp, q_first, right, wa_s, wb_s, row_lanes],
        temporaries=[held, held_b, held_b, held_b, held_b, order, swap],
        front=[(got, 1), (got, 0)],
        lead=4,
        flops=12 * cube,
    )[0]
    got = exchange(message)
    evolved = run_staged(
        functools.partial(even_finish, s),
        [(shape(1, planes * per_device, band, extent), planes * per_device)],
        [(blocks, v) for v in range(planes * per_device)],
        temporaries=[held_b],
        front=[(got, 0), (got, 1)],
        flops=2 * cube,
    )[0]
    return evolved.reshape(density.shape)


def body(density, *others):
    planes, per_device, band, extent = density.shape
    s = Sizes(lax.axis_size("aux"), lax.axis_size("row"), per_device, band, extent)
    even = band % s.devices == 0 and s.local % 16 == 0 and LANES % s.za == 0
    even = even and s.lanes == extent and planes * per_device * band == extent
    even = even and planes * per_device == MODES and per_device <= s.rows and s.devices <= s.band
    if even:
        return even_body(s, density, *others)
    return general_body(density, *others)


def solution(mesh):
    return jax.shard_map(
        body,
        mesh=mesh,
        in_specs=(
            P(None, "aux", "row", None),
            P(),
            P(),
            P(),
            P(),
            P("aux", None),
            P(),
            P(),
            P(),
            P(),
            P(),
        ),
        out_specs=P(None, "aux", "row", None),
        check_vma=False,
    )
```

```python
import functools

import jax
import jax.numpy as jnp
from jax import lax
from jax.experimental import pallas as pl
from jax.experimental.pallas import tpu as pltpu
from jax.sharding import PartitionSpec as P

MODES = 4
LINKS = 8
LANES = 128
STEP = 0.5
BOTH = ("aux", "row")
GRANT = 52 << 20
MOST = 60 << 20
ROWS = 512

F32 = jnp.float32
BF16 = jnp.bfloat16


class Sizes:
    def __init__(self, groups, rows, per_device, band, extent):
        self.groups, self.rows, self.per_device = groups, rows, per_device
        self.band, self.extent = band, extent
        self.devices = groups * rows
        self.local = band // groups
        self.auxes = per_device * groups
        self.za = 2 * self.auxes
        self.lanes = self.local * self.za
        self.fold = max(1, LANES // self.za)
        self.tile = self.fold * self.za
        self.tiles = self.local // self.fold
        self.joined = self.local % 16 == 0


def dot(a, b, dims=((1,), (0,))):
    return lax.dot_general(a, b, (dims, ((), ())), preferred_element_type=F32)


def run(kernel, outs, args, scratch=(), flops=0, scalars=()):
    spec = pl.BlockSpec(memory_space=pltpu.VMEM)
    flat = pl.BlockSpec(memory_space=pltpu.SMEM)
    moved = sum(a.size * a.dtype.itemsize for a in args)
    moved += sum(o.size * o.dtype.itemsize for o in outs)
    return pl.pallas_call(
        kernel,
        out_shape=list(outs),
        in_specs=[flat if n in scalars else spec for n in range(len(args))],
        out_specs=[spec] * len(outs),
        scratch_shapes=list(scratch),
        compiler_params=pltpu.CompilerParams(vmem_limit_bytes=16 << 20),
        cost_estimate=pl.CostEstimate(flops=flops, bytes_accessed=moved, transcendentals=0),
    )(*args)


def shape(*dims, dtype=F32):
    return jax.ShapeDtypeStruct(dims, dtype)


def one_hot(target, count):
    return (target[:, None] == jnp.arange(count, dtype=jnp.int32)[None, :]).astype(BF16)


def matrix_index(s, index, device):
    group, row = device // s.rows, device % s.rows
    return row * s.band + index * s.groups + group


def row_blocks(extent, size=128):
    return range(0, extent, size)


def send_start_kernel(d_ref, pick_rows, pick_cols, out_ref):
    planes, number, band, extent = d_ref.shape
    flat = d_ref[...].reshape(planes * number * band, extent).astype(BF16)
    for b in row_blocks(flat.shape[0]):
        moved = dot(pick_rows[b : b + 128, :], flat).astype(BF16)
        out_ref[b : b + 128, :] = dot(moved, pick_cols[...]).astype(BF16)


def take_start_kernel(got_ref, pick_lanes, message_rows, s_ref, m_ref):
    for b in row_blocks(got_ref.shape[1]):
        s_ref[b : b + 128, :] = dot(
            got_ref[:, b : b + 128], pick_lanes[...], ((0,), (0,))
        ).astype(BF16)
    for b in row_blocks(m_ref.shape[0]):
        m_ref[b : b + 128, :] = dot(message_rows[b : b + 128, :], s_ref[...]).astype(BF16)


def turn(s, load, order, swap, put):
    size = order.shape[0]
    span = size // s.local
    blocks = s.extent // size
    parts = []
    for block in range(blocks):
        moved = dot(order[...], load(block * size, size))
        for ih in range(s.tiles):
            for jh in range(s.tiles):
                lanes = slice(jh * s.tile, (jh + 1) * s.tile)
                pieces = [
                    moved[(ih * s.fold + f) * span : (ih * s.fold + f + 1) * span, lanes]
                    for f in range(s.fold)
                ]
                parts.append(jnp.concatenate(pieces, axis=1) if s.fold > 1 else pieces[0])
    turned = dot(jnp.concatenate(parts, axis=0).astype(BF16), swap[...])
    for block in range(blocks):
        for ih in range(s.tiles):
            for jh in range(s.tiles):
                start = ((block * s.tiles + ih) * s.tiles + jh) * span
                for f in range(s.fold):
                    first = (jh * s.fold + f) * s.devices + block * span
                    put(
                        slice(first, first + span),
                        slice(ih * s.tile, (ih + 1) * s.tile),
                        turned[start : start + span, f * s.tile : (f + 1) * s.tile],
                    )


def take_columns_kernel(s, got_ref, order, swap, first_rows, left_rows, s_ref, t_ref, *message):
    def put(rows, lanes, value):
        t_ref[rows, lanes] = value.astype(BF16)

    turn(s, lambda start, size: got_ref[start : start + size, :], order, swap, put)
    write_messages(s, first_rows, left_rows, s_ref, t_ref, message)


def write_messages(s, right_rows, left_rows, s_ref, t_ref, message):
    pairs = ((left_rows, t_ref), (right_rows, s_ref))
    if not s.joined and len(message) == 1:
        pairs = pairs[:1]
    both = s.joined and message[0].shape[0] == 2 * s.extent
    for part, (matrix, state) in enumerate(pairs):
        if s.joined and part == 1 and not both:
            continue
        for b in row_blocks(s.extent):
            product = dot(matrix[b : b + 128, :], state[...]).astype(BF16)
            if not s.joined:
                message[part][b : b + 128, :] = product
            elif not both:
                message[0][b : b + 128, :] = product
            else:
                for k in range(128 // s.local):
                    start = ((b // s.local + k) * 2 + part) * s.local
                    message[0][start : start + s.local, :] = product[
                        k * s.local : (k + 1) * s.local, :
                    ]


def slope_kernel(
    s, with_columns, s_ref, t_ref, ys_ref, yt_ref, damp, q_ref, right, left, unit, wa_s, wb_s, wa_t, wb_t, *rest
):
    if with_columns:
        ks_ref, kt_ref, turned = rest
    else:
        ks_ref, turned = rest

    def one(direct, mirror, y_ref, h, wa, wb, out_ref, sign):
        for th in range(s.tiles):
            lanes = slice(th * s.tile, (th + 1) * s.tile)
            turned[:, lanes] = dot(direct[:, lanes], unit[...]).astype(BF16)
        for b in row_blocks(s.extent):
            rows = slice(b, b + 128)
            whole = dot(h[rows, :], turned[...])
            for th in range(s.tiles):
                lanes = slice(th * s.tile, (th + 1) * s.tile)
                source = jnp.concatenate([direct[rows, lanes], mirror[rows, lanes]], axis=1)
                source = jnp.concatenate([source, source], axis=1)
                total = dot(source, wa[th]) - damp[:, lanes] * y_ref[rows, lanes].astype(F32)
                total = total + sign * whole[:, lanes]
                fields = dot(source, wb[...])
                for k in range(MODES):
                    total = total + q_ref[rows, k : k + 1] * fields[:, k * s.tile : (k + 1) * s.tile]
                out_ref[rows, lanes] = total

    one(s_ref, t_ref, ys_ref, right, wa_s, wb_s, ks_ref, -1.0)
    if with_columns:
        one(t_ref, s_ref, yt_ref, left, wa_t, wb_t, kt_ref, 1.0)


def part_loader(s, refs, part):
    def load(start, size):
        if not s.joined:
            return refs[part][start : start + size, :]
        step = s.local
        pieces = []
        for first in range(start, start + size, step):
            at = (first // step * 2 + part) * step
            pieces.append(refs[0][at : at + step, :])
        return jnp.concatenate(pieces, axis=0)

    return load


def next_kernel(s, weight, step, has_total, both, got_count, *refs):
    got = refs[:got_count]
    refs = refs[got_count:]
    order, swap, right_rows, left_rows, ks_ref, kt_ref, ds_ref, dt_ref = refs[:8]
    refs = refs[8:]
    total_in = None
    if has_total:
        total_in, refs = refs[0], refs[1:]
    s_ref, t_ref, ys_ref, yt_ref, total_ref = refs[:5]
    message, arrived = refs[5:-1], refs[-1]

    def put(rows, lanes, value):
        arrived[rows, lanes] = value

    for part in range(2):
        turn(s, part_loader(s, got, part), order, swap, put)
        for b in row_blocks(s.extent, 64):
            rows = slice(b, b + 64)
            if part == 0:
                slope = ks_ref[rows, :] + arrived[rows, :]
                grown = weight * slope
                total_ref[rows, :] = total_in[rows, :] + grown if has_total else grown
                state = ds_ref[rows, :].astype(F32) + step * slope
                ys_ref[rows, :] = state
                s_ref[rows, :] = state.astype(BF16)
            else:
                slope = kt_ref[rows, :] - arrived[rows, :]
                state = dt_ref[rows, :].astype(F32) + step * slope
                yt_ref[rows, :] = state
                t_ref[rows, :] = state.astype(BF16)
    if message:
        write_messages(s, right_rows, left_rows, s_ref, t_ref, message)


def last_kernel(s, weight, got_ref, order, swap, ks_ref, total_in, pick_lanes, out_ref, arrived, grown):
    def put(rows, lanes, value):
        arrived[rows, lanes] = value

    turn(s, lambda start, size: got_ref[start : start + size, :], order, swap, put)
    for b in row_blocks(s.extent, 64):
        rows = slice(b, b + 64)
        change = total_in[rows, :] + weight * (ks_ref[rows, :] + arrived[rows, :])
        grown[rows, :] = change.astype(BF16)
    for b in row_blocks(s.lanes):
        out_ref[b : b + 128, :] = dot(
            pick_lanes[b : b + 128, :], grown[...], ((1,), (1,))
        ).astype(BF16)


def finish_kernel(got_ref, place_rows, place_cols, d_ref, out_ref):
    planes, number, band, extent = d_ref.shape
    for z in range(planes):
        for n in range(number):
            at = (z * number + n) * band
            for b in range(0, band, min(band, 128)):
                size = min(band, 128)
                rows = slice(at + b, at + b + size)
                moved = dot(place_rows[rows, :], got_ref[...]).astype(BF16)
                out_ref[z, n, b : b + size, :] = d_ref[z, n, b : b + size, :] + dot(
                    moved, place_cols[...]
                )


def link_matrices(s, counts, weight_real, weight_imag, link_index, link_mirror):
    ones = jnp.ones_like(counts)
    real = jnp.stack([ones, counts * weight_real[None, :]], 1)
    imag = jnp.stack([jnp.zeros_like(counts), counts * weight_imag[None, :]], 1)
    index = link_index.reshape(s.auxes, 2, MODES)
    mirror = link_mirror.reshape(s.auxes, 2, MODES)
    source = jnp.arange(s.auxes, dtype=jnp.int32)
    hit = index[None] == source[:, None, None, None]
    kinds = jnp.stack([hit & (mirror[None] == 0), hit & (mirror[None] == 1)]).astype(F32)
    along = jnp.sum(kinds * real, 3)
    cross = jnp.sum(kinds * imag, 3)
    along, cross = (jnp.transpose(m, (0, 3, 1, 2)) for m in (along, cross))
    flip = jnp.array([1.0, -1.0], F32).reshape(2, 1, 1, 1)

    def build(sign):
        upper = jnp.concatenate([cross, -sign * along], 3)
        lower = jnp.concatenate([sign * along, cross], 3) * flip
        return jnp.concatenate([upper, lower], 2)

    return build(1.0), build(-1.0)


def two_pieces(weights, axis):
    high = lax.reduce_precision(weights, 8, 7)
    low = weights - high
    return jnp.concatenate([high.astype(BF16), low.astype(BF16)], axis)


def coupling_weights(s, by_local, by_first, local_q):
    eye = jnp.eye(s.fold, dtype=F32)
    near = jnp.einsum("ki,xkuv->ixuv", local_q, by_local, precision=lax.Precision.HIGHEST)
    near = near.reshape(s.tiles, s.fold, 2, s.za, s.za)
    near = jnp.transpose(near, (0, 2, 1, 3, 4))[:, :, :, :, None, :] * eye[None, None, :, None, :, None]
    near = near.reshape(s.tiles, 2 * s.tile, s.tile)
    far = jnp.transpose(by_first, (0, 2, 1, 3))[:, None, :, :, None, :] * eye[None, :, None, None, :, None]
    far = far.reshape(2 * s.tile, MODES * s.tile)
    return two_pieces(near, 1), two_pieces(far, 0)


def general_body(
    density,
    couplings,
    weight_real,
    weight_imag,
    mode_rates,
    tier_counts,
    link_index,
    link_mirror,
    block_diagonal,
    block_outer,
    block_column,
):
    planes, per_device, band, extent = density.shape
    s = Sizes(lax.axis_size("aux"), lax.axis_size("row"), per_device, band, extent)
    blocks, block = block_diagonal.shape[0], block_diagonal.shape[1]
    group, row = lax.axis_index("aux"), lax.axis_index("row")
    device = group * s.rows + row
    cube = 2 * extent * extent * s.lanes

    number = jnp.arange(extent, dtype=jnp.int32)
    first_to_matrix = matrix_index(s, number // s.devices, number % s.devices)
    posted_to_matrix = matrix_index(s, number % s.local, number // s.local)
    posted_to_first = number % s.local * s.devices + number // s.local

    wide = jnp.arange(s.lanes, dtype=jnp.int32)
    sub = planes * per_device * s.local
    start_source = wide % sub * s.groups + wide // sub
    pick_rows = one_hot(start_source, s.lanes)
    pick_cols = one_hot(first_to_matrix, extent).T
    lane_of = (
        wide % s.local * s.za
        + wide // (per_device * s.local) % planes * s.auxes
        + wide // sub * per_device
        + wide // s.local % per_device
    )
    pick_lanes = one_hot(lane_of, s.lanes)
    message_rows = one_hot(posted_to_first, extent)
    start_message = run(
        send_start_kernel,
        [shape(s.lanes, extent, dtype=BF16)],
        [density, pick_rows, pick_cols],
        flops=2 * cube,
    )[0]
    start_got = lax.all_to_all(
        start_message.reshape(s.groups, sub, extent), "aux", split_axis=0, concat_axis=0, tiled=True
    ).reshape(s.lanes, extent)

    selector = block_column[:, None] == jnp.arange(blocks, dtype=jnp.int32)[None, :]
    own = jnp.eye(blocks, dtype=F32)
    whole_h = (
        own[:, None, :, None] * block_diagonal.astype(F32)[:, :, None, :]
        + selector.astype(F32)[:, None, :, None] * block_outer.astype(F32)[:, :, None, :]
    ).reshape(extent, extent).astype(BF16)
    first_h = one_hot(first_to_matrix, extent)
    left = jnp.dot(
        jnp.dot(first_h, whole_h, preferred_element_type=BF16), first_h.T, preferred_element_type=BF16
    )
    right = left.T
    left_rows = jnp.dot(message_rows, left, preferred_element_type=BF16)
    right_rows = jnp.dot(message_rows, right, preferred_element_type=BF16)

    counts = lax.all_gather(tier_counts, "aux", axis=0, tiled=True).astype(F32)
    damping = jnp.sum(counts * mode_rates[None, :], axis=1)
    damp = jnp.tile(damping, (planes * s.local,))[None, :]
    q_first = jnp.dot(
        couplings, first_h.T.astype(F32), precision=lax.Precision.HIGHEST
    ).T
    local_pick = (matrix_index(s, jnp.arange(s.local, dtype=jnp.int32), device)[None, :] == number[:, None])
    local_q = jnp.dot(couplings, local_pick.astype(F32), precision=lax.Precision.HIGHEST)
    by_row, by_column = link_matrices(s, counts, weight_real, weight_imag, link_index, link_mirror)
    wa_s, wb_s = coupling_weights(s, by_row, by_column, local_q)
    wa_t, wb_t = coupling_weights(s, by_column, by_row, local_q)

    lane = jnp.arange(s.za, dtype=jnp.int32)
    unit = jnp.where(
        lane[:, None] == (lane[None, :] + s.auxes) % s.za,
        jnp.where(lane[None, :] < s.auxes, 1.0, -1.0),
        0.0,
    )
    eye_fold = jnp.eye(s.fold, dtype=F32)
    unit_tile = (eye_fold[:, None, :, None] * unit[None, :, None, :]).reshape(s.tile, s.tile).astype(BF16)
    swap = (
        eye_fold[:, None, None, None, :, None]
        * eye_fold[None, :, None, :, None, None]
        * unit[None, None, :, None, None, :]
    ).reshape(s.fold * s.tile, s.fold * s.tile).astype(BF16)
    keep = (
        eye_fold[:, None, None, None, :, None]
        * eye_fold[None, :, None, :, None, None]
        * jnp.eye(s.za, dtype=F32)[None, None, :, None, None, :]
    ).reshape(s.fold * s.tile, s.fold * s.tile).astype(BF16)
    size = min(extent, max(256, 16 * s.local))
    span = size // s.local
    at = jnp.arange(size, dtype=jnp.int32)
    order = one_hot(at % span * s.local + at // span, size)

    state = shape(extent, s.lanes, dtype=BF16)
    full = shape(extent, s.lanes)
    held = pltpu.VMEM((extent, s.lanes), F32)
    held_b = pltpu.VMEM((extent, s.lanes), BF16)

    def exchange(messages):
        parts = [m.reshape(s.devices, -1, s.lanes) for m in messages]
        sent = parts[0] if len(parts) == 1 else jnp.concatenate(parts, 1)
        got = lax.all_to_all(sent, BOTH, split_axis=0, concat_axis=0, tiled=True)
        if len(parts) == 1:
            return [got.reshape(-1, s.lanes)]
        height = s.local
        return [got[:, p * height : (p + 1) * height].reshape(-1, s.lanes) for p in range(2)]

    if s.joined:
        pair = [shape(2 * extent, s.lanes, dtype=BF16)]
    else:
        pair = [state, state]

    s_now, posted = run(
        take_start_kernel, [state, state], [start_got, pick_lanes, message_rows], flops=2 * cube
    )
    got = exchange([posted])
    t_now, *messages = run(
        functools.partial(take_columns_kernel, s),
        [state] + pair,
        [got[0], order, keep, right_rows, left_rows, s_now],
        flops=4 * cube,
    )
    start_s, start_t = s_now, t_now
    ys, yt = s_now, t_now
    total = None
    shares = [STEP / 6.0, STEP / 3.0, STEP / 3.0, STEP / 6.0]
    steps = [0.25, 0.25, 0.5]
    for section in range(4):
        got = exchange(messages)
        columns = section < 3
        slopes = run(
            functools.partial(slope_kernel, s, columns),
            [full, full] if columns else [full],
            [s_now, t_now, ys, yt, damp, q_first, right, left, unit_tile, wa_s, wb_s, wa_t, wb_t],
            scratch=[held_b],
            flops=(12 if columns else 6) * cube,
        )
        if columns:
            args = list(got) + [order, swap, right_rows, left_rows, *slopes, start_s, start_t]
            if total is not None:
                args.append(total)
            outs = [state, state, full, full, full]
            outs += pair if section < 2 else [state]
            s_now, t_now, ys, yt, total, *messages = run(
                functools.partial(
                    next_kernel, s, shares[section], steps[section], total is not None, section < 2, len(got)
                ),
                outs,
                args,
                scratch=[held],
                flops=6 * cube,
            )
    change = run(
        functools.partial(last_kernel, s, shares[3]),
        [shape(s.lanes, extent, dtype=BF16)],
        [got[0], order, swap, slopes[0], total, pick_lanes],
        scratch=[held, held_b],
        flops=3 * cube,
    )[0]
    back = lax.all_to_all(
        change.reshape(s.groups, sub, extent), "aux", split_axis=0, concat_axis=0, tiled=True
    ).reshape(s.lanes, extent)
    return run(
        finish_kernel,
        [shape(planes, per_device, band, extent)],
        [back, pick_rows.T, pick_cols.T, density],
        flops=2 * cube,
    )[0]


def iotas(rows, columns):
    return (
        lax.broadcasted_iota(jnp.int32, (rows, columns), 0),
        lax.broadcasted_iota(jnp.int32, (rows, columns), 1),
    )


def mask_to(value):
    return value.astype(F32).astype(BF16)


def post_matrix(s):
    row, column = iotas(s.extent, s.extent)
    return mask_to(column == row % s.local * s.devices + row // s.local)


class Stage:
    def __init__(self, sources, buffers, targets, results, semaphores, offset, lead):
        self.buffers, self.results, self.targets = buffers, results, targets
        self.semaphores, self.next, self.offset = semaphores, 0, offset
        self.sources, self.lead = sources, lead
        self.coming = [self.copy(a, b) for a, b in zip(sources[:lead], buffers)]
        self.going = []

    def copy(self, source, target):
        made = pltpu.make_async_copy(source, target, self.semaphores.at[self.next])
        self.next += 1
        made.start()
        return made

    def front(self, index):
        return self.need(index - self.offset)

    def need(self, index):
        index += self.offset
        if index >= len(self.coming):
            self.start_rest()
        if self.coming[index] is not None:
            self.coming[index].wait()
            self.coming[index] = None
        return self.buffers[index]

    def start_rest(self):
        known = len(self.coming)
        self.coming += [self.copy(a, b) for a, b in zip(self.sources[known:], self.buffers[known:])]

    def send(self, index):
        self.going.append(self.copy(self.results[index], self.targets[index]))

    def finish(self):
        for made in self.going:
            made.wait()


def run_staged(body, outs, args, temporaries=(), scalars=(), front=(), lead=None, grant=GRANT, flops=0):
    arrays, views = [], []
    for arg in [*front, *args]:
        array, part = arg if isinstance(arg, tuple) else (arg, None)
        if not any(array is a for a in arrays):
            arrays.append(array)
        views.append(([array is a for a in arrays].index(True), part))
    shapes, places = [], []
    for out in outs:
        if isinstance(out, tuple):
            for part in range(out[1]):
                places.append((len(shapes), part))
            shapes.append(out[0])
        else:
            places.append((len(shapes), None))
            shapes.append(out)
    tall = lambda x, part: x.shape if part is None else x.shape[:1] + x.shape[2:]
    buffers = [pltpu.VMEM(tall(arrays[k], part), arrays[k].dtype) for k, part in views]
    results = [pltpu.VMEM(tall(shapes[k], part), shapes[k].dtype) for k, part in places]
    count = len(buffers) + len(results)

    def kernel(*refs):
        small, refs = refs[: len(scalars)], refs[len(scalars) :]
        source, refs = refs[: len(arrays)], refs[len(arrays) :]
        target, refs = refs[: len(shapes)], refs[len(shapes) :]
        own, refs = refs[: len(buffers)], refs[len(buffers) :]
        made, refs = refs[: len(results)], refs[len(results) :]
        pick = lambda ref, part: ref if part is None else ref.at[:, part]
        stage = Stage(
            [pick(source[k], part) for k, part in views],
            own,
            [pick(target[k], part) for k, part in places],
            made,
            refs[-1],
            len(front),
            len(views) if lead is None else lead,
        )
        body(stage, small, refs[:-1])
        stage.finish()

    moved = sum(a.size * a.dtype.itemsize for a in arrays)
    moved += sum(o.size * o.dtype.itemsize for o in shapes)
    far = pl.BlockSpec(memory_space=pltpu.HBM)
    return pl.pallas_call(
        kernel,
        out_shape=shapes,
        in_specs=[pl.BlockSpec(memory_space=pltpu.SMEM)] * len(scalars) + [far] * len(arrays),
        out_specs=[far] * len(shapes),
        scratch_shapes=buffers + results + list(temporaries) + [pltpu.SemaphoreType.DMA((count,))],
        compiler_params=pltpu.CompilerParams(vmem_limit_bytes=grant),
        cost_estimate=pl.CostEstimate(flops=flops, bytes_accessed=moved, transcendentals=0),
    )(*scalars, *arrays)


def fill(s, result, first, value, lanes=slice(None)):
    count = value.shape[0] // s.local
    device = first // s.local
    result[device : device + count, :, lanes] = value.reshape(count, s.local, value.shape[1])


def flat_rows(ref, rows, lanes=slice(None)):
    piece = ref[rows, :, lanes]
    return piece.reshape(piece.shape[0] * piece.shape[1], piece.shape[2])


def even_start(s, stage, small, temporaries):
    (post,) = temporaries
    post[...] = post_matrix(s)
    blocks = s.extent // s.band
    which = lax.axis_index("row") % s.per_device
    flats = [stage.need(v)[...].reshape(s.band, s.extent).astype(BF16) for v in range(blocks)]
    row, lane = iotas(ROWS, s.band)
    counts = stage.need(blocks)[...].astype(F32)
    mine = counts[0:1, :]
    for n in range(1, s.per_device):
        mine = jnp.where(which == n, counts[n : n + 1, :], mine)
    for v in range(blocks):
        count = mine[:, v : v + 1]
        for b in row_blocks(s.extent, ROWS):
            value = dot(post[b : b + ROWS, :], flats[v], ((1,), (1,)))
            own = (row % s.local == 0) & (lane == (row + b) // s.local)
            value = jnp.where(own, count, value).astype(BF16)
            fill(s, stage.results[1], b, value, slice(v * s.band, (v + 1) * s.band))
    stage.send(1)
    flat = jnp.concatenate(flats, axis=0)
    for b in row_blocks(s.extent, ROWS):
        fill(s, stage.results[0], b, dot(post[b : b + ROWS, :], flat).astype(BF16))
    stage.send(0)


def send_products(s, stage, matrix, state_ref, index):
    for b in row_blocks(s.extent, ROWS):
        fill(s, stage.results[index], b, dot(matrix[b : b + ROWS, :], state_ref[...]).astype(BF16))
    stage.send(index)


def even_take(s, stage, small, temporaries):
    s_ref, t_ref = stage.results[2], stage.results[3]
    me = lax.axis_index("aux") * s.rows + lax.axis_index("row")
    everyone = slice(0, s.devices)
    rows_in, row_lanes = stage.front(0), stage.need(0)
    for b in row_blocks(s.extent, ROWS):
        s_ref[b : b + ROWS, :] = dot(
            flat_rows(rows_in, everyone, slice(b, b + ROWS)), row_lanes[...], ((0,), (0,))
        ).astype(BF16)
    stage.send(2)
    send_products(s, stage, stage.need(1), s_ref, 1)
    columns_in, column_lanes = stage.front(1), stage.need(2)
    blocks = s.extent // s.band
    parts = s.band // s.devices
    row, lane = iotas(s.devices, s.tile)
    mine = (row == me) & (lane < s.za)
    for q in range(s.rows):
        pieces = []
        for v in range(blocks):
            for g in range(s.groups):
                pieces.append(columns_in[g * s.rows + q, :, v * s.band : (v + 1) * s.band])
        t_ref[q * s.band : (q + 1) * s.band, :] = dot(
            jnp.concatenate(pieces, axis=0), column_lanes[...], ((0,), (0,))
        ).astype(BF16)
        rows = slice(q * s.band, q * s.band + s.devices)
        first = q * parts * s.za
        kept = s_ref[: s.devices, first : first + s.tile].astype(F32)
        t_ref[rows, : s.tile] = jnp.where(mine, kept, t_ref[rows, : s.tile].astype(F32)).astype(BF16)
    stage.send(3)
    send_products(s, stage, stage.need(3), t_ref, 0)


def turn_matrices(s, order, swap):
    size = order.shape[0]
    span = size // s.local
    k, n = lax.broadcasted_iota(jnp.int32, (size, 1), 0), lax.broadcasted_iota(jnp.int32, (1, size), 1)
    order[...] = mask_to(n == k % span * s.local + k // span)
    wide = s.fold * s.tile
    k, n = lax.broadcasted_iota(jnp.int32, (wide, 1), 0), lax.broadcasted_iota(jnp.int32, (1, wide), 1)
    sign = jnp.where(n // s.auxes % 2 == 0, 1.0, -1.0)
    there = (k // s.za % s.fold * s.fold + k // s.tile) * s.za + (k + s.auxes) % s.za
    swap[...] = jnp.where(there == n, sign, 0.0).astype(BF16)


def even_turn(s, got, order, swap, put):
    def load(start, size):
        return flat_rows(got, slice(start // s.local, (start + size) // s.local))

    turn(s, load, order, swap, put)


def updates(scale, base_ref, keep):
    def put(rows, lanes, value):
        keep(rows, lanes, base_ref[rows, lanes] + scale * value)

    return put


def even_next(s, step, stage, small, temporaries):
    s_ref, t_ref, order, swap = temporaries
    turn_matrices(s, order, swap)

    def keep_in(ref):
        def keep(rows, lanes, value):
            ref[rows, lanes] = value.astype(BF16)

        return keep

    got = stage.front(0)
    stage.start_rest()
    even_turn(s, got, order, swap, updates(step, stage.need(0), keep_in(s_ref)))
    send_products(s, stage, stage.need(1), s_ref, 1)
    got = stage.need(2)
    even_turn(s, got, order, swap, updates(-step, stage.need(3), keep_in(t_ref)))
    send_products(s, stage, stage.need(4), t_ref, 0)


def even_slope_part(s, direct, mirror, y_ref, h, unit, damp, q_ref, wa, wb, turned, sign, put):
    for th in range(s.tiles):
        lanes = slice(th * s.tile, (th + 1) * s.tile)
        turned[:, lanes] = dot(direct[:, lanes], unit[...]).astype(BF16)
    for b in row_blocks(s.extent, ROWS):
        rows = slice(b, b + ROWS)
        whole = dot(h[rows, :], turned[...])
        for th in range(s.tiles):
            lanes = slice(th * s.tile, (th + 1) * s.tile)
            source = jnp.concatenate([direct[rows, lanes], mirror[rows, lanes]], axis=1)
            source = jnp.concatenate([source, source], axis=1)
            total = dot(source, wa[th]) - damp[:, lanes] * y_ref[rows, lanes].astype(F32)
            total = total + sign * whole[:, lanes]
            fields = dot(source, wb[...])
            for k in range(MODES):
                total = total + q_ref[rows, k : k + 1] * fields[:, k * s.tile : (k + 1) * s.tile]
            put(rows, lanes, total)


def put_base(ref, start_ref, step):
    def put(rows, lanes, value):
        ref[rows, lanes] = start_ref[rows, lanes].astype(F32) + step * value

    return put


def even_first_slope(s, step, stage, small, temporaries):
    (turned,) = temporaries
    need = stage.need
    first, second = stage.results
    s_ref, t_ref, unit, damp, q_ref = need(0), need(1), need(2), need(3), need(4)
    put = put_base(first, s_ref, step)
    even_slope_part(s, s_ref, t_ref, s_ref, need(5), unit, damp, q_ref, need(6), need(7), turned, -1.0, put)
    stage.send(0)
    put = put_base(second, t_ref, step)
    even_slope_part(s, t_ref, s_ref, t_ref, need(8), unit, damp, q_ref, need(9), need(10), turned, 1.0, put)
    stage.send(1)


def even_slope(s, step, next_step, ratio, less, has_total, stage, small, temporaries):
    turned, s_ref, t_ref, ys_ref, yt_ref, order, swap = temporaries
    turn_matrices(s, order, swap)
    need = stage.need
    first, second, total_ref = stage.results

    def keep_in(ref, exact):
        def keep(rows, lanes, value):
            exact[rows, lanes] = value
            ref[rows, lanes] = value.astype(BF16)

        return keep

    even_turn(s, stage.front(0), order, swap, updates(step, need(0), keep_in(s_ref, ys_ref)))
    even_turn(s, stage.front(1), order, swap, updates(-step, need(1), keep_in(t_ref, yt_ref)))
    ds_ref, dt_ref = need(2), need(3)
    total_in = need(13) if has_total else None
    for b in row_blocks(s.extent, 64):
        rows = slice(b, b + 64)
        grown = ratio * ys_ref[rows, :] - (ratio + less) * ds_ref[rows, :].astype(F32)
        total_ref[rows, :] = total_in[rows, :] + grown if has_total else grown
    stage.send(2)
    unit, damp, q_ref = need(4), need(5), need(6)
    put = put_base(first, ds_ref, next_step)
    even_slope_part(s, s_ref, t_ref, ys_ref, need(7), unit, damp, q_ref, need(8), need(9), turned, -1.0, put)
    stage.send(0)
    put = put_base(second, dt_ref, next_step)
    even_slope_part(s, t_ref, s_ref, yt_ref, need(10), unit, damp, q_ref, need(11), need(12), turned, 1.0, put)
    stage.send(1)


def even_last(s, step, ratio, weight, stage, small, temporaries):
    ys_ref, s_ref, t_ref, grown, turned, order, swap = temporaries
    turn_matrices(s, order, swap)
    need = stage.need

    def keep_columns(rows, lanes, value):
        t_ref[rows, lanes] = value.astype(BF16)

    got = stage.front(0)
    stage.start_rest()
    even_turn(s, got, order, swap, updates(-step, need(0), keep_columns))
    unit, left, column_lanes = need(1), need(2), need(3)
    for th in range(s.tiles):
        lanes = slice(th * s.tile, (th + 1) * s.tile)
        turned[:, lanes] = dot(t_ref[:, lanes], unit[...]).astype(BF16)
    for b in row_blocks(s.extent, ROWS):
        rows = slice(b, b + ROWS)
        grown[rows, :] = (weight * dot(left[rows, :], turned[...])).astype(BF16)
    out = stage.results[1]
    for q in range(s.rows):
        value = dot(column_lanes[...], grown[q * s.band : (q + 1) * s.band, :], ((1,), (1,))).astype(BF16)
        for v in range(s.extent // s.band):
            for g in range(s.groups):
                at = (v * s.groups + g) * s.local
                out[g * s.rows + q, :, v * s.band : (v + 1) * s.band] = value[at : at + s.local, :]
    stage.send(1)

    def keep_rows(rows, lanes, value):
        ys_ref[rows, lanes] = value
        s_ref[rows, lanes] = value.astype(BF16)

    even_turn(s, stage.front(1), order, swap, updates(step, need(4), keep_rows))
    total_in = need(5)

    def put_change(rows, lanes, value):
        change = total_in[rows, lanes] + ratio * ys_ref[rows, lanes]
        grown[rows, lanes] = (change + weight * value).astype(BF16)

    even_slope_part(
        s, s_ref, t_ref, ys_ref, need(8), unit, need(6), need(7), need(9), need(10), turned, -1.0, put_change
    )
    row_lanes = need(11)
    for b in row_blocks(s.extent, ROWS):
        fill(s, stage.results[0], b, dot(row_lanes[b : b + ROWS, :], grown[...], ((1,), (1,))).astype(BF16))
    stage.send(0)


def even_finish(s, stage, small, temporaries):
    (post,) = temporaries
    post[...] = post_matrix(s)
    everyone = slice(0, s.devices)
    for v in range(s.extent // s.band):
        lanes = slice(v * s.band, (v + 1) * s.band)
        change = dot(post[:, lanes], flat_rows(stage.front(0), everyone), ((0,), (0,)))
        change = change + dot(flat_rows(stage.front(1), everyone, lanes), post[...], ((0,), (0,)))
        stage.results[v][...] = (stage.need(v)[...].reshape(s.band, s.extent) + change).reshape(
            stage.results[v].shape
        )
        stage.send(v)


def even_hamiltonian(s, stage, small, temporaries):
    (where_ref,) = small
    (post,) = temporaries
    left, right, left_rows, right_rows = stage.results
    own_ref, outer_ref = stage.need(0), stage.need(1)
    blocks, block = own_ref.shape[0], own_ref.shape[1]
    post[...] = post_matrix(s)
    row, column = iotas(block, s.extent)
    for b in range(blocks):
        spread = column - row
        to_own = mask_to(spread == b * block)
        to_far = mask_to(spread == where_ref[b] * block)
        left[b * block : (b + 1) * block, :] = (dot(own_ref[b], to_own) + dot(outer_ref[b], to_far)).astype(BF16)
    row, column = iotas(s.extent, s.extent)
    same = mask_to(row == column)
    for b in row_blocks(s.extent, ROWS):
        rows = slice(b, b + ROWS)
        right[rows, :] = dot(same[rows, :], left[...], ((1,), (1,))).astype(BF16)
        left_rows[rows, :] = dot(post[rows, :], left[...]).astype(BF16)
        right_rows[rows, :] = dot(post[rows, :], left[...], ((1,), (1,))).astype(BF16)
    for index in range(4):
        stage.send(index)


def even_weights(s, stage, small, temporaries):
    real_ref, imag_ref, rate_ref = small
    wa_s, wb_s, wa_t, wb_t, damp = stage.results
    columns_in, index_ref, mirror_ref, couplings_ref = [stage.need(k) for k in range(4)]
    me = lax.axis_index("aux") * s.rows + lax.axis_index("row")
    depth, wide = 2 * s.tile, MODES * s.tile
    row, column = iotas(s.auxes, wide)
    by_lane = mask_to(column % s.auxes == row)

    def spread(table):
        return dot(table.astype(F32).astype(BF16), by_lane, ((0,), (0,)))

    row, lane = iotas(s.extent, MODES)
    gather = mask_to(row == lane * s.band + me)
    row, lane = iotas(s.auxes, s.auxes * s.local)
    wanted = mask_to(lane == row * s.local)
    pieces = [columns_in[a // s.per_device * s.rows + a % s.per_device] for a in range(s.auxes)]
    counts = spread(dot(wanted, dot(jnp.concatenate(pieces, axis=0), gather).astype(BF16)))
    index, mirror = spread(index_ref[...]), spread(mirror_ref[...])
    lane_mode = lax.broadcasted_iota(jnp.int32, (1, wide), 1) // s.tile

    def of_mode(values):
        out = values[0]
        for k in range(1, MODES):
            out = jnp.where(lane_mode == k, values[k], out)
        return out

    take = lambda table, first: of_mode([table[first + k : first + k + 1, :] for k in range(MODES)])
    ups, downs = take(index, 0), take(index, MODES)
    up_kinds, down_kinds = take(mirror, 0), take(mirror, MODES)
    real = of_mode([counts[k : k + 1, :] * real_ref[k] for k in range(MODES)])
    imag = of_mode([counts[k : k + 1, :] * imag_ref[k] for k in range(MODES)])
    rates = counts[0:1, :] * rate_ref[0]
    for k in range(1, MODES):
        rates = rates + counts[k : k + 1, :] * rate_ref[k]
    damp[...] = rates

    row, column = iotas(s.extent, s.lanes)
    pick = (row % s.devices == me) & (row // s.devices == column // s.za)
    local_q = lax.dot_general(
        couplings_ref[...],
        pick.astype(F32),
        (((1,), (0,)), ((), ())),
        precision=lax.Precision.HIGHEST,
        preferred_element_type=F32,
    )

    row, column = iotas(depth, wide)
    same = row // s.za % s.fold == column // s.za % s.fold
    source, kind = (row % s.auxes).astype(F32), (row // s.tile).astype(F32)
    from_imag, to_imag = row // s.auxes % 2, column // s.auxes % 2
    up = same & (ups == source) & (up_kinds == kind)
    down = same & (downs == source) & (down_kinds == kind)
    along = jnp.where(up, 1.0, 0.0) + jnp.where(down, real, 0.0)
    cross = jnp.where(down, imag, 0.0)
    along = jnp.where(from_imag == 1, along, -along)
    flip = jnp.where((from_imag == 1) & (row // s.tile == 1), -1.0, 1.0)
    by_row = flip * jnp.where(from_imag == to_imag, cross, along)
    by_column = flip * jnp.where(from_imag == to_imag, cross, -along)

    def pieces(value):
        high = value.astype(BF16)
        return high, (value - high.astype(F32)).astype(BF16)

    for near, far, wa, wb in ((by_row, by_column, wa_s, wb_s), (by_column, by_row, wa_t, wb_t)):
        wb[:depth, :], wb[depth:, :] = pieces(far)
        for th in range(s.tiles):
            lanes = slice(th * s.tile, (th + 1) * s.tile)
            total = local_q[0:1, lanes] * near[:, : s.tile]
            for k in range(1, MODES):
                total = total + local_q[k : k + 1, lanes] * near[:, k * s.tile : (k + 1) * s.tile]
            wa[th, :depth, :], wa[th, depth:, :] = pieces(total)
    for index in range(5):
        stage.send(index)


def even_body(
    s,
    density,
    couplings,
    weight_real,
    weight_imag,
    mode_rates,
    tier_counts,
    link_index,
    link_mirror,
    block_diagonal,
    block_outer,
    block_column,
):
    planes, per_device, band, extent = density.shape
    cube = 2 * extent * extent * s.lanes
    state = shape(extent, s.lanes, dtype=BF16)
    full = shape(extent, s.lanes)
    pair = (shape(s.devices, 2, s.local, s.lanes, dtype=BF16), 2)
    held = pltpu.VMEM((extent, s.lanes), F32)
    held_b = pltpu.VMEM((extent, s.lanes), BF16)

    def exchange(message):
        return lax.all_to_all(message, BOTH, split_axis=0, concat_axis=0, tiled=True)

    blocks = density.reshape(1, planes * per_device, band, extent)
    message = run_staged(
        functools.partial(even_start, s),
        [pair],
        [(blocks, v) for v in range(planes * per_device)] + [tier_counts],
        temporaries=[held_b],
        grant=MOST,
        flops=2 * cube,
    )[0]
    got = exchange(message)

    left, right, left_rows, right_rows = run_staged(
        functools.partial(even_hamiltonian, s),
        [state] * 4,
        [block_diagonal, block_outer],
        temporaries=[held_b],
        scalars=[block_column],
        grant=MOST,
        flops=4 * cube,
    )
    q_first = couplings.T

    k, n = iotas(s.lanes, s.lanes)
    parts = band // s.devices
    row_lanes = (
        n
        == (k // s.local % s.rows * parts + k % parts) * s.za
        + k // (parts * per_device) % planes * s.auxes
        + k // (s.local * s.rows) * per_device
        + k // parts % per_device
    ).astype(BF16)
    column_lanes = (
        n
        == k % s.local * s.za
        + k // (s.local * s.groups * per_device) * s.auxes
        + k // s.local % s.groups * per_device
        + k // (s.local * s.groups) % per_device
    ).astype(BF16)

    k, n = iotas(s.tile, s.tile)
    sign = jnp.where(n // s.auxes % 2 == 0, 1.0, -1.0)
    unit = jnp.where(k // s.za * s.za + (k + s.auxes) % s.za == n, sign, 0.0).astype(BF16)
    wide, size = s.fold * s.tile, max(256, 16 * s.local)
    swap, order = pltpu.VMEM((wide, wide), BF16), pltpu.VMEM((size, size), BF16)

    message, s_now, t_now = run_staged(
        functools.partial(even_take, s),
        [pair, state, state],
        [row_lanes, right_rows, column_lanes, left_rows],
        front=[(got, 0), (got, 1)],
        grant=MOST,
        flops=4 * cube,
    )
    wa = shape(s.tiles, 4 * s.tile, s.tile, dtype=BF16)
    wb = shape(4 * s.tile, MODES * s.tile, dtype=BF16)
    wa_s, wb_s, wa_t, wb_t, damp = run_staged(
        functools.partial(even_weights, s),
        [wa, wb, wa, wb, shape(1, s.lanes)],
        [(got, 1), link_index, link_mirror, couplings],
        scalars=[weight_real, weight_imag, mode_rates],
        grant=MOST,
        flops=cube,
    )
    tables = [unit, damp, q_first, right, wa_s, wb_s, left, wa_t, wb_t]
    shares = [STEP / 6.0, STEP / 3.0, STEP / 3.0, STEP / 6.0]
    steps = [0.25, 0.25, 0.5]
    ratios = [share / step for share, step in zip(shares, steps)]
    got = exchange(message)
    base_s, base_t = run_staged(
        functools.partial(even_first_slope, s, steps[0]),
        [full, full],
        [s_now, t_now] + tables,
        temporaries=[held_b],
        flops=12 * cube,
    )
    total = None
    for section in range(2):
        step = steps[section]
        message = run_staged(
            functools.partial(even_next, s, step),
            [pair],
            [base_s, right_rows, (got, 1), base_t, left_rows],
            temporaries=[held_b, held_b, order, swap],
            front=[(got, 0)],
            flops=5 * cube,
        )[0]
        arrived, got = got, exchange(message)
        less = ratios[2] if section == 1 else 0.0
        base_s, base_t, total = run_staged(
            functools.partial(even_slope, s, step, steps[section + 1], ratios[section], less, total is not None),
            [full, full, full],
            [base_s, base_t, s_now, t_now] + tables + ([] if total is None else [total]),
            temporaries=[held_b, held_b, held_b, held, held, order, swap],
            front=[(arrived, 0), (arrived, 1)],
            flops=15 * cube,
        )
    message = run_staged(
        functools.partial(even_last, s, steps[2], ratios[2], shares[3]),
        [pair],
        [base_t, unit, left, column_lanes, base_s, total, damp, q_first, right, wa_s, wb_s, row_lanes],
        temporaries=[held, held_b, held_b, held_b, held_b, order, swap],
        front=[(got, 1), (got, 0)],
        flops=12 * cube,
    )[0]
    got = exchange(message)
    evolved = run_staged(
        functools.partial(even_finish, s),
        [(shape(1, planes * per_device, band, extent), planes * per_device)],
        [(blocks, v) for v in range(planes * per_device)],
        temporaries=[held_b],
        front=[(got, 0), (got, 1)],
        flops=2 * cube,
    )[0]
    return evolved.reshape(density.shape)


def body(density, *others):
    planes, per_device, band, extent = density.shape
    s = Sizes(lax.axis_size("aux"), lax.axis_size("row"), per_device, band, extent)
    even = band % s.devices == 0 and s.local % 16 == 0 and LANES % s.za == 0
    even = even and s.lanes == extent and planes * per_device * band == extent
    even = even and planes * per_device == MODES and per_device <= s.rows and s.devices <= s.band
    if even:
        return even_body(s, density, *others)
    return general_body(density, *others)


def solution(mesh):
    return jax.shard_map(
        body,
        mesh=mesh,
        in_specs=(
            P(None, "aux", "row", None),
            P(),
            P(),
            P(),
            P(),
            P("aux", None),
            P(),
            P(),
            P(),
            P(),
            P(),
        ),
        out_specs=P(None, "aux", "row", None),
        check_vma=False,
    )
```

```python
import functools

import jax
import jax.numpy as jnp
from jax import lax
from jax.experimental import pallas as pl
from jax.experimental.pallas import tpu as pltpu
from jax.sharding import PartitionSpec as P

MODES = 4
LINKS = 8
LANES = 128
STEP = 0.5
BOTH = ("aux", "row")
GRANT = 52 << 20
MOST = 60 << 20
ROWS = 512

F32 = jnp.float32
BF16 = jnp.bfloat16


class Sizes:
    def __init__(self, groups, rows, per_device, band, extent):
        self.groups, self.rows, self.per_device = groups, rows, per_device
        self.band, self.extent = band, extent
        self.devices = groups * rows
        self.local = band // groups
        self.auxes = per_device * groups
        self.za = 2 * self.auxes
        self.lanes = self.local * self.za
        self.fold = max(1, LANES // self.za)
        self.tile = self.fold * self.za
        self.tiles = self.local // self.fold
        self.joined = self.local % 16 == 0


def dot(a, b, dims=((1,), (0,))):
    return lax.dot_general(a, b, (dims, ((), ())), preferred_element_type=F32)


def run(kernel, outs, args, scratch=(), flops=0, scalars=()):
    spec = pl.BlockSpec(memory_space=pltpu.VMEM)
    flat = pl.BlockSpec(memory_space=pltpu.SMEM)
    moved = sum(a.size * a.dtype.itemsize for a in args)
    moved += sum(o.size * o.dtype.itemsize for o in outs)
    return pl.pallas_call(
        kernel,
        out_shape=list(outs),
        in_specs=[flat if n in scalars else spec for n in range(len(args))],
        out_specs=[spec] * len(outs),
        scratch_shapes=list(scratch),
        compiler_params=pltpu.CompilerParams(vmem_limit_bytes=16 << 20),
        cost_estimate=pl.CostEstimate(flops=flops, bytes_accessed=moved, transcendentals=0),
    )(*args)


def shape(*dims, dtype=F32):
    return jax.ShapeDtypeStruct(dims, dtype)


def one_hot(target, count):
    return (target[:, None] == jnp.arange(count, dtype=jnp.int32)[None, :]).astype(BF16)


def matrix_index(s, index, device):
    group, row = device // s.rows, device % s.rows
    return row * s.band + index * s.groups + group


def row_blocks(extent, size=128):
    return range(0, extent, size)


def send_start_kernel(d_ref, pick_rows, pick_cols, out_ref):
    planes, number, band, extent = d_ref.shape
    flat = d_ref[...].reshape(planes * number * band, extent).astype(BF16)
    for b in row_blocks(flat.shape[0]):
        moved = dot(pick_rows[b : b + 128, :], flat).astype(BF16)
        out_ref[b : b + 128, :] = dot(moved, pick_cols[...]).astype(BF16)


def take_start_kernel(got_ref, pick_lanes, message_rows, s_ref, m_ref):
    for b in row_blocks(got_ref.shape[1]):
        s_ref[b : b + 128, :] = dot(
            got_ref[:, b : b + 128], pick_lanes[...], ((0,), (0,))
        ).astype(BF16)
    for b in row_blocks(m_ref.shape[0]):
        m_ref[b : b + 128, :] = dot(message_rows[b : b + 128, :], s_ref[...]).astype(BF16)


def turn(s, load, order, swap, put):
    size = order.shape[0]
    span = size // s.local
    blocks = s.extent // size
    parts = []
    for block in range(blocks):
        moved = dot(order[...], load(block * size, size))
        for ih in range(s.tiles):
            for jh in range(s.tiles):
                lanes = slice(jh * s.tile, (jh + 1) * s.tile)
                pieces = [
                    moved[(ih * s.fold + f) * span : (ih * s.fold + f + 1) * span, lanes]
                    for f in range(s.fold)
                ]
                parts.append(jnp.concatenate(pieces, axis=1) if s.fold > 1 else pieces[0])
    turned = dot(jnp.concatenate(parts, axis=0).astype(BF16), swap[...])
    for block in range(blocks):
        for ih in range(s.tiles):
            for jh in range(s.tiles):
                start = ((block * s.tiles + ih) * s.tiles + jh) * span
                for f in range(s.fold):
                    first = (jh * s.fold + f) * s.devices + block * span
                    put(
                        slice(first, first + span),
                        slice(ih * s.tile, (ih + 1) * s.tile),
                        turned[start : start + span, f * s.tile : (f + 1) * s.tile],
                    )


def take_columns_kernel(s, got_ref, order, swap, first_rows, left_rows, s_ref, t_ref, *message):
    def put(rows, lanes, value):
        t_ref[rows, lanes] = value.astype(BF16)

    turn(s, lambda start, size: got_ref[start : start + size, :], order, swap, put)
    write_messages(s, first_rows, left_rows, s_ref, t_ref, message)


def write_messages(s, right_rows, left_rows, s_ref, t_ref, message):
    pairs = ((left_rows, t_ref), (right_rows, s_ref))
    if not s.joined and len(message) == 1:
        pairs = pairs[:1]
    both = s.joined and message[0].shape[0] == 2 * s.extent
    for part, (matrix, state) in enumerate(pairs):
        if s.joined and part == 1 and not both:
            continue
        for b in row_blocks(s.extent):
            product = dot(matrix[b : b + 128, :], state[...]).astype(BF16)
            if not s.joined:
                message[part][b : b + 128, :] = product
            elif not both:
                message[0][b : b + 128, :] = product
            else:
                for k in range(128 // s.local):
                    start = ((b // s.local + k) * 2 + part) * s.local
                    message[0][start : start + s.local, :] = product[
                        k * s.local : (k + 1) * s.local, :
                    ]


def slope_kernel(
    s, with_columns, s_ref, t_ref, ys_ref, yt_ref, damp, q_ref, right, left, unit, wa_s, wb_s, wa_t, wb_t, *rest
):
    if with_columns:
        ks_ref, kt_ref, turned = rest
    else:
        ks_ref, turned = rest

    def one(direct, mirror, y_ref, h, wa, wb, out_ref, sign):
        for th in range(s.tiles):
            lanes = slice(th * s.tile, (th + 1) * s.tile)
            turned[:, lanes] = dot(direct[:, lanes], unit[...]).astype(BF16)
        for b in row_blocks(s.extent):
            rows = slice(b, b + 128)
            whole = dot(h[rows, :], turned[...])
            for th in range(s.tiles):
                lanes = slice(th * s.tile, (th + 1) * s.tile)
                source = jnp.concatenate([direct[rows, lanes], mirror[rows, lanes]], axis=1)
                source = jnp.concatenate([source, source], axis=1)
                total = dot(source, wa[th]) - damp[:, lanes] * y_ref[rows, lanes].astype(F32)
                total = total + sign * whole[:, lanes]
                fields = dot(source, wb[...])
                for k in range(MODES):
                    total = total + q_ref[rows, k : k + 1] * fields[:, k * s.tile : (k + 1) * s.tile]
                out_ref[rows, lanes] = total

    one(s_ref, t_ref, ys_ref, right, wa_s, wb_s, ks_ref, -1.0)
    if with_columns:
        one(t_ref, s_ref, yt_ref, left, wa_t, wb_t, kt_ref, 1.0)


def part_loader(s, refs, part):
    def load(start, size):
        if not s.joined:
            return refs[part][start : start + size, :]
        step = s.local
        pieces = []
        for first in range(start, start + size, step):
            at = (first // step * 2 + part) * step
            pieces.append(refs[0][at : at + step, :])
        return jnp.concatenate(pieces, axis=0)

    return load


def next_kernel(s, weight, step, has_total, both, got_count, *refs):
    got = refs[:got_count]
    refs = refs[got_count:]
    order, swap, right_rows, left_rows, ks_ref, kt_ref, ds_ref, dt_ref = refs[:8]
    refs = refs[8:]
    total_in = None
    if has_total:
        total_in, refs = refs[0], refs[1:]
    s_ref, t_ref, ys_ref, yt_ref, total_ref = refs[:5]
    message, arrived = refs[5:-1], refs[-1]

    def put(rows, lanes, value):
        arrived[rows, lanes] = value

    for part in range(2):
        turn(s, part_loader(s, got, part), order, swap, put)
        for b in row_blocks(s.extent, 64):
            rows = slice(b, b + 64)
            if part == 0:
                slope = ks_ref[rows, :] + arrived[rows, :]
                grown = weight * slope
                total_ref[rows, :] = total_in[rows, :] + grown if has_total else grown
                state = ds_ref[rows, :].astype(F32) + step * slope
                ys_ref[rows, :] = state
                s_ref[rows, :] = state.astype(BF16)
            else:
                slope = kt_ref[rows, :] - arrived[rows, :]
                state = dt_ref[rows, :].astype(F32) + step * slope
                yt_ref[rows, :] = state
                t_ref[rows, :] = state.astype(BF16)
    if message:
        write_messages(s, right_rows, left_rows, s_ref, t_ref, message)


def last_kernel(s, weight, got_ref, order, swap, ks_ref, total_in, pick_lanes, out_ref, arrived, grown):
    def put(rows, lanes, value):
        arrived[rows, lanes] = value

    turn(s, lambda start, size: got_ref[start : start + size, :], order, swap, put)
    for b in row_blocks(s.extent, 64):
        rows = slice(b, b + 64)
        change = total_in[rows, :] + weight * (ks_ref[rows, :] + arrived[rows, :])
        grown[rows, :] = change.astype(BF16)
    for b in row_blocks(s.lanes):
        out_ref[b : b + 128, :] = dot(
            pick_lanes[b : b + 128, :], grown[...], ((1,), (1,))
        ).astype(BF16)


def finish_kernel(got_ref, place_rows, place_cols, d_ref, out_ref):
    planes, number, band, extent = d_ref.shape
    for z in range(planes):
        for n in range(number):
            at = (z * number + n) * band
            for b in range(0, band, min(band, 128)):
                size = min(band, 128)
                rows = slice(at + b, at + b + size)
                moved = dot(place_rows[rows, :], got_ref[...]).astype(BF16)
                out_ref[z, n, b : b + size, :] = d_ref[z, n, b : b + size, :] + dot(
                    moved, place_cols[...]
                )


def link_matrices(s, counts, weight_real, weight_imag, link_index, link_mirror):
    ones = jnp.ones_like(counts)
    real = jnp.stack([ones, counts * weight_real[None, :]], 1)
    imag = jnp.stack([jnp.zeros_like(counts), counts * weight_imag[None, :]], 1)
    index = link_index.reshape(s.auxes, 2, MODES)
    mirror = link_mirror.reshape(s.auxes, 2, MODES)
    source = jnp.arange(s.auxes, dtype=jnp.int32)
    hit = index[None] == source[:, None, None, None]
    kinds = jnp.stack([hit & (mirror[None] == 0), hit & (mirror[None] == 1)]).astype(F32)
    along = jnp.sum(kinds * real, 3)
    cross = jnp.sum(kinds * imag, 3)
    along, cross = (jnp.transpose(m, (0, 3, 1, 2)) for m in (along, cross))
    flip = jnp.array([1.0, -1.0], F32).reshape(2, 1, 1, 1)

    def build(sign):
        upper = jnp.concatenate([cross, -sign * along], 3)
        lower = jnp.concatenate([sign * along, cross], 3) * flip
        return jnp.concatenate([upper, lower], 2)

    return build(1.0), build(-1.0)


def two_pieces(weights, axis):
    high = lax.reduce_precision(weights, 8, 7)
    low = weights - high
    return jnp.concatenate([high.astype(BF16), low.astype(BF16)], axis)


def coupling_weights(s, by_local, by_first, local_q):
    eye = jnp.eye(s.fold, dtype=F32)
    near = jnp.einsum("ki,xkuv->ixuv", local_q, by_local, precision=lax.Precision.HIGHEST)
    near = near.reshape(s.tiles, s.fold, 2, s.za, s.za)
    near = jnp.transpose(near, (0, 2, 1, 3, 4))[:, :, :, :, None, :] * eye[None, None, :, None, :, None]
    near = near.reshape(s.tiles, 2 * s.tile, s.tile)
    far = jnp.transpose(by_first, (0, 2, 1, 3))[:, None, :, :, None, :] * eye[None, :, None, None, :, None]
    far = far.reshape(2 * s.tile, MODES * s.tile)
    return two_pieces(near, 1), two_pieces(far, 0)


def general_body(
    density,
    couplings,
    weight_real,
    weight_imag,
    mode_rates,
    tier_counts,
    link_index,
    link_mirror,
    block_diagonal,
    block_outer,
    block_column,
):
    planes, per_device, band, extent = density.shape
    s = Sizes(lax.axis_size("aux"), lax.axis_size("row"), per_device, band, extent)
    blocks, block = block_diagonal.shape[0], block_diagonal.shape[1]
    group, row = lax.axis_index("aux"), lax.axis_index("row")
    device = group * s.rows + row
    cube = 2 * extent * extent * s.lanes

    number = jnp.arange(extent, dtype=jnp.int32)
    first_to_matrix = matrix_index(s, number // s.devices, number % s.devices)
    posted_to_matrix = matrix_index(s, number % s.local, number // s.local)
    posted_to_first = number % s.local * s.devices + number // s.local

    wide = jnp.arange(s.lanes, dtype=jnp.int32)
    sub = planes * per_device * s.local
    start_source = wide % sub * s.groups + wide // sub
    pick_rows = one_hot(start_source, s.lanes)
    pick_cols = one_hot(first_to_matrix, extent).T
    lane_of = (
        wide % s.local * s.za
        + wide // (per_device * s.local) % planes * s.auxes
        + wide // sub * per_device
        + wide // s.local % per_device
    )
    pick_lanes = one_hot(lane_of, s.lanes)
    message_rows = one_hot(posted_to_first, extent)
    start_message = run(
        send_start_kernel,
        [shape(s.lanes, extent, dtype=BF16)],
        [density, pick_rows, pick_cols],
        flops=2 * cube,
    )[0]
    start_got = lax.all_to_all(
        start_message.reshape(s.groups, sub, extent), "aux", split_axis=0, concat_axis=0, tiled=True
    ).reshape(s.lanes, extent)

    selector = block_column[:, None] == jnp.arange(blocks, dtype=jnp.int32)[None, :]
    own = jnp.eye(blocks, dtype=F32)
    whole_h = (
        own[:, None, :, None] * block_diagonal.astype(F32)[:, :, None, :]
        + selector.astype(F32)[:, None, :, None] * block_outer.astype(F32)[:, :, None, :]
    ).reshape(extent, extent).astype(BF16)
    first_h = one_hot(first_to_matrix, extent)
    left = jnp.dot(
        jnp.dot(first_h, whole_h, preferred_element_type=BF16), first_h.T, preferred_element_type=BF16
    )
    right = left.T
    left_rows = jnp.dot(message_rows, left, preferred_element_type=BF16)
    right_rows = jnp.dot(message_rows, right, preferred_element_type=BF16)

    counts = lax.all_gather(tier_counts, "aux", axis=0, tiled=True).astype(F32)
    damping = jnp.sum(counts * mode_rates[None, :], axis=1)
    damp = jnp.tile(damping, (planes * s.local,))[None, :]
    q_first = jnp.dot(
        couplings, first_h.T.astype(F32), precision=lax.Precision.HIGHEST
    ).T
    local_pick = (matrix_index(s, jnp.arange(s.local, dtype=jnp.int32), device)[None, :] == number[:, None])
    local_q = jnp.dot(couplings, local_pick.astype(F32), precision=lax.Precision.HIGHEST)
    by_row, by_column = link_matrices(s, counts, weight_real, weight_imag, link_index, link_mirror)
    wa_s, wb_s = coupling_weights(s, by_row, by_column, local_q)
    wa_t, wb_t = coupling_weights(s, by_column, by_row, local_q)

    lane = jnp.arange(s.za, dtype=jnp.int32)
    unit = jnp.where(
        lane[:, None] == (lane[None, :] + s.auxes) % s.za,
        jnp.where(lane[None, :] < s.auxes, 1.0, -1.0),
        0.0,
    )
    eye_fold = jnp.eye(s.fold, dtype=F32)
    unit_tile = (eye_fold[:, None, :, None] * unit[None, :, None, :]).reshape(s.tile, s.tile).astype(BF16)
    swap = (
        eye_fold[:, None, None, None, :, None]
        * eye_fold[None, :, None, :, None, None]
        * unit[None, None, :, None, None, :]
    ).reshape(s.fold * s.tile, s.fold * s.tile).astype(BF16)
    keep = (
        eye_fold[:, None, None, None, :, None]
        * eye_fold[None, :, None, :, None, None]
        * jnp.eye(s.za, dtype=F32)[None, None, :, None, None, :]
    ).reshape(s.fold * s.tile, s.fold * s.tile).astype(BF16)
    size = min(extent, max(256, 16 * s.local))
    span = size // s.local
    at = jnp.arange(size, dtype=jnp.int32)
    order = one_hot(at % span * s.local + at // span, size)

    state = shape(extent, s.lanes, dtype=BF16)
    full = shape(extent, s.lanes)
    held = pltpu.VMEM((extent, s.lanes), F32)
    held_b = pltpu.VMEM((extent, s.lanes), BF16)

    def exchange(messages):
        parts = [m.reshape(s.devices, -1, s.lanes) for m in messages]
        sent = parts[0] if len(parts) == 1 else jnp.concatenate(parts, 1)
        got = lax.all_to_all(sent, BOTH, split_axis=0, concat_axis=0, tiled=True)
        if len(parts) == 1:
            return [got.reshape(-1, s.lanes)]
        height = s.local
        return [got[:, p * height : (p + 1) * height].reshape(-1, s.lanes) for p in range(2)]

    if s.joined:
        pair = [shape(2 * extent, s.lanes, dtype=BF16)]
    else:
        pair = [state, state]

    s_now, posted = run(
        take_start_kernel, [state, state], [start_got, pick_lanes, message_rows], flops=2 * cube
    )
    got = exchange([posted])
    t_now, *messages = run(
        functools.partial(take_columns_kernel, s),
        [state] + pair,
        [got[0], order, keep, right_rows, left_rows, s_now],
        flops=4 * cube,
    )
    start_s, start_t = s_now, t_now
    ys, yt = s_now, t_now
    total = None
    shares = [STEP / 6.0, STEP / 3.0, STEP / 3.0, STEP / 6.0]
    steps = [0.25, 0.25, 0.5]
    for section in range(4):
        got = exchange(messages)
        columns = section < 3
        slopes = run(
            functools.partial(slope_kernel, s, columns),
            [full, full] if columns else [full],
            [s_now, t_now, ys, yt, damp, q_first, right, left, unit_tile, wa_s, wb_s, wa_t, wb_t],
            scratch=[held_b],
            flops=(12 if columns else 6) * cube,
        )
        if columns:
            args = list(got) + [order, swap, right_rows, left_rows, *slopes, start_s, start_t]
            if total is not None:
                args.append(total)
            outs = [state, state, full, full, full]
            outs += pair if section < 2 else [state]
            s_now, t_now, ys, yt, total, *messages = run(
                functools.partial(
                    next_kernel, s, shares[section], steps[section], total is not None, section < 2, len(got)
                ),
                outs,
                args,
                scratch=[held],
                flops=6 * cube,
            )
    change = run(
        functools.partial(last_kernel, s, shares[3]),
        [shape(s.lanes, extent, dtype=BF16)],
        [got[0], order, swap, slopes[0], total, pick_lanes],
        scratch=[held, held_b],
        flops=3 * cube,
    )[0]
    back = lax.all_to_all(
        change.reshape(s.groups, sub, extent), "aux", split_axis=0, concat_axis=0, tiled=True
    ).reshape(s.lanes, extent)
    return run(
        finish_kernel,
        [shape(planes, per_device, band, extent)],
        [back, pick_rows.T, pick_cols.T, density],
        flops=2 * cube,
    )[0]


def iotas(rows, columns):
    return (
        lax.broadcasted_iota(jnp.int32, (rows, columns), 0),
        lax.broadcasted_iota(jnp.int32, (rows, columns), 1),
    )


def mask_to(value):
    return value.astype(F32).astype(BF16)


def post_matrix(s):
    row, column = iotas(s.extent, s.extent)
    return mask_to(column == row % s.local * s.devices + row // s.local)


class Stage:
    def __init__(self, sources, buffers, targets, results, semaphores, offset, lead):
        self.buffers, self.results, self.targets = buffers, results, targets
        self.semaphores, self.next, self.offset = semaphores, 0, offset
        self.sources, self.lead = sources, lead
        self.coming = [self.copy(a, b) for a, b in zip(sources[:lead], buffers)]
        self.going = []

    def copy(self, source, target):
        made = pltpu.make_async_copy(source, target, self.semaphores.at[self.next])
        self.next += 1
        made.start()
        return made

    def front(self, index):
        return self.need(index - self.offset)

    def need(self, index):
        index += self.offset
        if index >= len(self.coming):
            self.start_rest()
        if self.coming[index] is not None:
            self.coming[index].wait()
            self.coming[index] = None
        return self.buffers[index]

    def start_rest(self):
        known = len(self.coming)
        self.coming += [self.copy(a, b) for a, b in zip(self.sources[known:], self.buffers[known:])]

    def send(self, index):
        self.going.append(self.copy(self.results[index], self.targets[index]))

    def finish(self):
        for made in self.going:
            made.wait()


def run_staged(body, outs, args, temporaries=(), scalars=(), front=(), lead=None, grant=GRANT, flops=0):
    arrays, views = [], []
    for arg in [*front, *args]:
        array, part = arg if isinstance(arg, tuple) else (arg, None)
        if not any(array is a for a in arrays):
            arrays.append(array)
        views.append(([array is a for a in arrays].index(True), part))
    shapes, places = [], []
    for out in outs:
        if isinstance(out, tuple):
            for part in range(out[1]):
                places.append((len(shapes), part))
            shapes.append(out[0])
        else:
            places.append((len(shapes), None))
            shapes.append(out)
    tall = lambda x, part: x.shape if part is None else x.shape[:1] + x.shape[2:]
    buffers = [pltpu.VMEM(tall(arrays[k], part), arrays[k].dtype) for k, part in views]
    results = [pltpu.VMEM(tall(shapes[k], part), shapes[k].dtype) for k, part in places]
    count = len(buffers) + len(results)

    def kernel(*refs):
        small, refs = refs[: len(scalars)], refs[len(scalars) :]
        source, refs = refs[: len(arrays)], refs[len(arrays) :]
        target, refs = refs[: len(shapes)], refs[len(shapes) :]
        own, refs = refs[: len(buffers)], refs[len(buffers) :]
        made, refs = refs[: len(results)], refs[len(results) :]
        pick = lambda ref, part: ref if part is None else ref.at[:, part]
        stage = Stage(
            [pick(source[k], part) for k, part in views],
            own,
            [pick(target[k], part) for k, part in places],
            made,
            refs[-1],
            len(front),
            len(views) if lead is None else lead,
        )
        body(stage, small, refs[:-1])
        stage.finish()

    moved = sum(a.size * a.dtype.itemsize for a in arrays)
    moved += sum(o.size * o.dtype.itemsize for o in shapes)
    far = pl.BlockSpec(memory_space=pltpu.HBM)
    return pl.pallas_call(
        kernel,
        out_shape=shapes,
        in_specs=[pl.BlockSpec(memory_space=pltpu.SMEM)] * len(scalars) + [far] * len(arrays),
        out_specs=[far] * len(shapes),
        scratch_shapes=buffers + results + list(temporaries) + [pltpu.SemaphoreType.DMA((count,))],
        compiler_params=pltpu.CompilerParams(vmem_limit_bytes=grant),
        cost_estimate=pl.CostEstimate(flops=flops, bytes_accessed=moved, transcendentals=0),
    )(*scalars, *arrays)


def fill(s, result, first, value, lanes=slice(None)):
    count = value.shape[0] // s.local
    device = first // s.local
    result[device : device + count, :, lanes] = value.reshape(count, s.local, value.shape[1])


def flat_rows(ref, rows, lanes=slice(None)):
    piece = ref[rows, :, lanes]
    return piece.reshape(piece.shape[0] * piece.shape[1], piece.shape[2])


def even_start(s, stage, small, temporaries):
    (post,) = temporaries
    post[...] = post_matrix(s)
    blocks = s.extent // s.band
    which = lax.axis_index("row") % s.per_device
    flats = [stage.need(v)[...].reshape(s.band, s.extent).astype(BF16) for v in range(blocks)]
    row, lane = iotas(ROWS, s.band)
    counts = stage.need(blocks)[...].astype(F32)
    mine = counts[0:1, :]
    for n in range(1, s.per_device):
        mine = jnp.where(which == n, counts[n : n + 1, :], mine)
    for v in range(blocks):
        count = mine[:, v : v + 1]
        for b in row_blocks(s.extent, ROWS):
            value = dot(post[b : b + ROWS, :], flats[v], ((1,), (1,)))
            own = (row % s.local == 0) & (lane == (row + b) // s.local)
            value = jnp.where(own, count, value).astype(BF16)
            fill(s, stage.results[1], b, value, slice(v * s.band, (v + 1) * s.band))
    stage.send(1)
    flat = jnp.concatenate(flats, axis=0)
    for b in row_blocks(s.extent, ROWS):
        fill(s, stage.results[0], b, dot(post[b : b + ROWS, :], flat).astype(BF16))
    stage.send(0)


def send_products(s, stage, matrix, state_ref, index):
    for b in row_blocks(s.extent, ROWS):
        fill(s, stage.results[index], b, dot(matrix[b : b + ROWS, :], state_ref[...]).astype(BF16))
    stage.send(index)


def even_take(s, stage, small, temporaries):
    s_ref, t_ref = stage.results[2], stage.results[3]
    me = lax.axis_index("aux") * s.rows + lax.axis_index("row")
    everyone = slice(0, s.devices)
    rows_in, row_lanes = stage.front(0), stage.need(0)
    for b in row_blocks(s.extent, ROWS):
        s_ref[b : b + ROWS, :] = dot(
            flat_rows(rows_in, everyone, slice(b, b + ROWS)), row_lanes[...], ((0,), (0,))
        ).astype(BF16)
    stage.send(2)
    send_products(s, stage, stage.need(1), s_ref, 1)
    columns_in, column_lanes = stage.front(1), stage.need(2)
    blocks = s.extent // s.band
    parts = s.band // s.devices
    row, lane = iotas(s.devices, s.tile)
    mine = (row == me) & (lane < s.za)
    bands = []
    for q in range(s.rows):
        pieces = []
        for v in range(blocks):
            for g in range(s.groups):
                pieces.append(columns_in[g * s.rows + q, :, v * s.band : (v + 1) * s.band])
        bands.append(jnp.concatenate(pieces, axis=0))
    t_ref[...] = dot(jnp.concatenate(bands, axis=1), column_lanes[...], ((0,), (0,))).astype(BF16)
    for q in range(s.rows):
        rows = slice(q * s.band, q * s.band + s.devices)
        first = q * parts * s.za
        kept = s_ref[: s.devices, first : first + s.tile].astype(F32)
        t_ref[rows, : s.tile] = jnp.where(mine, kept, t_ref[rows, : s.tile].astype(F32)).astype(BF16)
    stage.send(3)
    send_products(s, stage, stage.need(3), t_ref, 0)


def turn_matrices(s, order, swap):
    size = order.shape[0]
    span = size // s.local
    k, n = lax.broadcasted_iota(jnp.int32, (size, 1), 0), lax.broadcasted_iota(jnp.int32, (1, size), 1)
    order[...] = mask_to(n == k % span * s.local + k // span)
    wide = s.fold * s.tile
    k, n = lax.broadcasted_iota(jnp.int32, (wide, 1), 0), lax.broadcasted_iota(jnp.int32, (1, wide), 1)
    sign = jnp.where(n // s.auxes % 2 == 0, 1.0, -1.0)
    there = (k // s.za % s.fold * s.fold + k // s.tile) * s.za + (k + s.auxes) % s.za
    swap[...] = jnp.where(there == n, sign, 0.0).astype(BF16)


def even_turn(s, got, order, swap, put):
    def load(start, size):
        return flat_rows(got, slice(start // s.local, (start + size) // s.local))

    turn(s, load, order, swap, put)


def updates(scale, base_ref, keep):
    def put(rows, lanes, value):
        keep(rows, lanes, base_ref[rows, lanes] + scale * value)

    return put


def even_next(s, step, stage, small, temporaries):
    s_ref, t_ref, order, swap = temporaries
    turn_matrices(s, order, swap)

    def keep_in(ref):
        def keep(rows, lanes, value):
            ref[rows, lanes] = value.astype(BF16)

        return keep

    got = stage.front(0)
    stage.start_rest()
    even_turn(s, got, order, swap, updates(step, stage.need(0), keep_in(s_ref)))
    send_products(s, stage, stage.need(1), s_ref, 1)
    got = stage.need(2)
    even_turn(s, got, order, swap, updates(-step, stage.need(3), keep_in(t_ref)))
    send_products(s, stage, stage.need(4), t_ref, 0)


def even_slope_part(s, direct, mirror, y_ref, h, unit, damp, q_ref, wa, wb, turned, sign, put):
    factors = [jnp.broadcast_to(q_ref[:, k : k + 1], (s.extent, s.tile)) for k in range(MODES)]
    for th in range(s.tiles):
        lanes = slice(th * s.tile, (th + 1) * s.tile)
        turned[:, lanes] = dot(direct[:, lanes], unit[...]).astype(BF16)
    for b in row_blocks(s.extent, ROWS):
        rows = slice(b, b + ROWS)
        whole = dot(h[rows, :], turned[...])
        for th in range(s.tiles):
            lanes = slice(th * s.tile, (th + 1) * s.tile)
            source = jnp.concatenate([direct[rows, lanes], mirror[rows, lanes]], axis=1)
            source = jnp.concatenate([source, source], axis=1)
            total = dot(source, wa[th]) - damp[:, lanes] * y_ref[rows, lanes].astype(F32)
            total = total + sign * whole[:, lanes]
            fields = dot(source, wb[...])
            for k in range(MODES):
                total = total + factors[k][rows, :] * fields[:, k * s.tile : (k + 1) * s.tile]
            put(rows, lanes, total)


def put_base(ref, start_ref, step):
    def put(rows, lanes, value):
        ref[rows, lanes] = start_ref[rows, lanes].astype(F32) + step * value

    return put


def even_first_slope(s, step, stage, small, temporaries):
    (turned,) = temporaries
    need = stage.need
    first, second = stage.results
    s_ref, t_ref, unit, damp, q_ref = need(0), need(1), need(2), need(3), need(4)
    put = put_base(first, s_ref, step)
    even_slope_part(s, s_ref, t_ref, s_ref, need(5), unit, damp, q_ref, need(6), need(7), turned, -1.0, put)
    stage.send(0)
    put = put_base(second, t_ref, step)
    even_slope_part(s, t_ref, s_ref, t_ref, need(8), unit, damp, q_ref, need(9), need(10), turned, 1.0, put)
    stage.send(1)


def even_slope(s, step, next_step, ratio, less, has_total, stage, small, temporaries):
    turned, s_ref, t_ref, ys_ref, yt_ref, order, swap = temporaries
    turn_matrices(s, order, swap)
    need = stage.need
    first, second, total_ref = stage.results

    def keep_in(ref, exact):
        def keep(rows, lanes, value):
            exact[rows, lanes] = value
            ref[rows, lanes] = value.astype(BF16)

        return keep

    even_turn(s, stage.front(0), order, swap, updates(step, need(0), keep_in(s_ref, ys_ref)))
    even_turn(s, stage.front(1), order, swap, updates(-step, need(1), keep_in(t_ref, yt_ref)))
    ds_ref, dt_ref = need(2), need(3)
    total_in = need(13) if has_total else None
    for b in row_blocks(s.extent, 64):
        rows = slice(b, b + 64)
        grown = ratio * ys_ref[rows, :] - (ratio + less) * ds_ref[rows, :].astype(F32)
        total_ref[rows, :] = total_in[rows, :] + grown if has_total else grown
    stage.send(2)
    unit, damp, q_ref = need(4), need(5), need(6)
    put = put_base(first, ds_ref, next_step)
    even_slope_part(s, s_ref, t_ref, ys_ref, need(7), unit, damp, q_ref, need(8), need(9), turned, -1.0, put)
    stage.send(0)
    put = put_base(second, dt_ref, next_step)
    even_slope_part(s, t_ref, s_ref, yt_ref, need(10), unit, damp, q_ref, need(11), need(12), turned, 1.0, put)
    stage.send(1)


def even_last(s, step, ratio, weight, stage, small, temporaries):
    ys_ref, s_ref, t_ref, grown, turned, order, swap = temporaries
    turn_matrices(s, order, swap)
    need = stage.need

    def keep_columns(rows, lanes, value):
        t_ref[rows, lanes] = value.astype(BF16)

    got = stage.front(0)
    stage.start_rest()
    even_turn(s, got, order, swap, updates(-step, need(0), keep_columns))
    unit, left, column_lanes = need(1), need(2), need(3)
    for th in range(s.tiles):
        lanes = slice(th * s.tile, (th + 1) * s.tile)
        turned[:, lanes] = dot(t_ref[:, lanes], unit[...]).astype(BF16)
    for b in row_blocks(s.extent, ROWS):
        rows = slice(b, b + ROWS)
        grown[rows, :] = (weight * dot(left[rows, :], turned[...])).astype(BF16)
    out = stage.results[1]
    value = dot(column_lanes[...], grown[...], ((1,), (1,))).astype(BF16)
    for q in range(s.rows):
        for v in range(s.extent // s.band):
            for g in range(s.groups):
                at = (v * s.groups + g) * s.local
                piece = value[at : at + s.local, q * s.band : (q + 1) * s.band]
                out[g * s.rows + q, :, v * s.band : (v + 1) * s.band] = piece
    stage.send(1)

    def keep_rows(rows, lanes, value):
        ys_ref[rows, lanes] = value
        s_ref[rows, lanes] = value.astype(BF16)

    even_turn(s, stage.front(1), order, swap, updates(step, need(4), keep_rows))
    total_in = need(5)

    def put_change(rows, lanes, value):
        change = total_in[rows, lanes] + ratio * ys_ref[rows, lanes]
        grown[rows, lanes] = (change + weight * value).astype(BF16)

    even_slope_part(
        s, s_ref, t_ref, ys_ref, need(8), unit, need(6), need(7), need(9), need(10), turned, -1.0, put_change
    )
    row_lanes = need(11)
    for b in row_blocks(s.extent, ROWS):
        fill(s, stage.results[0], b, dot(row_lanes[b : b + ROWS, :], grown[...], ((1,), (1,))).astype(BF16))
    stage.send(0)


def even_finish(s, stage, small, temporaries):
    (post,) = temporaries
    post[...] = post_matrix(s)
    everyone = slice(0, s.devices)
    change = dot(post[...], flat_rows(stage.front(0), everyone), ((0,), (0,)))
    change = change + dot(flat_rows(stage.front(1), everyone), post[...], ((0,), (0,)))
    for v in range(s.extent // s.band):
        rows = slice(v * s.band, (v + 1) * s.band)
        stage.results[v][...] = (stage.need(v)[...].reshape(s.band, s.extent) + change[rows, :]).reshape(
            stage.results[v].shape
        )
        stage.send(v)


def even_hamiltonian(s, stage, small, temporaries):
    (where_ref,) = small
    (post,) = temporaries
    left, right, left_rows, right_rows = stage.results
    own_ref, outer_ref = stage.need(0), stage.need(1)
    blocks, block = own_ref.shape[0], own_ref.shape[1]
    post[...] = post_matrix(s)
    row, column = iotas(block, s.extent)
    for b in range(blocks):
        spread = column - row
        to_own = mask_to(spread == b * block)
        to_far = mask_to(spread == where_ref[b] * block)
        left[b * block : (b + 1) * block, :] = (dot(own_ref[b], to_own) + dot(outer_ref[b], to_far)).astype(BF16)
    row, column = iotas(s.extent, s.extent)
    same = mask_to(row == column)
    for b in row_blocks(s.extent, ROWS):
        rows = slice(b, b + ROWS)
        right[rows, :] = dot(same[rows, :], left[...], ((1,), (1,))).astype(BF16)
        left_rows[rows, :] = dot(post[rows, :], left[...]).astype(BF16)
        right_rows[rows, :] = dot(post[rows, :], left[...], ((1,), (1,))).astype(BF16)
    for index in range(4):
        stage.send(index)


def even_weights(s, stage, small, temporaries):
    real_ref, imag_ref, rate_ref = small
    wa_s, wb_s, wa_t, wb_t, damp = stage.results
    columns_in, index_ref, mirror_ref, couplings_ref = [stage.need(k) for k in range(4)]
    me = lax.axis_index("aux") * s.rows + lax.axis_index("row")
    depth, wide = 2 * s.tile, MODES * s.tile
    row, column = iotas(s.auxes, wide)
    by_lane = mask_to(column % s.auxes == row)

    def spread(table):
        return dot(table.astype(F32).astype(BF16), by_lane, ((0,), (0,)))

    row, lane = iotas(s.extent, MODES)
    gather = mask_to(row == lane * s.band + me)
    row, lane = iotas(s.auxes, s.auxes * s.local)
    wanted = mask_to(lane == row * s.local)
    pieces = [columns_in[a // s.per_device * s.rows + a % s.per_device] for a in range(s.auxes)]
    counts = spread(dot(wanted, dot(jnp.concatenate(pieces, axis=0), gather).astype(BF16)))
    index, mirror = spread(index_ref[...]), spread(mirror_ref[...])
    lane_mode = lax.broadcasted_iota(jnp.int32, (1, wide), 1) // s.tile

    def of_mode(values):
        out = values[0]
        for k in range(1, MODES):
            out = jnp.where(lane_mode == k, values[k], out)
        return out

    take = lambda table, first: of_mode([table[first + k : first + k + 1, :] for k in range(MODES)])
    ups, downs = take(index, 0), take(index, MODES)
    up_kinds, down_kinds = take(mirror, 0), take(mirror, MODES)
    real = of_mode([counts[k : k + 1, :] * real_ref[k] for k in range(MODES)])
    imag = of_mode([counts[k : k + 1, :] * imag_ref[k] for k in range(MODES)])
    rates = counts[0:1, :] * rate_ref[0]
    for k in range(1, MODES):
        rates = rates + counts[k : k + 1, :] * rate_ref[k]
    damp[...] = rates

    row, column = iotas(s.extent, s.lanes)
    pick = (row % s.devices == me) & (row // s.devices == column // s.za)
    local_q = lax.dot_general(
        couplings_ref[...],
        pick.astype(F32),
        (((1,), (0,)), ((), ())),
        precision=lax.Precision.HIGHEST,
        preferred_element_type=F32,
    )

    row, column = iotas(depth, wide)
    same = row // s.za % s.fold == column // s.za % s.fold
    source, kind = (row % s.auxes).astype(F32), (row // s.tile).astype(F32)
    from_imag, to_imag = row // s.auxes % 2, column // s.auxes % 2
    up = same & (ups == source) & (up_kinds == kind)
    down = same & (downs == source) & (down_kinds == kind)
    along = jnp.where(up, 1.0, 0.0) + jnp.where(down, real, 0.0)
    cross = jnp.where(down, imag, 0.0)
    along = jnp.where(from_imag == 1, along, -along)
    flip = jnp.where((from_imag == 1) & (row // s.tile == 1), -1.0, 1.0)
    by_row = flip * jnp.where(from_imag == to_imag, cross, along)
    by_column = flip * jnp.where(from_imag == to_imag, cross, -along)

    def pieces(value):
        high = value.astype(BF16)
        return high, (value - high.astype(F32)).astype(BF16)

    for near, far, wa, wb in ((by_row, by_column, wa_s, wb_s), (by_column, by_row, wa_t, wb_t)):
        wb[:depth, :], wb[depth:, :] = pieces(far)
        for th in range(s.tiles):
            lanes = slice(th * s.tile, (th + 1) * s.tile)
            total = local_q[0:1, lanes] * near[:, : s.tile]
            for k in range(1, MODES):
                total = total + local_q[k : k + 1, lanes] * near[:, k * s.tile : (k + 1) * s.tile]
            wa[th, :depth, :], wa[th, depth:, :] = pieces(total)
    for index in range(5):
        stage.send(index)


def even_body(
    s,
    density,
    couplings,
    weight_real,
    weight_imag,
    mode_rates,
    tier_counts,
    link_index,
    link_mirror,
    block_diagonal,
    block_outer,
    block_column,
):
    planes, per_device, band, extent = density.shape
    cube = 2 * extent * extent * s.lanes
    state = shape(extent, s.lanes, dtype=BF16)
    full = shape(extent, s.lanes)
    pair = (shape(s.devices, 2, s.local, s.lanes, dtype=BF16), 2)
    held = pltpu.VMEM((extent, s.lanes), F32)
    held_b = pltpu.VMEM((extent, s.lanes), BF16)

    def exchange(message):
        return lax.all_to_all(message, BOTH, split_axis=0, concat_axis=0, tiled=True)

    blocks = density.reshape(1, planes * per_device, band, extent)
    message = run_staged(
        functools.partial(even_start, s),
        [pair],
        [(blocks, v) for v in range(planes * per_device)] + [tier_counts],
        temporaries=[held_b],
        grant=MOST,
        flops=2 * cube,
    )[0]
    got = exchange(message)

    left, right, left_rows, right_rows = run_staged(
        functools.partial(even_hamiltonian, s),
        [state] * 4,
        [block_diagonal, block_outer],
        temporaries=[held_b],
        scalars=[block_column],
        grant=MOST,
        flops=4 * cube,
    )
    q_first = couplings.T

    k, n = iotas(s.lanes, s.lanes)
    parts = band // s.devices
    row_lanes = (
        n
        == (k // s.local % s.rows * parts + k % parts) * s.za
        + k // (parts * per_device) % planes * s.auxes
        + k // (s.local * s.rows) * per_device
        + k // parts % per_device
    ).astype(BF16)
    column_lanes = (
        n
        == k % s.local * s.za
        + k // (s.local * s.groups * per_device) * s.auxes
        + k // s.local % s.groups * per_device
        + k // (s.local * s.groups) % per_device
    ).astype(BF16)

    k, n = iotas(s.tile, s.tile)
    sign = jnp.where(n // s.auxes % 2 == 0, 1.0, -1.0)
    unit = jnp.where(k // s.za * s.za + (k + s.auxes) % s.za == n, sign, 0.0).astype(BF16)
    wide, size = s.fold * s.tile, max(256, 16 * s.local)
    swap, order = pltpu.VMEM((wide, wide), BF16), pltpu.VMEM((size, size), BF16)

    message, s_now, t_now = run_staged(
        functools.partial(even_take, s),
        [pair, state, state],
        [row_lanes, right_rows, column_lanes, left_rows],
        front=[(got, 0), (got, 1)],
        grant=MOST,
        flops=4 * cube,
    )
    wa = shape(s.tiles, 4 * s.tile, s.tile, dtype=BF16)
    wb = shape(4 * s.tile, MODES * s.tile, dtype=BF16)
    wa_s, wb_s, wa_t, wb_t, damp = run_staged(
        functools.partial(even_weights, s),
        [wa, wb, wa, wb, shape(1, s.lanes)],
        [(got, 1), link_index, link_mirror, couplings],
        scalars=[weight_real, weight_imag, mode_rates],
        grant=MOST,
        flops=cube,
    )
    tables = [unit, damp, q_first, right, wa_s, wb_s, left, wa_t, wb_t]
    shares = [STEP / 6.0, STEP / 3.0, STEP / 3.0, STEP / 6.0]
    steps = [0.25, 0.25, 0.5]
    ratios = [share / step for share, step in zip(shares, steps)]
    got = exchange(message)
    base_s, base_t = run_staged(
        functools.partial(even_first_slope, s, steps[0]),
        [full, full],
        [s_now, t_now] + tables,
        temporaries=[held_b],
        flops=12 * cube,
    )
    total = None
    for section in range(2):
        step = steps[section]
        message = run_staged(
            functools.partial(even_next, s, step),
            [pair],
            [base_s, right_rows, (got, 1), base_t, left_rows],
            temporaries=[held_b, held_b, order, swap],
            front=[(got, 0)],
            flops=5 * cube,
        )[0]
        arrived, got = got, exchange(message)
        less = ratios[2] if section == 1 else 0.0
        base_s, base_t, total = run_staged(
            functools.partial(even_slope, s, step, steps[section + 1], ratios[section], less, total is not None),
            [full, full, full],
            [base_s, base_t, s_now, t_now] + tables + ([] if total is None else [total]),
            temporaries=[held_b, held_b, held_b, held, held, order, swap],
            front=[(arrived, 0), (arrived, 1)],
            flops=15 * cube,
        )
    message = run_staged(
        functools.partial(even_last, s, steps[2], ratios[2], shares[3]),
        [pair],
        [base_t, unit, left, column_lanes, base_s, total, damp, q_first, right, wa_s, wb_s, row_lanes],
        temporaries=[held, held_b, held_b, held_b, held_b, order, swap],
        front=[(got, 1), (got, 0)],
        flops=12 * cube,
    )[0]
    got = exchange(message)
    evolved = run_staged(
        functools.partial(even_finish, s),
        [(shape(1, planes * per_device, band, extent), planes * per_device)],
        [(blocks, v) for v in range(planes * per_device)],
        temporaries=[held_b],
        front=[(got, 0), (got, 1)],
        flops=2 * cube,
    )[0]
    return evolved.reshape(density.shape)


def body(density, *others):
    planes, per_device, band, extent = density.shape
    s = Sizes(lax.axis_size("aux"), lax.axis_size("row"), per_device, band, extent)
    even = band % s.devices == 0 and s.local % 16 == 0 and LANES % s.za == 0
    even = even and s.lanes == extent and planes * per_device * band == extent
    even = even and planes * per_device == MODES and per_device <= s.rows and s.devices <= s.band
    if even:
        return even_body(s, density, *others)
    return general_body(density, *others)


def solution(mesh):
    return jax.shard_map(
        body,
        mesh=mesh,
        in_specs=(
            P(None, "aux", "row", None),
            P(),
            P(),
            P(),
            P(),
            P("aux", None),
            P(),
            P(),
            P(),
            P(),
            P(),
        ),
        out_specs=P(None, "aux", "row", None),
        check_vma=False,
    )
```

```python
import functools

import jax
import jax.numpy as jnp
from jax import lax
from jax.experimental import pallas as pl
from jax.experimental.pallas import tpu as pltpu
from jax.sharding import PartitionSpec as P

MODES = 4
LINKS = 8
LANES = 128
STEP = 0.5
BOTH = ("aux", "row")
GRANT = 52 << 20
MOST = 60 << 20
TAKE = 44 << 20
ROWS = 512

F32 = jnp.float32
BF16 = jnp.bfloat16


class Sizes:
    def __init__(self, groups, rows, per_device, band, extent):
        self.groups, self.rows, self.per_device = groups, rows, per_device
        self.band, self.extent = band, extent
        self.devices = groups * rows
        self.local = band // groups
        self.auxes = per_device * groups
        self.za = 2 * self.auxes
        self.lanes = self.local * self.za
        self.fold = max(1, LANES // self.za)
        self.tile = self.fold * self.za
        self.tiles = self.local // self.fold
        self.joined = self.local % 16 == 0


def dot(a, b, dims=((1,), (0,))):
    return lax.dot_general(a, b, (dims, ((), ())), preferred_element_type=F32)


def run(kernel, outs, args, scratch=(), flops=0, scalars=()):
    spec = pl.BlockSpec(memory_space=pltpu.VMEM)
    flat = pl.BlockSpec(memory_space=pltpu.SMEM)
    moved = sum(a.size * a.dtype.itemsize for a in args)
    moved += sum(o.size * o.dtype.itemsize for o in outs)
    return pl.pallas_call(
        kernel,
        out_shape=list(outs),
        in_specs=[flat if n in scalars else spec for n in range(len(args))],
        out_specs=[spec] * len(outs),
        scratch_shapes=list(scratch),
        compiler_params=pltpu.CompilerParams(vmem_limit_bytes=16 << 20),
        cost_estimate=pl.CostEstimate(flops=flops, bytes_accessed=moved, transcendentals=0),
    )(*args)


def shape(*dims, dtype=F32):
    return jax.ShapeDtypeStruct(dims, dtype)


def one_hot(target, count):
    return (target[:, None] == jnp.arange(count, dtype=jnp.int32)[None, :]).astype(BF16)


def matrix_index(s, index, device):
    group, row = device // s.rows, device % s.rows
    return row * s.band + index * s.groups + group


def row_blocks(extent, size=128):
    return range(0, extent, size)


def send_start_kernel(d_ref, pick_rows, pick_cols, out_ref):
    planes, number, band, extent = d_ref.shape
    flat = d_ref[...].reshape(planes * number * band, extent).astype(BF16)
    for b in row_blocks(flat.shape[0]):
        moved = dot(pick_rows[b : b + 128, :], flat).astype(BF16)
        out_ref[b : b + 128, :] = dot(moved, pick_cols[...]).astype(BF16)


def take_start_kernel(got_ref, pick_lanes, message_rows, s_ref, m_ref):
    for b in row_blocks(got_ref.shape[1]):
        s_ref[b : b + 128, :] = dot(
            got_ref[:, b : b + 128], pick_lanes[...], ((0,), (0,))
        ).astype(BF16)
    for b in row_blocks(m_ref.shape[0]):
        m_ref[b : b + 128, :] = dot(message_rows[b : b + 128, :], s_ref[...]).astype(BF16)


def turn(s, load, order, swap, put):
    size = order.shape[0]
    span = size // s.local
    blocks = s.extent // size
    parts = []
    for block in range(blocks):
        moved = dot(order[...], load(block * size, size))
        for ih in range(s.tiles):
            for jh in range(s.tiles):
                lanes = slice(jh * s.tile, (jh + 1) * s.tile)
                pieces = [
                    moved[(ih * s.fold + f) * span : (ih * s.fold + f + 1) * span, lanes]
                    for f in range(s.fold)
                ]
                parts.append(jnp.concatenate(pieces, axis=1) if s.fold > 1 else pieces[0])
    turned = dot(jnp.concatenate(parts, axis=0).astype(BF16), swap[...])
    for block in range(blocks):
        for ih in range(s.tiles):
            for jh in range(s.tiles):
                start = ((block * s.tiles + ih) * s.tiles + jh) * span
                for f in range(s.fold):
                    first = (jh * s.fold + f) * s.devices + block * span
                    put(
                        slice(first, first + span),
                        slice(ih * s.tile, (ih + 1) * s.tile),
                        turned[start : start + span, f * s.tile : (f + 1) * s.tile],
                    )


def take_columns_kernel(s, got_ref, order, swap, first_rows, left_rows, s_ref, t_ref, *message):
    def put(rows, lanes, value):
        t_ref[rows, lanes] = value.astype(BF16)

    turn(s, lambda start, size: got_ref[start : start + size, :], order, swap, put)
    write_messages(s, first_rows, left_rows, s_ref, t_ref, message)


def write_messages(s, right_rows, left_rows, s_ref, t_ref, message):
    pairs = ((left_rows, t_ref), (right_rows, s_ref))
    if not s.joined and len(message) == 1:
        pairs = pairs[:1]
    both = s.joined and message[0].shape[0] == 2 * s.extent
    for part, (matrix, state) in enumerate(pairs):
        if s.joined and part == 1 and not both:
            continue
        for b in row_blocks(s.extent):
            product = dot(matrix[b : b + 128, :], state[...]).astype(BF16)
            if not s.joined:
                message[part][b : b + 128, :] = product
            elif not both:
                message[0][b : b + 128, :] = product
            else:
                for k in range(128 // s.local):
                    start = ((b // s.local + k) * 2 + part) * s.local
                    message[0][start : start + s.local, :] = product[
                        k * s.local : (k + 1) * s.local, :
                    ]


def slope_kernel(
    s, with_columns, s_ref, t_ref, ys_ref, yt_ref, damp, q_ref, right, left, unit, wa_s, wb_s, wa_t, wb_t, *rest
):
    if with_columns:
        ks_ref, kt_ref, turned = rest
    else:
        ks_ref, turned = rest

    def one(direct, mirror, y_ref, h, wa, wb, out_ref, sign):
        for th in range(s.tiles):
            lanes = slice(th * s.tile, (th + 1) * s.tile)
            turned[:, lanes] = dot(direct[:, lanes], unit[...]).astype(BF16)
        for b in row_blocks(s.extent):
            rows = slice(b, b + 128)
            whole = dot(h[rows, :], turned[...])
            for th in range(s.tiles):
                lanes = slice(th * s.tile, (th + 1) * s.tile)
                source = jnp.concatenate([direct[rows, lanes], mirror[rows, lanes]], axis=1)
                source = jnp.concatenate([source, source], axis=1)
                total = dot(source, wa[th]) - damp[:, lanes] * y_ref[rows, lanes].astype(F32)
                total = total + sign * whole[:, lanes]
                fields = dot(source, wb[...])
                for k in range(MODES):
                    total = total + q_ref[rows, k : k + 1] * fields[:, k * s.tile : (k + 1) * s.tile]
                out_ref[rows, lanes] = total

    one(s_ref, t_ref, ys_ref, right, wa_s, wb_s, ks_ref, -1.0)
    if with_columns:
        one(t_ref, s_ref, yt_ref, left, wa_t, wb_t, kt_ref, 1.0)


def part_loader(s, refs, part):
    def load(start, size):
        if not s.joined:
            return refs[part][start : start + size, :]
        step = s.local
        pieces = []
        for first in range(start, start + size, step):
            at = (first // step * 2 + part) * step
            pieces.append(refs[0][at : at + step, :])
        return jnp.concatenate(pieces, axis=0)

    return load


def next_kernel(s, weight, step, has_total, both, got_count, *refs):
    got = refs[:got_count]
    refs = refs[got_count:]
    order, swap, right_rows, left_rows, ks_ref, kt_ref, ds_ref, dt_ref = refs[:8]
    refs = refs[8:]
    total_in = None
    if has_total:
        total_in, refs = refs[0], refs[1:]
    s_ref, t_ref, ys_ref, yt_ref, total_ref = refs[:5]
    message, arrived = refs[5:-1], refs[-1]

    def put(rows, lanes, value):
        arrived[rows, lanes] = value

    for part in range(2):
        turn(s, part_loader(s, got, part), order, swap, put)
        for b in row_blocks(s.extent, 64):
            rows = slice(b, b + 64)
            if part == 0:
                slope = ks_ref[rows, :] + arrived[rows, :]
                grown = weight * slope
                total_ref[rows, :] = total_in[rows, :] + grown if has_total else grown
                state = ds_ref[rows, :].astype(F32) + step * slope
                ys_ref[rows, :] = state
                s_ref[rows, :] = state.astype(BF16)
            else:
                slope = kt_ref[rows, :] - arrived[rows, :]
                state = dt_ref[rows, :].astype(F32) + step * slope
                yt_ref[rows, :] = state
                t_ref[rows, :] = state.astype(BF16)
    if message:
        write_messages(s, right_rows, left_rows, s_ref, t_ref, message)


def last_kernel(s, weight, got_ref, order, swap, ks_ref, total_in, pick_lanes, out_ref, arrived, grown):
    def put(rows, lanes, value):
        arrived[rows, lanes] = value

    turn(s, lambda start, size: got_ref[start : start + size, :], order, swap, put)
    for b in row_blocks(s.extent, 64):
        rows = slice(b, b + 64)
        change = total_in[rows, :] + weight * (ks_ref[rows, :] + arrived[rows, :])
        grown[rows, :] = change.astype(BF16)
    for b in row_blocks(s.lanes):
        out_ref[b : b + 128, :] = dot(
            pick_lanes[b : b + 128, :], grown[...], ((1,), (1,))
        ).astype(BF16)


def finish_kernel(got_ref, place_rows, place_cols, d_ref, out_ref):
    planes, number, band, extent = d_ref.shape
    for z in range(planes):
        for n in range(number):
            at = (z * number + n) * band
            for b in range(0, band, min(band, 128)):
                size = min(band, 128)
                rows = slice(at + b, at + b + size)
                moved = dot(place_rows[rows, :], got_ref[...]).astype(BF16)
                out_ref[z, n, b : b + size, :] = d_ref[z, n, b : b + size, :] + dot(
                    moved, place_cols[...]
                )


def link_matrices(s, counts, weight_real, weight_imag, link_index, link_mirror):
    ones = jnp.ones_like(counts)
    real = jnp.stack([ones, counts * weight_real[None, :]], 1)
    imag = jnp.stack([jnp.zeros_like(counts), counts * weight_imag[None, :]], 1)
    index = link_index.reshape(s.auxes, 2, MODES)
    mirror = link_mirror.reshape(s.auxes, 2, MODES)
    source = jnp.arange(s.auxes, dtype=jnp.int32)
    hit = index[None] == source[:, None, None, None]
    kinds = jnp.stack([hit & (mirror[None] == 0), hit & (mirror[None] == 1)]).astype(F32)
    along = jnp.sum(kinds * real, 3)
    cross = jnp.sum(kinds * imag, 3)
    along, cross = (jnp.transpose(m, (0, 3, 1, 2)) for m in (along, cross))
    flip = jnp.array([1.0, -1.0], F32).reshape(2, 1, 1, 1)

    def build(sign):
        upper = jnp.concatenate([cross, -sign * along], 3)
        lower = jnp.concatenate([sign * along, cross], 3) * flip
        return jnp.concatenate([upper, lower], 2)

    return build(1.0), build(-1.0)


def two_pieces(weights, axis):
    high = lax.reduce_precision(weights, 8, 7)
    low = weights - high
    return jnp.concatenate([high.astype(BF16), low.astype(BF16)], axis)


def coupling_weights(s, by_local, by_first, local_q):
    eye = jnp.eye(s.fold, dtype=F32)
    near = jnp.einsum("ki,xkuv->ixuv", local_q, by_local, precision=lax.Precision.HIGHEST)
    near = near.reshape(s.tiles, s.fold, 2, s.za, s.za)
    near = jnp.transpose(near, (0, 2, 1, 3, 4))[:, :, :, :, None, :] * eye[None, None, :, None, :, None]
    near = near.reshape(s.tiles, 2 * s.tile, s.tile)
    far = jnp.transpose(by_first, (0, 2, 1, 3))[:, None, :, :, None, :] * eye[None, :, None, None, :, None]
    far = far.reshape(2 * s.tile, MODES * s.tile)
    return two_pieces(near, 1), two_pieces(far, 0)


def general_body(
    density,
    couplings,
    weight_real,
    weight_imag,
    mode_rates,
    tier_counts,
    link_index,
    link_mirror,
    block_diagonal,
    block_outer,
    block_column,
):
    planes, per_device, band, extent = density.shape
    s = Sizes(lax.axis_size("aux"), lax.axis_size("row"), per_device, band, extent)
    blocks, block = block_diagonal.shape[0], block_diagonal.shape[1]
    group, row = lax.axis_index("aux"), lax.axis_index("row")
    device = group * s.rows + row
    cube = 2 * extent * extent * s.lanes

    number = jnp.arange(extent, dtype=jnp.int32)
    first_to_matrix = matrix_index(s, number // s.devices, number % s.devices)
    posted_to_matrix = matrix_index(s, number % s.local, number // s.local)
    posted_to_first = number % s.local * s.devices + number // s.local

    wide = jnp.arange(s.lanes, dtype=jnp.int32)
    sub = planes * per_device * s.local
    start_source = wide % sub * s.groups + wide // sub
    pick_rows = one_hot(start_source, s.lanes)
    pick_cols = one_hot(first_to_matrix, extent).T
    lane_of = (
        wide % s.local * s.za
        + wide // (per_device * s.local) % planes * s.auxes
        + wide // sub * per_device
        + wide // s.local % per_device
    )
    pick_lanes = one_hot(lane_of, s.lanes)
    message_rows = one_hot(posted_to_first, extent)
    start_message = run(
        send_start_kernel,
        [shape(s.lanes, extent, dtype=BF16)],
        [density, pick_rows, pick_cols],
        flops=2 * cube,
    )[0]
    start_got = lax.all_to_all(
        start_message.reshape(s.groups, sub, extent), "aux", split_axis=0, concat_axis=0, tiled=True
    ).reshape(s.lanes, extent)

    selector = block_column[:, None] == jnp.arange(blocks, dtype=jnp.int32)[None, :]
    own = jnp.eye(blocks, dtype=F32)
    whole_h = (
        own[:, None, :, None] * block_diagonal.astype(F32)[:, :, None, :]
        + selector.astype(F32)[:, None, :, None] * block_outer.astype(F32)[:, :, None, :]
    ).reshape(extent, extent).astype(BF16)
    first_h = one_hot(first_to_matrix, extent)
    left = jnp.dot(
        jnp.dot(first_h, whole_h, preferred_element_type=BF16), first_h.T, preferred_element_type=BF16
    )
    right = left.T
    left_rows = jnp.dot(message_rows, left, preferred_element_type=BF16)
    right_rows = jnp.dot(message_rows, right, preferred_element_type=BF16)

    counts = lax.all_gather(tier_counts, "aux", axis=0, tiled=True).astype(F32)
    damping = jnp.sum(counts * mode_rates[None, :], axis=1)
    damp = jnp.tile(damping, (planes * s.local,))[None, :]
    q_first = jnp.dot(
        couplings, first_h.T.astype(F32), precision=lax.Precision.HIGHEST
    ).T
    local_pick = (matrix_index(s, jnp.arange(s.local, dtype=jnp.int32), device)[None, :] == number[:, None])
    local_q = jnp.dot(couplings, local_pick.astype(F32), precision=lax.Precision.HIGHEST)
    by_row, by_column = link_matrices(s, counts, weight_real, weight_imag, link_index, link_mirror)
    wa_s, wb_s = coupling_weights(s, by_row, by_column, local_q)
    wa_t, wb_t = coupling_weights(s, by_column, by_row, local_q)

    lane = jnp.arange(s.za, dtype=jnp.int32)
    unit = jnp.where(
        lane[:, None] == (lane[None, :] + s.auxes) % s.za,
        jnp.where(lane[None, :] < s.auxes, 1.0, -1.0),
        0.0,
    )
    eye_fold = jnp.eye(s.fold, dtype=F32)
    unit_tile = (eye_fold[:, None, :, None] * unit[None, :, None, :]).reshape(s.tile, s.tile).astype(BF16)
    swap = (
        eye_fold[:, None, None, None, :, None]
        * eye_fold[None, :, None, :, None, None]
        * unit[None, None, :, None, None, :]
    ).reshape(s.fold * s.tile, s.fold * s.tile).astype(BF16)
    keep = (
        eye_fold[:, None, None, None, :, None]
        * eye_fold[None, :, None, :, None, None]
        * jnp.eye(s.za, dtype=F32)[None, None, :, None, None, :]
    ).reshape(s.fold * s.tile, s.fold * s.tile).astype(BF16)
    size = min(extent, max(256, 16 * s.local))
    span = size // s.local
    at = jnp.arange(size, dtype=jnp.int32)
    order = one_hot(at % span * s.local + at // span, size)

    state = shape(extent, s.lanes, dtype=BF16)
    full = shape(extent, s.lanes)
    held = pltpu.VMEM((extent, s.lanes), F32)
    held_b = pltpu.VMEM((extent, s.lanes), BF16)

    def exchange(messages):
        parts = [m.reshape(s.devices, -1, s.lanes) for m in messages]
        sent = parts[0] if len(parts) == 1 else jnp.concatenate(parts, 1)
        got = lax.all_to_all(sent, BOTH, split_axis=0, concat_axis=0, tiled=True)
        if len(parts) == 1:
            return [got.reshape(-1, s.lanes)]
        height = s.local
        return [got[:, p * height : (p + 1) * height].reshape(-1, s.lanes) for p in range(2)]

    if s.joined:
        pair = [shape(2 * extent, s.lanes, dtype=BF16)]
    else:
        pair = [state, state]

    s_now, posted = run(
        take_start_kernel, [state, state], [start_got, pick_lanes, message_rows], flops=2 * cube
    )
    got = exchange([posted])
    t_now, *messages = run(
        functools.partial(take_columns_kernel, s),
        [state] + pair,
        [got[0], order, keep, right_rows, left_rows, s_now],
        flops=4 * cube,
    )
    start_s, start_t = s_now, t_now
    ys, yt = s_now, t_now
    total = None
    shares = [STEP / 6.0, STEP / 3.0, STEP / 3.0, STEP / 6.0]
    steps = [0.25, 0.25, 0.5]
    for section in range(4):
        got = exchange(messages)
        columns = section < 3
        slopes = run(
            functools.partial(slope_kernel, s, columns),
            [full, full] if columns else [full],
            [s_now, t_now, ys, yt, damp, q_first, right, left, unit_tile, wa_s, wb_s, wa_t, wb_t],
            scratch=[held_b],
            flops=(12 if columns else 6) * cube,
        )
        if columns:
            args = list(got) + [order, swap, right_rows, left_rows, *slopes, start_s, start_t]
            if total is not None:
                args.append(total)
            outs = [state, state, full, full, full]
            outs += pair if section < 2 else [state]
            s_now, t_now, ys, yt, total, *messages = run(
                functools.partial(
                    next_kernel, s, shares[section], steps[section], total is not None, section < 2, len(got)
                ),
                outs,
                args,
                scratch=[held],
                flops=6 * cube,
            )
    change = run(
        functools.partial(last_kernel, s, shares[3]),
        [shape(s.lanes, extent, dtype=BF16)],
        [got[0], order, swap, slopes[0], total, pick_lanes],
        scratch=[held, held_b],
        flops=3 * cube,
    )[0]
    back = lax.all_to_all(
        change.reshape(s.groups, sub, extent), "aux", split_axis=0, concat_axis=0, tiled=True
    ).reshape(s.lanes, extent)
    return run(
        finish_kernel,
        [shape(planes, per_device, band, extent)],
        [back, pick_rows.T, pick_cols.T, density],
        flops=2 * cube,
    )[0]


def iotas(rows, columns):
    return (
        lax.broadcasted_iota(jnp.int32, (rows, columns), 0),
        lax.broadcasted_iota(jnp.int32, (rows, columns), 1),
    )


def mask_to(value):
    return value.astype(F32).astype(BF16)


def post_matrix(s):
    row, column = iotas(s.extent, s.extent)
    return mask_to(column == row % s.local * s.devices + row // s.local)


class Stage:
    def __init__(self, sources, buffers, targets, results, semaphores, offset, lead):
        self.buffers, self.results, self.targets = buffers, results, targets
        self.semaphores, self.next, self.offset = semaphores, 0, offset
        self.sources, self.lead = sources, lead
        self.coming = [self.copy(a, b) for a, b in zip(sources[:lead], buffers)]
        self.going = []

    def copy(self, source, target):
        made = pltpu.make_async_copy(source, target, self.semaphores.at[self.next])
        self.next += 1
        made.start()
        return made

    def front(self, index):
        return self.need(index - self.offset)

    def need(self, index):
        index += self.offset
        if index >= len(self.coming):
            self.start_rest()
        if self.coming[index] is not None:
            self.coming[index].wait()
            self.coming[index] = None
        return self.buffers[index]

    def start_rest(self):
        known = len(self.coming)
        self.coming += [self.copy(a, b) for a, b in zip(self.sources[known:], self.buffers[known:])]

    def send(self, index):
        self.going.append(self.copy(self.results[index], self.targets[index]))

    def finish(self):
        for made in self.going:
            made.wait()


def run_staged(body, outs, args, temporaries=(), scalars=(), front=(), lead=None, grant=GRANT, flops=0):
    arrays, views = [], []
    for arg in [*front, *args]:
        array, part = arg if isinstance(arg, tuple) else (arg, None)
        if not any(array is a for a in arrays):
            arrays.append(array)
        views.append(([array is a for a in arrays].index(True), part))
    shapes, places = [], []
    for out in outs:
        if isinstance(out, tuple):
            for part in range(out[1]):
                places.append((len(shapes), part))
            shapes.append(out[0])
        else:
            places.append((len(shapes), None))
            shapes.append(out)
    tall = lambda x, part: x.shape if part is None else x.shape[:1] + x.shape[2:]
    buffers = [pltpu.VMEM(tall(arrays[k], part), arrays[k].dtype) for k, part in views]
    results = [pltpu.VMEM(tall(shapes[k], part), shapes[k].dtype) for k, part in places]
    count = len(buffers) + len(results)

    def kernel(*refs):
        small, refs = refs[: len(scalars)], refs[len(scalars) :]
        source, refs = refs[: len(arrays)], refs[len(arrays) :]
        target, refs = refs[: len(shapes)], refs[len(shapes) :]
        own, refs = refs[: len(buffers)], refs[len(buffers) :]
        made, refs = refs[: len(results)], refs[len(results) :]
        pick = lambda ref, part: ref if part is None else ref.at[:, part]
        stage = Stage(
            [pick(source[k], part) for k, part in views],
            own,
            [pick(target[k], part) for k, part in places],
            made,
            refs[-1],
            len(front),
            len(views) if lead is None else lead,
        )
        body(stage, small, refs[:-1])
        stage.finish()

    moved = sum(a.size * a.dtype.itemsize for a in arrays)
    moved += sum(o.size * o.dtype.itemsize for o in shapes)
    far = pl.BlockSpec(memory_space=pltpu.HBM)
    return pl.pallas_call(
        kernel,
        out_shape=shapes,
        in_specs=[pl.BlockSpec(memory_space=pltpu.SMEM)] * len(scalars) + [far] * len(arrays),
        out_specs=[far] * len(shapes),
        scratch_shapes=buffers + results + list(temporaries) + [pltpu.SemaphoreType.DMA((count,))],
        compiler_params=pltpu.CompilerParams(vmem_limit_bytes=grant),
        cost_estimate=pl.CostEstimate(flops=flops, bytes_accessed=moved, transcendentals=0),
    )(*scalars, *arrays)


def fill(s, result, first, value, lanes=slice(None)):
    count = value.shape[0] // s.local
    device = first // s.local
    result[device : device + count, :, lanes] = value.reshape(count, s.local, value.shape[1])


def flat_rows(ref, rows, lanes=slice(None)):
    piece = ref[rows, :, lanes]
    return piece.reshape(piece.shape[0] * piece.shape[1], piece.shape[2])


def even_start(s, stage, small, temporaries):
    (post,) = temporaries
    post[...] = post_matrix(s)
    blocks = s.extent // s.band
    which = lax.axis_index("row") % s.per_device
    flats = [stage.need(v)[...].reshape(s.band, s.extent).astype(BF16) for v in range(blocks)]
    row, lane = iotas(ROWS, s.band)
    counts = stage.need(blocks)[...].astype(F32)
    mine = counts[0:1, :]
    for n in range(1, s.per_device):
        mine = jnp.where(which == n, counts[n : n + 1, :], mine)
    for v in range(blocks):
        count = mine[:, v : v + 1]
        for b in row_blocks(s.extent, ROWS):
            value = dot(post[b : b + ROWS, :], flats[v], ((1,), (1,)))
            own = (row % s.local == 0) & (lane == (row + b) // s.local)
            value = jnp.where(own, count, value).astype(BF16)
            fill(s, stage.results[1], b, value, slice(v * s.band, (v + 1) * s.band))
    stage.send(1)
    flat = jnp.concatenate(flats, axis=0)
    for b in row_blocks(s.extent, ROWS):
        fill(s, stage.results[0], b, dot(post[b : b + ROWS, :], flat).astype(BF16))
    stage.send(0)


def send_products(s, stage, matrix, state_ref, index):
    for b in row_blocks(s.extent, ROWS):
        fill(s, stage.results[index], b, dot(matrix[b : b + ROWS, :], state_ref[...]).astype(BF16))
    stage.send(index)


def take_rows(s, rows_in, row_lanes, s_ref):
    rows = flat_rows(rows_in, slice(0, s.devices))
    s_ref[...] = dot(rows, row_lanes[...], ((0,), (0,))).astype(BF16)


def take_columns(s, columns_in, column_lanes, s_ref, t_ref):
    me = lax.axis_index("aux") * s.rows + lax.axis_index("row")
    blocks = s.extent // s.band
    parts = s.band // s.devices
    row, lane = iotas(s.devices, s.tile)
    mine = (row == me) & (lane < s.za)
    bands = []
    for q in range(s.rows):
        pieces = []
        for v in range(blocks):
            for g in range(s.groups):
                pieces.append(columns_in[g * s.rows + q, :, v * s.band : (v + 1) * s.band])
        bands.append(jnp.concatenate(pieces, axis=0))
    t_ref[...] = dot(jnp.concatenate(bands, axis=1), column_lanes[...], ((0,), (0,))).astype(BF16)
    for q in range(s.rows):
        rows = slice(q * s.band, q * s.band + s.devices)
        first = q * parts * s.za
        kept = s_ref[: s.devices, first : first + s.tile].astype(F32)
        t_ref[rows, : s.tile] = jnp.where(mine, kept, t_ref[rows, : s.tile].astype(F32)).astype(BF16)


def even_take(s, stage, small, temporaries):
    s_ref, t_ref = temporaries
    take_rows(s, stage.front(0), stage.need(0), s_ref)
    send_products(s, stage, stage.need(1), s_ref, 1)
    take_columns(s, stage.front(1), stage.need(2), s_ref, t_ref)
    send_products(s, stage, stage.need(3), t_ref, 0)


def turn_matrices(s, order, swap):
    size = order.shape[0]
    span = size // s.local
    k, n = lax.broadcasted_iota(jnp.int32, (size, 1), 0), lax.broadcasted_iota(jnp.int32, (1, size), 1)
    order[...] = mask_to(n == k % span * s.local + k // span)
    wide = s.fold * s.tile
    k, n = lax.broadcasted_iota(jnp.int32, (wide, 1), 0), lax.broadcasted_iota(jnp.int32, (1, wide), 1)
    sign = jnp.where(n // s.auxes % 2 == 0, 1.0, -1.0)
    there = (k // s.za % s.fold * s.fold + k // s.tile) * s.za + (k + s.auxes) % s.za
    swap[...] = jnp.where(there == n, sign, 0.0).astype(BF16)


def even_turn(s, got, order, swap, put):
    def load(start, size):
        return flat_rows(got, slice(start // s.local, (start + size) // s.local))

    turn(s, load, order, swap, put)


def updates(scale, base_ref, keep):
    def put(rows, lanes, value):
        keep(rows, lanes, base_ref[rows, lanes] + scale * value)

    return put


def even_next(s, step, stage, small, temporaries):
    s_ref, t_ref, order, swap = temporaries
    turn_matrices(s, order, swap)

    def keep_in(ref):
        def keep(rows, lanes, value):
            ref[rows, lanes] = value.astype(BF16)

        return keep

    got = stage.front(0)
    stage.start_rest()
    even_turn(s, got, order, swap, updates(step, stage.need(0), keep_in(s_ref)))
    send_products(s, stage, stage.need(1), s_ref, 1)
    got = stage.need(2)
    even_turn(s, got, order, swap, updates(-step, stage.need(3), keep_in(t_ref)))
    send_products(s, stage, stage.need(4), t_ref, 0)


def even_slope_part(s, direct, mirror, y_ref, h, unit, damp, q_ref, wa, wb, turned, sign, put):
    factors = [jnp.broadcast_to(q_ref[:, k : k + 1], (s.extent, s.tile)) for k in range(MODES)]
    for th in range(s.tiles):
        lanes = slice(th * s.tile, (th + 1) * s.tile)
        turned[:, lanes] = dot(direct[:, lanes], unit[...]).astype(BF16)
    for b in row_blocks(s.extent, ROWS):
        rows = slice(b, b + ROWS)
        whole = dot(h[rows, :], turned[...])
        for th in range(s.tiles):
            lanes = slice(th * s.tile, (th + 1) * s.tile)
            source = jnp.concatenate([direct[rows, lanes], mirror[rows, lanes]], axis=1)
            source = jnp.concatenate([source, source], axis=1)
            total = dot(source, wa[th]) - damp[:, lanes] * y_ref[rows, lanes].astype(F32)
            total = total + sign * whole[:, lanes]
            fields = dot(source, wb[...])
            for k in range(MODES):
                total = total + factors[k][rows, :] * fields[:, k * s.tile : (k + 1) * s.tile]
            put(rows, lanes, total)


def put_base(ref, start_ref, step):
    def put(rows, lanes, value):
        ref[rows, lanes] = start_ref[rows, lanes].astype(F32) + step * value

    return put


def even_first_slope(s, step, stage, small, temporaries):
    (turned,) = temporaries
    need = stage.need
    first, second, s_ref, t_ref = stage.results
    take_rows(s, stage.front(0), need(0), s_ref)
    stage.send(2)
    take_columns(s, stage.front(1), need(1), s_ref, t_ref)
    stage.send(3)
    unit, damp, q_ref = need(2), need(3), need(4)
    put = put_base(first, s_ref, step)
    even_slope_part(s, s_ref, t_ref, s_ref, need(5), unit, damp, q_ref, need(6), need(7), turned, -1.0, put)
    stage.send(0)
    put = put_base(second, t_ref, step)
    even_slope_part(s, t_ref, s_ref, t_ref, need(8), unit, damp, q_ref, need(9), need(10), turned, 1.0, put)
    stage.send(1)


def even_slope(s, step, next_step, ratio, less, has_total, stage, small, temporaries):
    turned, s_ref, t_ref, ys_ref, yt_ref, order, swap = temporaries
    turn_matrices(s, order, swap)
    need = stage.need
    first, second, total_ref = stage.results

    def keep_in(ref, exact):
        def keep(rows, lanes, value):
            exact[rows, lanes] = value
            ref[rows, lanes] = value.astype(BF16)

        return keep

    even_turn(s, stage.front(0), order, swap, updates(step, need(0), keep_in(s_ref, ys_ref)))
    even_turn(s, stage.front(1), order, swap, updates(-step, need(1), keep_in(t_ref, yt_ref)))
    ds_ref, dt_ref = need(2), need(3)
    total_in = need(13) if has_total else None
    for b in row_blocks(s.extent, 64):
        rows = slice(b, b + 64)
        grown = ratio * ys_ref[rows, :] - (ratio + less) * ds_ref[rows, :].astype(F32)
        total_ref[rows, :] = total_in[rows, :] + grown if has_total else grown
    stage.send(2)
    unit, damp, q_ref = need(4), need(5), need(6)
    put = put_base(first, ds_ref, next_step)
    even_slope_part(s, s_ref, t_ref, ys_ref, need(7), unit, damp, q_ref, need(8), need(9), turned, -1.0, put)
    stage.send(0)
    put = put_base(second, dt_ref, next_step)
    even_slope_part(s, t_ref, s_ref, yt_ref, need(10), unit, damp, q_ref, need(11), need(12), turned, 1.0, put)
    stage.send(1)


def even_last(s, step, ratio, weight, stage, small, temporaries):
    ys_ref, s_ref, t_ref, grown, turned, order, swap = temporaries
    turn_matrices(s, order, swap)
    need = stage.need

    def keep_columns(rows, lanes, value):
        t_ref[rows, lanes] = value.astype(BF16)

    got = stage.front(0)
    stage.start_rest()
    even_turn(s, got, order, swap, updates(-step, need(0), keep_columns))
    unit, left, column_lanes = need(1), need(2), need(3)
    for th in range(s.tiles):
        lanes = slice(th * s.tile, (th + 1) * s.tile)
        turned[:, lanes] = dot(t_ref[:, lanes], unit[...]).astype(BF16)
    for b in row_blocks(s.extent, ROWS):
        rows = slice(b, b + ROWS)
        grown[rows, :] = (weight * dot(left[rows, :], turned[...])).astype(BF16)
    out = stage.results[1]
    value = dot(column_lanes[...], grown[...], ((1,), (1,))).astype(BF16)
    for q in range(s.rows):
        for v in range(s.extent // s.band):
            for g in range(s.groups):
                at = (v * s.groups + g) * s.local
                piece = value[at : at + s.local, q * s.band : (q + 1) * s.band]
                out[g * s.rows + q, :, v * s.band : (v + 1) * s.band] = piece
    stage.send(1)

    def keep_rows(rows, lanes, value):
        ys_ref[rows, lanes] = value
        s_ref[rows, lanes] = value.astype(BF16)

    even_turn(s, stage.front(1), order, swap, updates(step, need(4), keep_rows))
    total_in = need(5)

    def put_change(rows, lanes, value):
        change = total_in[rows, lanes] + ratio * ys_ref[rows, lanes]
        grown[rows, lanes] = (change + weight * value).astype(BF16)

    even_slope_part(
        s, s_ref, t_ref, ys_ref, need(8), unit, need(6), need(7), need(9), need(10), turned, -1.0, put_change
    )
    row_lanes = need(11)
    for b in row_blocks(s.extent, ROWS):
        fill(s, stage.results[0], b, dot(row_lanes[b : b + ROWS, :], grown[...], ((1,), (1,))).astype(BF16))
    stage.send(0)


def even_finish(s, stage, small, temporaries):
    (post,) = temporaries
    post[...] = post_matrix(s)
    everyone = slice(0, s.devices)
    change = dot(post[...], flat_rows(stage.front(0), everyone), ((0,), (0,)))
    change = change + dot(flat_rows(stage.front(1), everyone), post[...], ((0,), (0,)))
    for v in range(s.extent // s.band):
        rows = slice(v * s.band, (v + 1) * s.band)
        stage.results[v][...] = (stage.need(v)[...].reshape(s.band, s.extent) + change[rows, :]).reshape(
            stage.results[v].shape
        )
        stage.send(v)


def even_hamiltonian(s, stage, small, temporaries):
    (where_ref,) = small
    (post,) = temporaries
    left, right, left_rows, right_rows = stage.results
    own_ref, outer_ref = stage.need(0), stage.need(1)
    blocks, block = own_ref.shape[0], own_ref.shape[1]
    post[...] = post_matrix(s)
    row, column = iotas(block, s.extent)
    for b in range(blocks):
        spread = column - row
        to_own = mask_to(spread == b * block)
        to_far = mask_to(spread == where_ref[b] * block)
        left[b * block : (b + 1) * block, :] = (dot(own_ref[b], to_own) + dot(outer_ref[b], to_far)).astype(BF16)
    row, column = iotas(s.extent, s.extent)
    same = mask_to(row == column)
    for b in row_blocks(s.extent, ROWS):
        rows = slice(b, b + ROWS)
        right[rows, :] = dot(same[rows, :], left[...], ((1,), (1,))).astype(BF16)
        left_rows[rows, :] = dot(post[rows, :], left[...]).astype(BF16)
        right_rows[rows, :] = dot(post[rows, :], left[...], ((1,), (1,))).astype(BF16)
    for index in range(4):
        stage.send(index)


def even_weights(s, stage, small, temporaries):
    real_ref, imag_ref, rate_ref = small
    wa_s, wb_s, wa_t, wb_t, damp = stage.results
    columns_in, index_ref, mirror_ref, couplings_ref = [stage.need(k) for k in range(4)]
    me = lax.axis_index("aux") * s.rows + lax.axis_index("row")
    depth, wide = 2 * s.tile, MODES * s.tile
    row, column = iotas(s.auxes, wide)
    by_lane = mask_to(column % s.auxes == row)

    def spread(table):
        return dot(table.astype(F32).astype(BF16), by_lane, ((0,), (0,)))

    row, lane = iotas(s.extent, MODES)
    gather = mask_to(row == lane * s.band + me)
    row, lane = iotas(s.auxes, s.auxes * s.local)
    wanted = mask_to(lane == row * s.local)
    pieces = [columns_in[a // s.per_device * s.rows + a % s.per_device] for a in range(s.auxes)]
    counts = spread(dot(wanted, dot(jnp.concatenate(pieces, axis=0), gather).astype(BF16)))
    index, mirror = spread(index_ref[...]), spread(mirror_ref[...])
    lane_mode = lax.broadcasted_iota(jnp.int32, (1, wide), 1) // s.tile

    def of_mode(values):
        out = values[0]
        for k in range(1, MODES):
            out = jnp.where(lane_mode == k, values[k], out)
        return out

    take = lambda table, first: of_mode([table[first + k : first + k + 1, :] for k in range(MODES)])
    ups, downs = take(index, 0), take(index, MODES)
    up_kinds, down_kinds = take(mirror, 0), take(mirror, MODES)
    real = of_mode([counts[k : k + 1, :] * real_ref[k] for k in range(MODES)])
    imag = of_mode([counts[k : k + 1, :] * imag_ref[k] for k in range(MODES)])
    rates = counts[0:1, :] * rate_ref[0]
    for k in range(1, MODES):
        rates = rates + counts[k : k + 1, :] * rate_ref[k]
    damp[...] = rates

    row, column = iotas(s.extent, s.lanes)
    pick = (row % s.devices == me) & (row // s.devices == column // s.za)
    local_q = lax.dot_general(
        couplings_ref[...],
        pick.astype(F32),
        (((1,), (0,)), ((), ())),
        precision=lax.Precision.HIGHEST,
        preferred_element_type=F32,
    )

    row, column = iotas(depth, wide)
    same = row // s.za % s.fold == column // s.za % s.fold
    source, kind = (row % s.auxes).astype(F32), (row // s.tile).astype(F32)
    from_imag, to_imag = row // s.auxes % 2, column // s.auxes % 2
    up = same & (ups == source) & (up_kinds == kind)
    down = same & (downs == source) & (down_kinds == kind)
    along = jnp.where(up, 1.0, 0.0) + jnp.where(down, real, 0.0)
    cross = jnp.where(down, imag, 0.0)
    along = jnp.where(from_imag == 1, along, -along)
    flip = jnp.where((from_imag == 1) & (row // s.tile == 1), -1.0, 1.0)
    by_row = flip * jnp.where(from_imag == to_imag, cross, along)
    by_column = flip * jnp.where(from_imag == to_imag, cross, -along)

    def pieces(value):
        high = value.astype(BF16)
        return high, (value - high.astype(F32)).astype(BF16)

    for near, far, wa, wb in ((by_row, by_column, wa_s, wb_s), (by_column, by_row, wa_t, wb_t)):
        wb[:depth, :], wb[depth:, :] = pieces(far)
        for th in range(s.tiles):
            lanes = slice(th * s.tile, (th + 1) * s.tile)
            total = local_q[0:1, lanes] * near[:, : s.tile]
            for k in range(1, MODES):
                total = total + local_q[k : k + 1, lanes] * near[:, k * s.tile : (k + 1) * s.tile]
            wa[th, :depth, :], wa[th, depth:, :] = pieces(total)
    for index in range(5):
        stage.send(index)


def even_body(
    s,
    density,
    couplings,
    weight_real,
    weight_imag,
    mode_rates,
    tier_counts,
    link_index,
    link_mirror,
    block_diagonal,
    block_outer,
    block_column,
):
    planes, per_device, band, extent = density.shape
    cube = 2 * extent * extent * s.lanes
    state = shape(extent, s.lanes, dtype=BF16)
    full = shape(extent, s.lanes)
    pair = (shape(s.devices, 2, s.local, s.lanes, dtype=BF16), 2)
    held = pltpu.VMEM((extent, s.lanes), F32)
    held_b = pltpu.VMEM((extent, s.lanes), BF16)

    def exchange(message):
        return lax.all_to_all(message, BOTH, split_axis=0, concat_axis=0, tiled=True)

    blocks = density.reshape(1, planes * per_device, band, extent)
    message = run_staged(
        functools.partial(even_start, s),
        [pair],
        [(blocks, v) for v in range(planes * per_device)] + [tier_counts],
        temporaries=[held_b],
        grant=MOST,
        flops=2 * cube,
    )[0]
    got = exchange(message)

    left, right, left_rows, right_rows = run_staged(
        functools.partial(even_hamiltonian, s),
        [state] * 4,
        [block_diagonal, block_outer],
        temporaries=[held_b],
        scalars=[block_column],
        grant=MOST,
        flops=4 * cube,
    )
    q_first = couplings.T

    k, n = iotas(s.lanes, s.lanes)
    parts = band // s.devices
    row_lanes = (
        n
        == (k // s.local % s.rows * parts + k % parts) * s.za
        + k // (parts * per_device) % planes * s.auxes
        + k // (s.local * s.rows) * per_device
        + k // parts % per_device
    ).astype(BF16)
    column_lanes = (
        n
        == k % s.local * s.za
        + k // (s.local * s.groups * per_device) * s.auxes
        + k // s.local % s.groups * per_device
        + k // (s.local * s.groups) % per_device
    ).astype(BF16)

    k, n = iotas(s.tile, s.tile)
    sign = jnp.where(n // s.auxes % 2 == 0, 1.0, -1.0)
    unit = jnp.where(k // s.za * s.za + (k + s.auxes) % s.za == n, sign, 0.0).astype(BF16)
    wide, size = s.fold * s.tile, max(256, 16 * s.local)
    swap, order = pltpu.VMEM((wide, wide), BF16), pltpu.VMEM((size, size), BF16)

    message = run_staged(
        functools.partial(even_take, s),
        [pair],
        [row_lanes, right_rows, column_lanes, left_rows],
        temporaries=[held_b, held_b],
        front=[(got, 0), (got, 1)],
        grant=TAKE,
        flops=4 * cube,
    )[0]
    wa = shape(s.tiles, 4 * s.tile, s.tile, dtype=BF16)
    wb = shape(4 * s.tile, MODES * s.tile, dtype=BF16)
    wa_s, wb_s, wa_t, wb_t, damp = run_staged(
        functools.partial(even_weights, s),
        [wa, wb, wa, wb, shape(1, s.lanes)],
        [(got, 1), link_index, link_mirror, couplings],
        scalars=[weight_real, weight_imag, mode_rates],
        grant=MOST,
        flops=cube,
    )
    tables = [unit, damp, q_first, right, wa_s, wb_s, left, wa_t, wb_t]
    shares = [STEP / 6.0, STEP / 3.0, STEP / 3.0, STEP / 6.0]
    steps = [0.25, 0.25, 0.5]
    ratios = [share / step for share, step in zip(shares, steps)]
    begun, got = got, exchange(message)
    base_s, base_t, s_now, t_now = run_staged(
        functools.partial(even_first_slope, s, steps[0]),
        [full, full, state, state],
        [row_lanes, column_lanes] + tables,
        temporaries=[held_b],
        front=[(begun, 0), (begun, 1)],
        flops=12 * cube,
    )
    total = None
    for section in range(2):
        step = steps[section]
        message = run_staged(
            functools.partial(even_next, s, step),
            [pair],
            [base_s, right_rows, (got, 1), base_t, left_rows],
            temporaries=[held_b, held_b, order, swap],
            front=[(got, 0)],
            flops=5 * cube,
        )[0]
        arrived, got = got, exchange(message)
        less = ratios[2] if section == 1 else 0.0
        base_s, base_t, total = run_staged(
            functools.partial(even_slope, s, step, steps[section + 1], ratios[section], less, total is not None),
            [full, full, full],
            [base_s, base_t, s_now, t_now] + tables + ([] if total is None else [total]),
            temporaries=[held_b, held_b, held_b, held, held, order, swap],
            front=[(arrived, 0), (arrived, 1)],
            flops=15 * cube,
        )
    message = run_staged(
        functools.partial(even_last, s, steps[2], ratios[2], shares[3]),
        [pair],
        [base_t, unit, left, column_lanes, base_s, total, damp, q_first, right, wa_s, wb_s, row_lanes],
        temporaries=[held, held_b, held_b, held_b, held_b, order, swap],
        front=[(got, 1), (got, 0)],
        flops=12 * cube,
    )[0]
    got = exchange(message)
    evolved = run_staged(
        functools.partial(even_finish, s),
        [(shape(1, planes * per_device, band, extent), planes * per_device)],
        [(blocks, v) for v in range(planes * per_device)],
        temporaries=[held_b],
        front=[(got, 0), (got, 1)],
        flops=2 * cube,
    )[0]
    return evolved.reshape(density.shape)


def body(density, *others):
    planes, per_device, band, extent = density.shape
    s = Sizes(lax.axis_size("aux"), lax.axis_size("row"), per_device, band, extent)
    even = band % s.devices == 0 and s.local % 16 == 0 and LANES % s.za == 0
    even = even and s.lanes == extent and planes * per_device * band == extent
    even = even and planes * per_device == MODES and per_device <= s.rows and s.devices <= s.band
    if even:
        return even_body(s, density, *others)
    return general_body(density, *others)


def solution(mesh):
    return jax.shard_map(
        body,
        mesh=mesh,
        in_specs=(
            P(None, "aux", "row", None),
            P(),
            P(),
            P(),
            P(),
            P("aux", None),
            P(),
            P(),
            P(),
            P(),
            P(),
        ),
        out_specs=P(None, "aux", "row", None),
        check_vma=False,
    )
```

```python
import functools

import jax
import jax.numpy as jnp
from jax import lax
from jax.experimental import pallas as pl
from jax.experimental.pallas import tpu as pltpu
from jax.sharding import PartitionSpec as P

MODES = 4
LINKS = 8
LANES = 128
STEP = 0.5
BOTH = ("aux", "row")
GRANT = 52 << 20
MOST = 60 << 20
TAKE = 44 << 20
ROWS = 512

F32 = jnp.float32
BF16 = jnp.bfloat16


class Sizes:
    def __init__(self, groups, rows, per_device, band, extent):
        self.groups, self.rows, self.per_device = groups, rows, per_device
        self.band, self.extent = band, extent
        self.devices = groups * rows
        self.local = band // groups
        self.auxes = per_device * groups
        self.za = 2 * self.auxes
        self.lanes = self.local * self.za
        self.fold = max(1, LANES // self.za)
        self.tile = self.fold * self.za
        self.tiles = self.local // self.fold
        self.joined = self.local % 16 == 0


def dot(a, b, dims=((1,), (0,))):
    return lax.dot_general(a, b, (dims, ((), ())), preferred_element_type=F32)


def run(kernel, outs, args, scratch=(), flops=0, scalars=()):
    spec = pl.BlockSpec(memory_space=pltpu.VMEM)
    flat = pl.BlockSpec(memory_space=pltpu.SMEM)
    moved = sum(a.size * a.dtype.itemsize for a in args)
    moved += sum(o.size * o.dtype.itemsize for o in outs)
    return pl.pallas_call(
        kernel,
        out_shape=list(outs),
        in_specs=[flat if n in scalars else spec for n in range(len(args))],
        out_specs=[spec] * len(outs),
        scratch_shapes=list(scratch),
        compiler_params=pltpu.CompilerParams(vmem_limit_bytes=16 << 20),
        cost_estimate=pl.CostEstimate(flops=flops, bytes_accessed=moved, transcendentals=0),
    )(*args)


def shape(*dims, dtype=F32):
    return jax.ShapeDtypeStruct(dims, dtype)


def one_hot(target, count):
    return (target[:, None] == jnp.arange(count, dtype=jnp.int32)[None, :]).astype(BF16)


def matrix_index(s, index, device):
    group, row = device // s.rows, device % s.rows
    return row * s.band + index * s.groups + group


def row_blocks(extent, size=128):
    return range(0, extent, size)


def send_start_kernel(d_ref, pick_rows, pick_cols, out_ref):
    planes, number, band, extent = d_ref.shape
    flat = d_ref[...].reshape(planes * number * band, extent).astype(BF16)
    for b in row_blocks(flat.shape[0]):
        moved = dot(pick_rows[b : b + 128, :], flat).astype(BF16)
        out_ref[b : b + 128, :] = dot(moved, pick_cols[...]).astype(BF16)


def take_start_kernel(got_ref, pick_lanes, message_rows, s_ref, m_ref):
    for b in row_blocks(got_ref.shape[1]):
        s_ref[b : b + 128, :] = dot(
            got_ref[:, b : b + 128], pick_lanes[...], ((0,), (0,))
        ).astype(BF16)
    for b in row_blocks(m_ref.shape[0]):
        m_ref[b : b + 128, :] = dot(message_rows[b : b + 128, :], s_ref[...]).astype(BF16)


def turn(s, load, order, swap, put):
    size = order.shape[0]
    span = size // s.local
    blocks = s.extent // size
    parts = []
    for block in range(blocks):
        moved = dot(order[...], load(block * size, size))
        for ih in range(s.tiles):
            for jh in range(s.tiles):
                lanes = slice(jh * s.tile, (jh + 1) * s.tile)
                pieces = [
                    moved[(ih * s.fold + f) * span : (ih * s.fold + f + 1) * span, lanes]
                    for f in range(s.fold)
                ]
                parts.append(jnp.concatenate(pieces, axis=1) if s.fold > 1 else pieces[0])
    turned = dot(jnp.concatenate(parts, axis=0).astype(BF16), swap[...])
    for block in range(blocks):
        for ih in range(s.tiles):
            for jh in range(s.tiles):
                start = ((block * s.tiles + ih) * s.tiles + jh) * span
                for f in range(s.fold):
                    first = (jh * s.fold + f) * s.devices + block * span
                    put(
                        slice(first, first + span),
                        slice(ih * s.tile, (ih + 1) * s.tile),
                        turned[start : start + span, f * s.tile : (f + 1) * s.tile],
                    )


def take_columns_kernel(s, got_ref, order, swap, first_rows, left_rows, s_ref, t_ref, *message):
    def put(rows, lanes, value):
        t_ref[rows, lanes] = value.astype(BF16)

    turn(s, lambda start, size: got_ref[start : start + size, :], order, swap, put)
    write_messages(s, first_rows, left_rows, s_ref, t_ref, message)


def write_messages(s, right_rows, left_rows, s_ref, t_ref, message):
    pairs = ((left_rows, t_ref), (right_rows, s_ref))
    if not s.joined and len(message) == 1:
        pairs = pairs[:1]
    both = s.joined and message[0].shape[0] == 2 * s.extent
    for part, (matrix, state) in enumerate(pairs):
        if s.joined and part == 1 and not both:
            continue
        for b in row_blocks(s.extent):
            product = dot(matrix[b : b + 128, :], state[...]).astype(BF16)
            if not s.joined:
                message[part][b : b + 128, :] = product
            elif not both:
                message[0][b : b + 128, :] = product
            else:
                for k in range(128 // s.local):
                    start = ((b // s.local + k) * 2 + part) * s.local
                    message[0][start : start + s.local, :] = product[
                        k * s.local : (k + 1) * s.local, :
                    ]


def slope_kernel(
    s, with_columns, s_ref, t_ref, ys_ref, yt_ref, damp, q_ref, right, left, unit, wa_s, wb_s, wa_t, wb_t, *rest
):
    if with_columns:
        ks_ref, kt_ref, turned = rest
    else:
        ks_ref, turned = rest

    def one(direct, mirror, y_ref, h, wa, wb, out_ref, sign):
        for th in range(s.tiles):
            lanes = slice(th * s.tile, (th + 1) * s.tile)
            turned[:, lanes] = dot(direct[:, lanes], unit[...]).astype(BF16)
        for b in row_blocks(s.extent):
            rows = slice(b, b + 128)
            whole = dot(h[rows, :], turned[...])
            for th in range(s.tiles):
                lanes = slice(th * s.tile, (th + 1) * s.tile)
                source = jnp.concatenate([direct[rows, lanes], mirror[rows, lanes]], axis=1)
                source = jnp.concatenate([source, source], axis=1)
                total = dot(source, wa[th]) - damp[:, lanes] * y_ref[rows, lanes].astype(F32)
                total = total + sign * whole[:, lanes]
                fields = dot(source, wb[...])
                for k in range(MODES):
                    total = total + q_ref[rows, k : k + 1] * fields[:, k * s.tile : (k + 1) * s.tile]
                out_ref[rows, lanes] = total

    one(s_ref, t_ref, ys_ref, right, wa_s, wb_s, ks_ref, -1.0)
    if with_columns:
        one(t_ref, s_ref, yt_ref, left, wa_t, wb_t, kt_ref, 1.0)


def part_loader(s, refs, part):
    def load(start, size):
        if not s.joined:
            return refs[part][start : start + size, :]
        step = s.local
        pieces = []
        for first in range(start, start + size, step):
            at = (first // step * 2 + part) * step
            pieces.append(refs[0][at : at + step, :])
        return jnp.concatenate(pieces, axis=0)

    return load


def next_kernel(s, weight, step, has_total, both, got_count, *refs):
    got = refs[:got_count]
    refs = refs[got_count:]
    order, swap, right_rows, left_rows, ks_ref, kt_ref, ds_ref, dt_ref = refs[:8]
    refs = refs[8:]
    total_in = None
    if has_total:
        total_in, refs = refs[0], refs[1:]
    s_ref, t_ref, ys_ref, yt_ref, total_ref = refs[:5]
    message, arrived = refs[5:-1], refs[-1]

    def put(rows, lanes, value):
        arrived[rows, lanes] = value

    for part in range(2):
        turn(s, part_loader(s, got, part), order, swap, put)
        for b in row_blocks(s.extent, 64):
            rows = slice(b, b + 64)
            if part == 0:
                slope = ks_ref[rows, :] + arrived[rows, :]
                grown = weight * slope
                total_ref[rows, :] = total_in[rows, :] + grown if has_total else grown
                state = ds_ref[rows, :].astype(F32) + step * slope
                ys_ref[rows, :] = state
                s_ref[rows, :] = state.astype(BF16)
            else:
                slope = kt_ref[rows, :] - arrived[rows, :]
                state = dt_ref[rows, :].astype(F32) + step * slope
                yt_ref[rows, :] = state
                t_ref[rows, :] = state.astype(BF16)
    if message:
        write_messages(s, right_rows, left_rows, s_ref, t_ref, message)


def last_kernel(s, weight, got_ref, order, swap, ks_ref, total_in, pick_lanes, out_ref, arrived, grown):
    def put(rows, lanes, value):
        arrived[rows, lanes] = value

    turn(s, lambda start, size: got_ref[start : start + size, :], order, swap, put)
    for b in row_blocks(s.extent, 64):
        rows = slice(b, b + 64)
        change = total_in[rows, :] + weight * (ks_ref[rows, :] + arrived[rows, :])
        grown[rows, :] = change.astype(BF16)
    for b in row_blocks(s.lanes):
        out_ref[b : b + 128, :] = dot(
            pick_lanes[b : b + 128, :], grown[...], ((1,), (1,))
        ).astype(BF16)


def finish_kernel(got_ref, place_rows, place_cols, d_ref, out_ref):
    planes, number, band, extent = d_ref.shape
    for z in range(planes):
        for n in range(number):
            at = (z * number + n) * band
            for b in range(0, band, min(band, 128)):
                size = min(band, 128)
                rows = slice(at + b, at + b + size)
                moved = dot(place_rows[rows, :], got_ref[...]).astype(BF16)
                out_ref[z, n, b : b + size, :] = d_ref[z, n, b : b + size, :] + dot(
                    moved, place_cols[...]
                )


def link_matrices(s, counts, weight_real, weight_imag, link_index, link_mirror):
    ones = jnp.ones_like(counts)
    real = jnp.stack([ones, counts * weight_real[None, :]], 1)
    imag = jnp.stack([jnp.zeros_like(counts), counts * weight_imag[None, :]], 1)
    index = link_index.reshape(s.auxes, 2, MODES)
    mirror = link_mirror.reshape(s.auxes, 2, MODES)
    source = jnp.arange(s.auxes, dtype=jnp.int32)
    hit = index[None] == source[:, None, None, None]
    kinds = jnp.stack([hit & (mirror[None] == 0), hit & (mirror[None] == 1)]).astype(F32)
    along = jnp.sum(kinds * real, 3)
    cross = jnp.sum(kinds * imag, 3)
    along, cross = (jnp.transpose(m, (0, 3, 1, 2)) for m in (along, cross))
    flip = jnp.array([1.0, -1.0], F32).reshape(2, 1, 1, 1)

    def build(sign):
        upper = jnp.concatenate([cross, -sign * along], 3)
        lower = jnp.concatenate([sign * along, cross], 3) * flip
        return jnp.concatenate([upper, lower], 2)

    return build(1.0), build(-1.0)


def two_pieces(weights, axis):
    high = lax.reduce_precision(weights, 8, 7)
    low = weights - high
    return jnp.concatenate([high.astype(BF16), low.astype(BF16)], axis)


def coupling_weights(s, by_local, by_first, local_q):
    eye = jnp.eye(s.fold, dtype=F32)
    near = jnp.einsum("ki,xkuv->ixuv", local_q, by_local, precision=lax.Precision.HIGHEST)
    near = near.reshape(s.tiles, s.fold, 2, s.za, s.za)
    near = jnp.transpose(near, (0, 2, 1, 3, 4))[:, :, :, :, None, :] * eye[None, None, :, None, :, None]
    near = near.reshape(s.tiles, 2 * s.tile, s.tile)
    far = jnp.transpose(by_first, (0, 2, 1, 3))[:, None, :, :, None, :] * eye[None, :, None, None, :, None]
    far = far.reshape(2 * s.tile, MODES * s.tile)
    return two_pieces(near, 1), two_pieces(far, 0)


def general_body(
    density,
    couplings,
    weight_real,
    weight_imag,
    mode_rates,
    tier_counts,
    link_index,
    link_mirror,
    block_diagonal,
    block_outer,
    block_column,
):
    planes, per_device, band, extent = density.shape
    s = Sizes(lax.axis_size("aux"), lax.axis_size("row"), per_device, band, extent)
    blocks, block = block_diagonal.shape[0], block_diagonal.shape[1]
    group, row = lax.axis_index("aux"), lax.axis_index("row")
    device = group * s.rows + row
    cube = 2 * extent * extent * s.lanes

    number = jnp.arange(extent, dtype=jnp.int32)
    first_to_matrix = matrix_index(s, number // s.devices, number % s.devices)
    posted_to_matrix = matrix_index(s, number % s.local, number // s.local)
    posted_to_first = number % s.local * s.devices + number // s.local

    wide = jnp.arange(s.lanes, dtype=jnp.int32)
    sub = planes * per_device * s.local
    start_source = wide % sub * s.groups + wide // sub
    pick_rows = one_hot(start_source, s.lanes)
    pick_cols = one_hot(first_to_matrix, extent).T
    lane_of = (
        wide % s.local * s.za
        + wide // (per_device * s.local) % planes * s.auxes
        + wide // sub * per_device
        + wide // s.local % per_device
    )
    pick_lanes = one_hot(lane_of, s.lanes)
    message_rows = one_hot(posted_to_first, extent)
    start_message = run(
        send_start_kernel,
        [shape(s.lanes, extent, dtype=BF16)],
        [density, pick_rows, pick_cols],
        flops=2 * cube,
    )[0]
    start_got = lax.all_to_all(
        start_message.reshape(s.groups, sub, extent), "aux", split_axis=0, concat_axis=0, tiled=True
    ).reshape(s.lanes, extent)

    selector = block_column[:, None] == jnp.arange(blocks, dtype=jnp.int32)[None, :]
    own = jnp.eye(blocks, dtype=F32)
    whole_h = (
        own[:, None, :, None] * block_diagonal.astype(F32)[:, :, None, :]
        + selector.astype(F32)[:, None, :, None] * block_outer.astype(F32)[:, :, None, :]
    ).reshape(extent, extent).astype(BF16)
    first_h = one_hot(first_to_matrix, extent)
    left = jnp.dot(
        jnp.dot(first_h, whole_h, preferred_element_type=BF16), first_h.T, preferred_element_type=BF16
    )
    right = left.T
    left_rows = jnp.dot(message_rows, left, preferred_element_type=BF16)
    right_rows = jnp.dot(message_rows, right, preferred_element_type=BF16)

    counts = lax.all_gather(tier_counts, "aux", axis=0, tiled=True).astype(F32)
    damping = jnp.sum(counts * mode_rates[None, :], axis=1)
    damp = jnp.tile(damping, (planes * s.local,))[None, :]
    q_first = jnp.dot(
        couplings, first_h.T.astype(F32), precision=lax.Precision.HIGHEST
    ).T
    local_pick = (matrix_index(s, jnp.arange(s.local, dtype=jnp.int32), device)[None, :] == number[:, None])
    local_q = jnp.dot(couplings, local_pick.astype(F32), precision=lax.Precision.HIGHEST)
    by_row, by_column = link_matrices(s, counts, weight_real, weight_imag, link_index, link_mirror)
    wa_s, wb_s = coupling_weights(s, by_row, by_column, local_q)
    wa_t, wb_t = coupling_weights(s, by_column, by_row, local_q)

    lane = jnp.arange(s.za, dtype=jnp.int32)
    unit = jnp.where(
        lane[:, None] == (lane[None, :] + s.auxes) % s.za,
        jnp.where(lane[None, :] < s.auxes, 1.0, -1.0),
        0.0,
    )
    eye_fold = jnp.eye(s.fold, dtype=F32)
    unit_tile = (eye_fold[:, None, :, None] * unit[None, :, None, :]).reshape(s.tile, s.tile).astype(BF16)
    swap = (
        eye_fold[:, None, None, None, :, None]
        * eye_fold[None, :, None, :, None, None]
        * unit[None, None, :, None, None, :]
    ).reshape(s.fold * s.tile, s.fold * s.tile).astype(BF16)
    keep = (
        eye_fold[:, None, None, None, :, None]
        * eye_fold[None, :, None, :, None, None]
        * jnp.eye(s.za, dtype=F32)[None, None, :, None, None, :]
    ).reshape(s.fold * s.tile, s.fold * s.tile).astype(BF16)
    size = min(extent, max(256, 16 * s.local))
    span = size // s.local
    at = jnp.arange(size, dtype=jnp.int32)
    order = one_hot(at % span * s.local + at // span, size)

    state = shape(extent, s.lanes, dtype=BF16)
    full = shape(extent, s.lanes)
    held = pltpu.VMEM((extent, s.lanes), F32)
    held_b = pltpu.VMEM((extent, s.lanes), BF16)

    def exchange(messages):
        parts = [m.reshape(s.devices, -1, s.lanes) for m in messages]
        sent = parts[0] if len(parts) == 1 else jnp.concatenate(parts, 1)
        got = lax.all_to_all(sent, BOTH, split_axis=0, concat_axis=0, tiled=True)
        if len(parts) == 1:
            return [got.reshape(-1, s.lanes)]
        height = s.local
        return [got[:, p * height : (p + 1) * height].reshape(-1, s.lanes) for p in range(2)]

    if s.joined:
        pair = [shape(2 * extent, s.lanes, dtype=BF16)]
    else:
        pair = [state, state]

    s_now, posted = run(
        take_start_kernel, [state, state], [start_got, pick_lanes, message_rows], flops=2 * cube
    )
    got = exchange([posted])
    t_now, *messages = run(
        functools.partial(take_columns_kernel, s),
        [state] + pair,
        [got[0], order, keep, right_rows, left_rows, s_now],
        flops=4 * cube,
    )
    start_s, start_t = s_now, t_now
    ys, yt = s_now, t_now
    total = None
    shares = [STEP / 6.0, STEP / 3.0, STEP / 3.0, STEP / 6.0]
    steps = [0.25, 0.25, 0.5]
    for section in range(4):
        got = exchange(messages)
        columns = section < 3
        slopes = run(
            functools.partial(slope_kernel, s, columns),
            [full, full] if columns else [full],
            [s_now, t_now, ys, yt, damp, q_first, right, left, unit_tile, wa_s, wb_s, wa_t, wb_t],
            scratch=[held_b],
            flops=(12 if columns else 6) * cube,
        )
        if columns:
            args = list(got) + [order, swap, right_rows, left_rows, *slopes, start_s, start_t]
            if total is not None:
                args.append(total)
            outs = [state, state, full, full, full]
            outs += pair if section < 2 else [state]
            s_now, t_now, ys, yt, total, *messages = run(
                functools.partial(
                    next_kernel, s, shares[section], steps[section], total is not None, section < 2, len(got)
                ),
                outs,
                args,
                scratch=[held],
                flops=6 * cube,
            )
    change = run(
        functools.partial(last_kernel, s, shares[3]),
        [shape(s.lanes, extent, dtype=BF16)],
        [got[0], order, swap, slopes[0], total, pick_lanes],
        scratch=[held, held_b],
        flops=3 * cube,
    )[0]
    back = lax.all_to_all(
        change.reshape(s.groups, sub, extent), "aux", split_axis=0, concat_axis=0, tiled=True
    ).reshape(s.lanes, extent)
    return run(
        finish_kernel,
        [shape(planes, per_device, band, extent)],
        [back, pick_rows.T, pick_cols.T, density],
        flops=2 * cube,
    )[0]


def iotas(rows, columns):
    return (
        lax.broadcasted_iota(jnp.int32, (rows, columns), 0),
        lax.broadcasted_iota(jnp.int32, (rows, columns), 1),
    )


def mask_to(value):
    return value.astype(F32).astype(BF16)


def post_matrix(s):
    row, column = iotas(s.extent, s.extent)
    return mask_to(column == row % s.local * s.devices + row // s.local)


class Stage:
    def __init__(self, sources, buffers, targets, results, semaphores, offset, lead):
        self.buffers, self.results, self.targets = buffers, results, targets
        self.semaphores, self.next, self.offset = semaphores, 0, offset
        self.sources, self.lead = sources, lead
        self.coming = [self.copy(a, b) for a, b in zip(sources[:lead], buffers)]
        self.going = []

    def copy(self, source, target):
        made = pltpu.make_async_copy(source, target, self.semaphores.at[self.next])
        self.next += 1
        made.start()
        return made

    def front(self, index):
        return self.need(index - self.offset)

    def need(self, index):
        index += self.offset
        if index >= len(self.coming):
            self.start_rest()
        if self.coming[index] is not None:
            self.coming[index].wait()
            self.coming[index] = None
        return self.buffers[index]

    def start_rest(self):
        known = len(self.coming)
        self.coming += [self.copy(a, b) for a, b in zip(self.sources[known:], self.buffers[known:])]

    def send(self, index, rows=None):
        made, target = self.results[index], self.targets[index]
        if rows is not None:
            made, target = made.at[rows], target.at[rows]
        self.going.append(self.copy(made, target))

    def finish(self):
        for made in self.going:
            made.wait()


def run_staged(body, outs, args, temporaries=(), scalars=(), front=(), lead=None, grant=GRANT, flops=0):
    arrays, views = [], []
    for arg in [*front, *args]:
        array, part = arg if isinstance(arg, tuple) else (arg, None)
        if not any(array is a for a in arrays):
            arrays.append(array)
        views.append(([array is a for a in arrays].index(True), part))
    shapes, places = [], []
    for out in outs:
        if isinstance(out, tuple):
            for part in range(out[1]):
                places.append((len(shapes), part))
            shapes.append(out[0])
        else:
            places.append((len(shapes), None))
            shapes.append(out)
    tall = lambda x, part: x.shape if part is None else x.shape[:1] + x.shape[2:]
    buffers = [pltpu.VMEM(tall(arrays[k], part), arrays[k].dtype) for k, part in views]
    results = [pltpu.VMEM(tall(shapes[k], part), shapes[k].dtype) for k, part in places]
    count = len(buffers) + 2 * len(results)

    def kernel(*refs):
        small, refs = refs[: len(scalars)], refs[len(scalars) :]
        source, refs = refs[: len(arrays)], refs[len(arrays) :]
        target, refs = refs[: len(shapes)], refs[len(shapes) :]
        own, refs = refs[: len(buffers)], refs[len(buffers) :]
        made, refs = refs[: len(results)], refs[len(results) :]
        pick = lambda ref, part: ref if part is None else ref.at[:, part]
        stage = Stage(
            [pick(source[k], part) for k, part in views],
            own,
            [pick(target[k], part) for k, part in places],
            made,
            refs[-1],
            len(front),
            len(views) if lead is None else lead,
        )
        body(stage, small, refs[:-1])
        stage.finish()

    moved = sum(a.size * a.dtype.itemsize for a in arrays)
    moved += sum(o.size * o.dtype.itemsize for o in shapes)
    far = pl.BlockSpec(memory_space=pltpu.HBM)
    return pl.pallas_call(
        kernel,
        out_shape=shapes,
        in_specs=[pl.BlockSpec(memory_space=pltpu.SMEM)] * len(scalars) + [far] * len(arrays),
        out_specs=[far] * len(shapes),
        scratch_shapes=buffers + results + list(temporaries) + [pltpu.SemaphoreType.DMA((count,))],
        compiler_params=pltpu.CompilerParams(vmem_limit_bytes=grant),
        cost_estimate=pl.CostEstimate(flops=flops, bytes_accessed=moved, transcendentals=0),
    )(*scalars, *arrays)


def fill(s, result, first, value, lanes=slice(None)):
    count = value.shape[0] // s.local
    device = first // s.local
    result[device : device + count, :, lanes] = value.reshape(count, s.local, value.shape[1])


def flat_rows(ref, rows, lanes=slice(None)):
    piece = ref[rows, :, lanes]
    return piece.reshape(piece.shape[0] * piece.shape[1], piece.shape[2])


def even_start(s, stage, small, temporaries):
    (post,) = temporaries
    post[...] = post_matrix(s)
    blocks = s.extent // s.band
    which = lax.axis_index("row") % s.per_device
    flats = [stage.need(v)[...].reshape(s.band, s.extent).astype(BF16) for v in range(blocks)]
    row, lane = iotas(ROWS, s.band)
    counts = stage.need(blocks)[...].astype(F32)
    mine = counts[0:1, :]
    for n in range(1, s.per_device):
        mine = jnp.where(which == n, counts[n : n + 1, :], mine)
    for v in range(blocks):
        count = mine[:, v : v + 1]
        for b in row_blocks(s.extent, ROWS):
            value = dot(post[b : b + ROWS, :], flats[v], ((1,), (1,)))
            own = (row % s.local == 0) & (lane == (row + b) // s.local)
            value = jnp.where(own, count, value).astype(BF16)
            fill(s, stage.results[1], b, value, slice(v * s.band, (v + 1) * s.band))
    stage.send(1)
    flat = jnp.concatenate(flats, axis=0)
    for b in row_blocks(s.extent, ROWS):
        fill(s, stage.results[0], b, dot(post[b : b + ROWS, :], flat).astype(BF16))
    stage.send(0)


def send_products(s, stage, matrix, state_ref, index):
    half = s.extent // 2
    for b in row_blocks(s.extent, half):
        fill(s, stage.results[index], b, dot(matrix[b : b + half, :], state_ref[...]).astype(BF16))
        stage.send(index, slice(b // s.local, (b + half) // s.local))


def take_rows(s, rows_in, row_lanes, s_ref):
    rows = flat_rows(rows_in, slice(0, s.devices))
    s_ref[...] = dot(rows, row_lanes[...], ((0,), (0,))).astype(BF16)


def take_columns(s, columns_in, column_lanes, s_ref, t_ref):
    me = lax.axis_index("aux") * s.rows + lax.axis_index("row")
    blocks = s.extent // s.band
    parts = s.band // s.devices
    row, lane = iotas(s.devices, s.tile)
    mine = (row == me) & (lane < s.za)
    bands = []
    for q in range(s.rows):
        pieces = []
        for v in range(blocks):
            for g in range(s.groups):
                pieces.append(columns_in[g * s.rows + q, :, v * s.band : (v + 1) * s.band])
        bands.append(jnp.concatenate(pieces, axis=0))
    t_ref[...] = dot(jnp.concatenate(bands, axis=1), column_lanes[...], ((0,), (0,))).astype(BF16)
    for q in range(s.rows):
        rows = slice(q * s.band, q * s.band + s.devices)
        first = q * parts * s.za
        kept = s_ref[: s.devices, first : first + s.tile].astype(F32)
        t_ref[rows, : s.tile] = jnp.where(mine, kept, t_ref[rows, : s.tile].astype(F32)).astype(BF16)


def even_take(s, stage, small, temporaries):
    s_ref, t_ref = temporaries
    take_rows(s, stage.front(0), stage.need(0), s_ref)
    send_products(s, stage, stage.need(1), s_ref, 1)
    take_columns(s, stage.front(1), stage.need(2), s_ref, t_ref)
    send_products(s, stage, stage.need(3), t_ref, 0)


def turn_matrices(s, order, swap):
    size = order.shape[0]
    span = size // s.local
    k, n = lax.broadcasted_iota(jnp.int32, (size, 1), 0), lax.broadcasted_iota(jnp.int32, (1, size), 1)
    order[...] = mask_to(n == k % span * s.local + k // span)
    wide = s.fold * s.tile
    k, n = lax.broadcasted_iota(jnp.int32, (wide, 1), 0), lax.broadcasted_iota(jnp.int32, (1, wide), 1)
    sign = jnp.where(n // s.auxes % 2 == 0, 1.0, -1.0)
    there = (k // s.za % s.fold * s.fold + k // s.tile) * s.za + (k + s.auxes) % s.za
    swap[...] = jnp.where(there == n, sign, 0.0).astype(BF16)


def even_turn(s, got, order, swap, put):
    def load(start, size):
        return flat_rows(got, slice(start // s.local, (start + size) // s.local))

    turn(s, load, order, swap, put)


def updates(scale, base_ref, keep):
    def put(rows, lanes, value):
        keep(rows, lanes, base_ref[rows, lanes] + scale * value)

    return put


def even_next(s, step, stage, small, temporaries):
    s_ref, t_ref, order, swap = temporaries
    turn_matrices(s, order, swap)

    def keep_in(ref):
        def keep(rows, lanes, value):
            ref[rows, lanes] = value.astype(BF16)

        return keep

    got = stage.front(0)
    stage.start_rest()
    even_turn(s, got, order, swap, updates(step, stage.need(0), keep_in(s_ref)))
    send_products(s, stage, stage.need(1), s_ref, 1)
    got = stage.need(2)
    even_turn(s, got, order, swap, updates(-step, stage.need(3), keep_in(t_ref)))
    send_products(s, stage, stage.need(4), t_ref, 0)


def even_slope_part(s, direct, mirror, y_ref, h, unit, damp, q_ref, wa, wb, turned, sign, put):
    factors = [jnp.broadcast_to(q_ref[:, k : k + 1], (s.extent, s.tile)) for k in range(MODES)]
    for th in range(s.tiles):
        lanes = slice(th * s.tile, (th + 1) * s.tile)
        turned[:, lanes] = dot(direct[:, lanes], unit[...]).astype(BF16)
    for b in row_blocks(s.extent, ROWS):
        rows = slice(b, b + ROWS)
        whole = dot(h[rows, :], turned[...])
        for th in range(s.tiles):
            lanes = slice(th * s.tile, (th + 1) * s.tile)
            source = jnp.concatenate([direct[rows, lanes], mirror[rows, lanes]], axis=1)
            source = jnp.concatenate([source, source], axis=1)
            total = dot(source, wa[th]) - damp[:, lanes] * y_ref[rows, lanes].astype(F32)
            total = total + sign * whole[:, lanes]
            fields = dot(source, wb[...])
            for k in range(MODES):
                total = total + factors[k][rows, :] * fields[:, k * s.tile : (k + 1) * s.tile]
            put(rows, lanes, total)


def put_base(ref, start_ref, step):
    def put(rows, lanes, value):
        ref[rows, lanes] = start_ref[rows, lanes].astype(F32) + step * value

    return put


def even_first_slope(s, step, stage, small, temporaries):
    (turned,) = temporaries
    need = stage.need
    first, second, s_ref, t_ref = stage.results
    take_rows(s, stage.front(0), need(0), s_ref)
    stage.send(2)
    take_columns(s, stage.front(1), need(1), s_ref, t_ref)
    stage.send(3)
    unit, damp, q_ref = need(2), need(3), need(4)
    put = put_base(first, s_ref, step)
    even_slope_part(s, s_ref, t_ref, s_ref, need(5), unit, damp, q_ref, need(6), need(7), turned, -1.0, put)
    stage.send(0)
    put = put_base(second, t_ref, step)
    even_slope_part(s, t_ref, s_ref, t_ref, need(8), unit, damp, q_ref, need(9), need(10), turned, 1.0, put)
    stage.send(1)


def even_slope(s, step, next_step, ratio, less, has_total, stage, small, temporaries):
    turned, s_ref, t_ref, ys_ref, yt_ref, order, swap = temporaries
    turn_matrices(s, order, swap)
    need = stage.need
    first, second, total_ref = stage.results

    def keep_in(ref, exact):
        def keep(rows, lanes, value):
            exact[rows, lanes] = value
            ref[rows, lanes] = value.astype(BF16)

        return keep

    even_turn(s, stage.front(0), order, swap, updates(step, need(0), keep_in(s_ref, ys_ref)))
    even_turn(s, stage.front(1), order, swap, updates(-step, need(1), keep_in(t_ref, yt_ref)))
    ds_ref, dt_ref = need(2), need(3)
    total_in = need(13) if has_total else None
    for b in row_blocks(s.extent, 64):
        rows = slice(b, b + 64)
        grown = ratio * ys_ref[rows, :] - (ratio + less) * ds_ref[rows, :].astype(F32)
        total_ref[rows, :] = total_in[rows, :] + grown if has_total else grown
    stage.send(2)
    unit, damp, q_ref = need(4), need(5), need(6)
    put = put_base(first, ds_ref, next_step)
    even_slope_part(s, s_ref, t_ref, ys_ref, need(7), unit, damp, q_ref, need(8), need(9), turned, -1.0, put)
    stage.send(0)
    put = put_base(second, dt_ref, next_step)
    even_slope_part(s, t_ref, s_ref, yt_ref, need(10), unit, damp, q_ref, need(11), need(12), turned, 1.0, put)
    stage.send(1)


def even_last(s, step, ratio, weight, stage, small, temporaries):
    ys_ref, s_ref, t_ref, grown, turned, order, swap = temporaries
    turn_matrices(s, order, swap)
    need = stage.need

    def keep_columns(rows, lanes, value):
        t_ref[rows, lanes] = value.astype(BF16)

    got = stage.front(0)
    stage.start_rest()
    even_turn(s, got, order, swap, updates(-step, need(0), keep_columns))
    unit, left, column_lanes = need(1), need(2), need(3)
    for th in range(s.tiles):
        lanes = slice(th * s.tile, (th + 1) * s.tile)
        turned[:, lanes] = dot(t_ref[:, lanes], unit[...]).astype(BF16)
    for b in row_blocks(s.extent, ROWS):
        rows = slice(b, b + ROWS)
        grown[rows, :] = (weight * dot(left[rows, :], turned[...])).astype(BF16)
    out = stage.results[1]
    value = dot(column_lanes[...], grown[...], ((1,), (1,))).astype(BF16)
    for q in range(s.rows):
        for v in range(s.extent // s.band):
            for g in range(s.groups):
                at = (v * s.groups + g) * s.local
                piece = value[at : at + s.local, q * s.band : (q + 1) * s.band]
                out[g * s.rows + q, :, v * s.band : (v + 1) * s.band] = piece
    stage.send(1)

    def keep_rows(rows, lanes, value):
        ys_ref[rows, lanes] = value
        s_ref[rows, lanes] = value.astype(BF16)

    even_turn(s, stage.front(1), order, swap, updates(step, need(4), keep_rows))
    total_in = need(5)

    def put_change(rows, lanes, value):
        change = total_in[rows, lanes] + ratio * ys_ref[rows, lanes]
        grown[rows, lanes] = (change + weight * value).astype(BF16)

    even_slope_part(
        s, s_ref, t_ref, ys_ref, need(8), unit, need(6), need(7), need(9), need(10), turned, -1.0, put_change
    )
    row_lanes = need(11)
    for b in row_blocks(s.extent, ROWS):
        fill(s, stage.results[0], b, dot(row_lanes[b : b + ROWS, :], grown[...], ((1,), (1,))).astype(BF16))
    stage.send(0)


def even_finish(s, stage, small, temporaries):
    (post,) = temporaries
    post[...] = post_matrix(s)
    everyone = slice(0, s.devices)
    change = dot(post[...], flat_rows(stage.front(0), everyone), ((0,), (0,)))
    change = change + dot(flat_rows(stage.front(1), everyone), post[...], ((0,), (0,)))
    for v in range(s.extent // s.band):
        rows = slice(v * s.band, (v + 1) * s.band)
        stage.results[v][...] = (stage.need(v)[...].reshape(s.band, s.extent) + change[rows, :]).reshape(
            stage.results[v].shape
        )
        stage.send(v)


def even_hamiltonian(s, stage, small, temporaries):
    (where_ref,) = small
    (post,) = temporaries
    left, right, left_rows, right_rows = stage.results
    own_ref, outer_ref = stage.need(0), stage.need(1)
    blocks, block = own_ref.shape[0], own_ref.shape[1]
    post[...] = post_matrix(s)
    row, column = iotas(block, s.extent)
    for b in range(blocks):
        spread = column - row
        to_own = mask_to(spread == b * block)
        to_far = mask_to(spread == where_ref[b] * block)
        left[b * block : (b + 1) * block, :] = (dot(own_ref[b], to_own) + dot(outer_ref[b], to_far)).astype(BF16)
    row, column = iotas(s.extent, s.extent)
    same = mask_to(row == column)
    for b in row_blocks(s.extent, ROWS):
        rows = slice(b, b + ROWS)
        right[rows, :] = dot(same[rows, :], left[...], ((1,), (1,))).astype(BF16)
        left_rows[rows, :] = dot(post[rows, :], left[...]).astype(BF16)
        right_rows[rows, :] = dot(post[rows, :], left[...], ((1,), (1,))).astype(BF16)
    for index in range(4):
        stage.send(index)


def even_weights(s, stage, small, temporaries):
    real_ref, imag_ref, rate_ref = small
    wa_s, wb_s, wa_t, wb_t, damp = stage.results
    columns_in, index_ref, mirror_ref, couplings_ref = [stage.need(k) for k in range(4)]
    me = lax.axis_index("aux") * s.rows + lax.axis_index("row")
    depth, wide = 2 * s.tile, MODES * s.tile
    row, column = iotas(s.auxes, wide)
    by_lane = mask_to(column % s.auxes == row)

    def spread(table):
        return dot(table.astype(F32).astype(BF16), by_lane, ((0,), (0,)))

    row, lane = iotas(s.extent, MODES)
    gather = mask_to(row == lane * s.band + me)
    row, lane = iotas(s.auxes, s.auxes * s.local)
    wanted = mask_to(lane == row * s.local)
    pieces = [columns_in[a // s.per_device * s.rows + a % s.per_device] for a in range(s.auxes)]
    counts = spread(dot(wanted, dot(jnp.concatenate(pieces, axis=0), gather).astype(BF16)))
    index, mirror = spread(index_ref[...]), spread(mirror_ref[...])
    lane_mode = lax.broadcasted_iota(jnp.int32, (1, wide), 1) // s.tile

    def of_mode(values):
        out = values[0]
        for k in range(1, MODES):
            out = jnp.where(lane_mode == k, values[k], out)
        return out

    take = lambda table, first: of_mode([table[first + k : first + k + 1, :] for k in range(MODES)])
    ups, downs = take(index, 0), take(index, MODES)
    up_kinds, down_kinds = take(mirror, 0), take(mirror, MODES)
    real = of_mode([counts[k : k + 1, :] * real_ref[k] for k in range(MODES)])
    imag = of_mode([counts[k : k + 1, :] * imag_ref[k] for k in range(MODES)])
    rates = counts[0:1, :] * rate_ref[0]
    for k in range(1, MODES):
        rates = rates + counts[k : k + 1, :] * rate_ref[k]
    damp[...] = rates

    row, column = iotas(s.extent, s.lanes)
    pick = (row % s.devices == me) & (row // s.devices == column // s.za)
    local_q = lax.dot_general(
        couplings_ref[...],
        pick.astype(F32),
        (((1,), (0,)), ((), ())),
        precision=lax.Precision.HIGHEST,
        preferred_element_type=F32,
    )

    row, column = iotas(depth, wide)
    same = row // s.za % s.fold == column // s.za % s.fold
    source, kind = (row % s.auxes).astype(F32), (row // s.tile).astype(F32)
    from_imag, to_imag = row // s.auxes % 2, column // s.auxes % 2
    up = same & (ups == source) & (up_kinds == kind)
    down = same & (downs == source) & (down_kinds == kind)
    along = jnp.where(up, 1.0, 0.0) + jnp.where(down, real, 0.0)
    cross = jnp.where(down, imag, 0.0)
    along = jnp.where(from_imag == 1, along, -along)
    flip = jnp.where((from_imag == 1) & (row // s.tile == 1), -1.0, 1.0)
    by_row = flip * jnp.where(from_imag == to_imag, cross, along)
    by_column = flip * jnp.where(from_imag == to_imag, cross, -along)

    def pieces(value):
        high = value.astype(BF16)
        return high, (value - high.astype(F32)).astype(BF16)

    for near, far, wa, wb in ((by_row, by_column, wa_s, wb_s), (by_column, by_row, wa_t, wb_t)):
        wb[:depth, :], wb[depth:, :] = pieces(far)
        for th in range(s.tiles):
            lanes = slice(th * s.tile, (th + 1) * s.tile)
            total = local_q[0:1, lanes] * near[:, : s.tile]
            for k in range(1, MODES):
                total = total + local_q[k : k + 1, lanes] * near[:, k * s.tile : (k + 1) * s.tile]
            wa[th, :depth, :], wa[th, depth:, :] = pieces(total)
    for index in range(5):
        stage.send(index)


def even_body(
    s,
    density,
    couplings,
    weight_real,
    weight_imag,
    mode_rates,
    tier_counts,
    link_index,
    link_mirror,
    block_diagonal,
    block_outer,
    block_column,
):
    planes, per_device, band, extent = density.shape
    cube = 2 * extent * extent * s.lanes
    state = shape(extent, s.lanes, dtype=BF16)
    full = shape(extent, s.lanes)
    pair = (shape(s.devices, 2, s.local, s.lanes, dtype=BF16), 2)
    held = pltpu.VMEM((extent, s.lanes), F32)
    held_b = pltpu.VMEM((extent, s.lanes), BF16)

    def exchange(message):
        return lax.all_to_all(message, BOTH, split_axis=0, concat_axis=0, tiled=True)

    blocks = density.reshape(1, planes * per_device, band, extent)
    message = run_staged(
        functools.partial(even_start, s),
        [pair],
        [(blocks, v) for v in range(planes * per_device)] + [tier_counts],
        temporaries=[held_b],
        grant=MOST,
        flops=2 * cube,
    )[0]
    got = exchange(message)

    left, right, left_rows, right_rows = run_staged(
        functools.partial(even_hamiltonian, s),
        [state] * 4,
        [block_diagonal, block_outer],
        temporaries=[held_b],
        scalars=[block_column],
        grant=MOST,
        flops=4 * cube,
    )
    q_first = couplings.T

    k, n = iotas(s.lanes, s.lanes)
    parts = band // s.devices
    row_lanes = (
        n
        == (k // s.local % s.rows * parts + k % parts) * s.za
        + k // (parts * per_device) % planes * s.auxes
        + k // (s.local * s.rows) * per_device
        + k // parts % per_device
    ).astype(BF16)
    column_lanes = (
        n
        == k % s.local * s.za
        + k // (s.local * s.groups * per_device) * s.auxes
        + k // s.local % s.groups * per_device
        + k // (s.local * s.groups) % per_device
    ).astype(BF16)

    k, n = iotas(s.tile, s.tile)
    sign = jnp.where(n // s.auxes % 2 == 0, 1.0, -1.0)
    unit = jnp.where(k // s.za * s.za + (k + s.auxes) % s.za == n, sign, 0.0).astype(BF16)
    wide, size = s.fold * s.tile, max(256, 16 * s.local)
    swap, order = pltpu.VMEM((wide, wide), BF16), pltpu.VMEM((size, size), BF16)

    message = run_staged(
        functools.partial(even_take, s),
        [pair],
        [row_lanes, right_rows, column_lanes, left_rows],
        temporaries=[held_b, held_b],
        front=[(got, 0), (got, 1)],
        grant=TAKE,
        flops=4 * cube,
    )[0]
    wa = shape(s.tiles, 4 * s.tile, s.tile, dtype=BF16)
    wb = shape(4 * s.tile, MODES * s.tile, dtype=BF16)
    wa_s, wb_s, wa_t, wb_t, damp = run_staged(
        functools.partial(even_weights, s),
        [wa, wb, wa, wb, shape(1, s.lanes)],
        [(got, 1), link_index, link_mirror, couplings],
        scalars=[weight_real, weight_imag, mode_rates],
        grant=MOST,
        flops=cube,
    )
    tables = [unit, damp, q_first, right, wa_s, wb_s, left, wa_t, wb_t]
    shares = [STEP / 6.0, STEP / 3.0, STEP / 3.0, STEP / 6.0]
    steps = [0.25, 0.25, 0.5]
    ratios = [share / step for share, step in zip(shares, steps)]
    begun, got = got, exchange(message)
    base_s, base_t, s_now, t_now = run_staged(
        functools.partial(even_first_slope, s, steps[0]),
        [full, full, state, state],
        [row_lanes, column_lanes] + tables,
        temporaries=[held_b],
        front=[(begun, 0), (begun, 1)],
        flops=12 * cube,
    )
    total = None
    for section in range(2):
        step = steps[section]
        message = run_staged(
            functools.partial(even_next, s, step),
            [pair],
            [base_s, right_rows, (got, 1), base_t, left_rows],
            temporaries=[held_b, held_b, order, swap],
            front=[(got, 0)],
            flops=5 * cube,
        )[0]
        arrived, got = got, exchange(message)
        less = ratios[2] if section == 1 else 0.0
        base_s, base_t, total = run_staged(
            functools.partial(even_slope, s, step, steps[section + 1], ratios[section], less, total is not None),
            [full, full, full],
            [base_s, base_t, s_now, t_now] + tables + ([] if total is None else [total]),
            temporaries=[held_b, held_b, held_b, held, held, order, swap],
            front=[(arrived, 0), (arrived, 1)],
            flops=15 * cube,
        )
    message = run_staged(
        functools.partial(even_last, s, steps[2], ratios[2], shares[3]),
        [pair],
        [base_t, unit, left, column_lanes, base_s, total, damp, q_first, right, wa_s, wb_s, row_lanes],
        temporaries=[held, held_b, held_b, held_b, held_b, order, swap],
        front=[(got, 1), (got, 0)],
        flops=12 * cube,
    )[0]
    got = exchange(message)
    evolved = run_staged(
        functools.partial(even_finish, s),
        [(shape(1, planes * per_device, band, extent), planes * per_device)],
        [(blocks, v) for v in range(planes * per_device)],
        temporaries=[held_b],
        front=[(got, 0), (got, 1)],
        flops=2 * cube,
    )[0]
    return evolved.reshape(density.shape)


def body(density, *others):
    planes, per_device, band, extent = density.shape
    s = Sizes(lax.axis_size("aux"), lax.axis_size("row"), per_device, band, extent)
    even = band % s.devices == 0 and s.local % 16 == 0 and LANES % s.za == 0
    even = even and s.lanes == extent and planes * per_device * band == extent
    even = even and planes * per_device == MODES and per_device <= s.rows and s.devices <= s.band
    if even:
        return even_body(s, density, *others)
    return general_body(density, *others)


def solution(mesh):
    return jax.shard_map(
        body,
        mesh=mesh,
        in_specs=(
            P(None, "aux", "row", None),
            P(),
            P(),
            P(),
            P(),
            P("aux", None),
            P(),
            P(),
            P(),
            P(),
            P(),
        ),
        out_specs=P(None, "aux", "row", None),
        check_vma=False,
    )
```
